32 devices in a mesh: grp: 2 (over x), role: 2 (over core), tp: 8 (over z, y).
Axes of the slice: x: 2, y: 2, z: 4, core: 2. Of those that a mesh axis runs over, the one named last changes fastest.
Arguments:
- stretch_tokens: bfloat16 [2, 1024, 8192], P('role', ('grp', 'tp')), parts along dimension 1, may hold values from -60 to 60
- norm_gain: bfloat16 [8192], replicated, may hold values from 0.5 to 8
- q_weight: bfloat16 [8192, 8192], P(None, 'tp'), may hold values from -0.0625 to 0.0625
- kv_weight: bfloat16 [8192, 2048], P(None, 'tp'), may hold values from -1 to 1
- dec_query: bfloat16 [128, 8192], P(('grp', 'role', 'tp')), parts along dimension 0, may hold values from -70 to 70
- dec_new_kv: bfloat16 [128, 2048], P(('grp', 'role', 'tp')), parts along dimension 0, may hold values from -6 to 6
- kv_pool: bfloat16 [3072, 16, 2048], P(('grp', 'role', 'tp')), parts along dimension 0, may hold values from -6 to 6
- page_table: int32 [128, 24], P(('grp', 'role', 'tp')), parts along dimension 0, may hold values from 0 to 95, as said below
- cache_lengths: int32 [128], P(('grp', 'role', 'tp')), parts along dimension 0, may hold values from 64 to 384, as said below
- handoff_slot: int32 [32, 4], P(('grp', 'role', 'tp')), parts along dimension 0, may hold values from 0 to 95, as said below
Outputs:
- prefill_context: bfloat16 [2, 1024, 8192], P('role', 'grp', 'tp'), parts along dimension 1
- decode_output: bfloat16 [128, 8192], P(('grp', 'role', 'tp')), parts along dimension 0
The draws below stay inside these ranges and needn't reach their ends.
There are 2 independent parts, one for each index of `grp`. The reference program is written for one: setup_inputs(seed, part) draws one part's arguments, and reference() takes and returns one part's arrays. A program takes and returns all parts, laid end to end along the dimension named above; an argument that names none is the same for every part. Nothing has to cross between parts.
Inputs may be any that keep to these rules, and one draw needn't show every extreme that they name: `page_table`: the 4 rows of each pool list distinct pages of that pool; together they list every page of it once. `cache_lengths`: some row of every draw holds 384 tokens. `handoff_slot`: the 4 pages of a pool are distinct, and each is a page that some row of that pool lists at a page-table entry lying wholly below its cache length.
All inputs are finite; a program needn't handle non-finite values.
Results may differ from the reference program's by a relative error of at most 0.017.
The reference program's roundings to bfloat16 on the way count: a program that leaves them out, or rounds other values in their place, can miss the bound.
Values may be sent and summed in bfloat16 or wider, within the bound.
No kernel may reach another device: no remote copies, remote signals or barrier semaphores. Data moves between devices by JAX's collectives and lax.ppermute only.
A program may use at most 192 MiB of HBM per device.

```python
import jax
import jax.numpy as jnp
from jax import lax

D = 8192
KVH = 8
HD = 128
PAGE = 16
MAXPG = 24
HB = 4
ROWS_DEV = 4
GROUP = 8
QW = 8192
KVW = 2048
TPP = 8
SUBS = 1
STRETCH = 512
PTOK = 512
POOL = 96
PART_DEVS = 16
ROWS = 64
N_ROLE = 2
N_TP = 8


def draw_stretch_tokens(key, part):
    first, second = jax.random.split(key, 2)
    scales = jnp.exp(jax.random.uniform(second, (N_ROLE, PTOK, 1), jnp.float32, 0.0, jnp.log(10.0)))
    values = jnp.clip(jax.random.normal(first, (N_ROLE, PTOK, D), jnp.float32), -6.0, 6.0)
    return (values * scales).astype(jnp.bfloat16)


def draw_norm_gain(key, part):
    values = 1.0 + 0.1 * jnp.clip(jax.random.normal(key, (D,), jnp.float32), -4.0, 4.0)
    return values.astype(jnp.bfloat16)


def draw_kv_weight(key, part):
    values = jnp.clip(jax.random.normal(key, (D, KVW), jnp.float32), -6.0, 6.0) * D ** (-0.5)
    return values.astype(jnp.bfloat16)


def draw_kv_pool(key, part):
    values = jnp.clip(jax.random.normal(key, (PART_DEVS * POOL, PAGE, KVW), jnp.float32), -6.0, 6.0)
    return values.astype(jnp.bfloat16)


def draw_dec_new_kv(key, part):
    values = jnp.clip(jax.random.normal(key, (ROWS, KVW), jnp.float32), -6.0, 6.0)
    return values.astype(jnp.bfloat16)


def draw_dec_query(key, part):
    values = jnp.clip(jax.random.normal(key, (ROWS, QW), jnp.float32), -6.0, 6.0)
    return values.astype(jnp.bfloat16)


def permuted_pool(one_key):
    return jax.random.permutation(one_key, POOL)


def cache_layout(key):
    folded = jax.random.fold_in(key, 4242)
    key_len, key_perm, key_row, key_full = jax.random.split(folded, 4)
    lengths = jax.random.randint(key_len, (ROWS,), HB * PAGE, MAXPG * PAGE + 1)
    longest = jax.random.randint(key_full, (), 0, ROWS)
    lengths = lengths.at[longest].set(MAXPG * PAGE)
    pool_keys = jax.random.split(key_perm, PART_DEVS)
    tables = jax.vmap(permuted_pool)(pool_keys).reshape(PART_DEVS, ROWS_DEV, MAXPG)
    chosen = jax.random.randint(key_row, (PART_DEVS, HB), 0, ROWS_DEV)
    owners = jnp.arange(PART_DEVS)[:, None]
    entries = jnp.arange(HB)[None, :]
    slots = tables[owners, chosen, entries]
    return (lengths.astype(jnp.int32), tables.reshape(ROWS, MAXPG).astype(jnp.int32), slots.astype(jnp.int32))


def draw_page_table(key, part):
    return cache_layout(key)[1]


def draw_cache_lengths(key, part):
    return cache_layout(key)[0]


def draw_handoff_slot(key, part):
    return cache_layout(key)[2]


def block_levels(key, dims, cuts, low, top_value):
    loudness, own = 1.0, jax.random.fold_in(key, 6)
    for axis_at, blocks in cuts:
        steps = jnp.exp(jax.random.uniform(jax.random.fold_in(own, axis_at), (blocks,), jnp.float32, low / len(cuts), top_value / len(cuts)))
        loudness = loudness * jnp.repeat(steps, dims[axis_at] // blocks).reshape([-1 if axis == axis_at else 1 for axis in range(len(dims))])
    return loudness


def noise(rng, dims, deviation, bound, cuts=(), held_as=jnp.bfloat16):
    values = jax.random.normal(rng, dims, jnp.float32) * deviation
    if len(cuts) > 0:
        values = block_levels(rng, dims, cuts, -0.22, 0.18) * values
    return jnp.clip(values, min=-bound, max=bound).astype(held_as)


def setup_inputs(seed: int = 0, part: int = 0) -> dict:
    key_of = jax.random.split(jax.random.key(seed), 11)
    own_keys = jax.random.split(jax.random.fold_in(key_of[10], part), 11)
    return {
        "stretch_tokens": draw_stretch_tokens(jax.random.fold_in(jax.random.fold_in(key_of[10], part), 71), part),
        "norm_gain": draw_norm_gain(jax.random.fold_in(key_of[10], 71), part),
        "q_weight": noise(key_of[2], (D, QW), D ** -0.5, 0.0625, ((1, 8),)),
        "kv_weight": draw_kv_weight(jax.random.fold_in(key_of[10], 71), part),
        "dec_query": draw_dec_query(jax.random.fold_in(jax.random.fold_in(key_of[10], part), 71), part),
        "dec_new_kv": draw_dec_new_kv(jax.random.fold_in(jax.random.fold_in(key_of[10], part), 71), part),
        "kv_pool": draw_kv_pool(jax.random.fold_in(jax.random.fold_in(key_of[10], part), 71), part),
        "page_table": draw_page_table(jax.random.fold_in(jax.random.fold_in(key_of[10], part), 71), part),
        "cache_lengths": draw_cache_lengths(jax.random.fold_in(jax.random.fold_in(key_of[10], part), 71), part),
        "handoff_slot": draw_handoff_slot(jax.random.fold_in(jax.random.fold_in(key_of[10], part), 71), part),
    }


norm_eps = 1e-05
rope_base = 500000.0

def rotate(matrix, first_col):
    count = matrix.shape[0]
    width = matrix.shape[1]
    pair_index = (first_col + jnp.arange(0, width, 2)) % HD // 2
    inverse = jnp.exp(-(2.0 * pair_index.astype(jnp.float32) / HD) * jnp.log(jnp.float32(rope_base)))
    angle = jnp.arange(count).astype(jnp.float32)[:, None] * inverse[None, :]
    cosine = jnp.cos(angle)
    sine = jnp.sin(angle)
    even_part = matrix[:, 0::2]
    odd_part = matrix[:, 1::2]
    turned = jnp.stack([even_part * cosine - odd_part * sine, even_part * sine + odd_part * cosine], axis=-1)
    return turned.reshape(count, width)

def prefill_stretch(tokens, norm_gain, q_weight, kv_weight):
    hidden = tokens.astype(jnp.float32)
    mean_sq = lax.optimization_barrier(jnp.mean(hidden * hidden, axis=-1, keepdims=True))
    normed = (hidden * lax.rsqrt(mean_sq + norm_eps) * norm_gain.astype(jnp.float32)).astype(jnp.bfloat16)
    queries = rotate(jnp.dot(normed, q_weight, preferred_element_type=jnp.float32), 0).astype(jnp.bfloat16)
    projected = jnp.dot(normed, kv_weight, preferred_element_type=jnp.float32)
    count = tokens.shape[0]
    heads = projected.reshape(count, KVH, 2 * HD)
    keys = rotate(heads[:, :, :HD].reshape(count, KVH * HD), 0).reshape(count, KVH, HD)
    joined = jnp.concatenate([keys, heads[:, :, HD:]], axis=2).astype(jnp.bfloat16)
    causal = jnp.arange(count)[:, None] >= jnp.arange(count)[None, :]

    def one_group(index):
        group_q = lax.dynamic_slice_in_dim(queries, index * (GROUP * HD), GROUP * HD, 1)
        group_q = group_q.reshape(count, GROUP, HD).astype(jnp.float32)
        head_kv = lax.dynamic_slice_in_dim(joined, index, 1, 1)[:, 0, :].astype(jnp.float32)
        group_k = head_kv[:, :HD]
        group_v = head_kv[:, HD:]
        scores = jnp.einsum('tjd,ud->jtu', group_q, group_k) * HD ** (-0.5)
        scores = jnp.where(causal[None], scores, -1e+30)
        highest = lax.optimization_barrier(jnp.max(scores, axis=-1, keepdims=True))
        weights = jnp.exp(scores - highest)
        weights = (weights / lax.optimization_barrier(jnp.sum(weights, axis=-1, keepdims=True))).astype(jnp.bfloat16)
        mixed = jnp.einsum('jtu,ud->tjd', weights.astype(jnp.float32), group_v)
        return mixed.astype(jnp.bfloat16)
    context = lax.map(one_group, jnp.arange(KVH).astype(jnp.int32))
    context = jnp.transpose(context, (1, 0, 2, 3)).reshape(count, QW)
    return (context, joined.reshape(count, KVW))

def decode_rows(pool_pages, tables, lengths, queries, new_kv):
    rows = tables.shape[0]
    cache = pool_pages[tables].reshape(rows, MAXPG * PAGE, KVH, 2 * HD)
    keys = cache[..., :HD].astype(jnp.float32)
    values = cache[..., HD:].astype(jnp.float32)
    query_heads = queries.reshape(rows, KVH, GROUP, HD).astype(jnp.float32)
    own = new_kv.reshape(rows, KVH, 2 * HD).astype(jnp.float32)
    own_key = own[..., :HD]
    own_value = own[..., HD:]
    scale = HD ** (-0.5)
    scores = jnp.einsum('rgjd,rcgd->rgjc', query_heads, keys) * scale
    live = jnp.arange(MAXPG * PAGE)[None, :] < lengths[:, None]
    scores = jnp.where(live[:, None, None, :], scores, -1e+30)
    own_score = jnp.einsum('rgjd,rgd->rgj', query_heads, own_key) * scale
    highest = jnp.maximum(lax.optimization_barrier(jnp.max(scores, axis=-1)), own_score)
    weights = jnp.exp(scores - highest[..., None])
    own_weight = jnp.exp(own_score - highest)
    total = lax.optimization_barrier(jnp.sum(weights, axis=-1)) + own_weight
    weights = (weights / total[..., None]).astype(jnp.bfloat16)
    own_weight = (own_weight / total).astype(jnp.bfloat16)
    mixed = jnp.einsum('rgjc,rcgd->rgjd', weights.astype(jnp.float32), values)
    mixed = mixed + own_weight.astype(jnp.float32)[..., None] * own_value[:, :, None, :]
    return mixed.reshape(rows, QW).astype(jnp.bfloat16)

def reference(stretch_tokens, norm_gain, q_weight, kv_weight, dec_query, dec_new_kv, kv_pool, page_table, cache_lengths, handoff_slot):
    block_rows = HB * PAGE
    block_cols = QW // TPP
    contexts = []
    side_kv = []
    for side in range(N_ROLE):
        blocks = stretch_tokens[side].reshape(TPP, SUBS, block_rows, D)
        stretch_contexts = []
        stretch_kvs = []
        for stretch in range(SUBS):
            tokens = blocks[:, stretch].reshape(STRETCH, D)
            context, joined = prefill_stretch(tokens, norm_gain, q_weight, kv_weight)
            stretch_contexts.append(context)
            stretch_kvs.append(joined)
        context = jnp.stack(stretch_contexts).reshape(SUBS, STRETCH, TPP, block_cols)
        context = jnp.transpose(context, (1, 2, 0, 3)).reshape(STRETCH, SUBS * QW)
        contexts.append(context)
        handed = jnp.stack(stretch_kvs).reshape(SUBS, TPP, block_rows, KVW)
        handed = jnp.transpose(handed, (1, 0, 2, 3)).reshape(N_TP, HB, PAGE, KVW)
        side_kv.append(handed)
    prefill_context = jnp.stack(contexts)
    handed = jnp.stack(side_kv)[::-1].reshape(PART_DEVS, HB, PAGE, KVW)
    pools = kv_pool.reshape(PART_DEVS, POOL, PAGE, KVW)
    owners = jnp.arange(PART_DEVS).astype(jnp.int32)[:, None]
    pools = pools.at[owners, handoff_slot].set(handed)
    tables = page_table.reshape(PART_DEVS, ROWS_DEV, MAXPG)
    lengths = cache_lengths.reshape(PART_DEVS, ROWS_DEV)
    queries = dec_query.reshape(PART_DEVS, ROWS_DEV, QW)
    new_kv = dec_new_kv.reshape(PART_DEVS, ROWS_DEV, KVW)

    def one_pool(items):
        return decode_rows(items[0], items[1], items[2], items[3], items[4])
    decode_output = lax.map(one_pool, (pools, tables, lengths, queries, new_kv)).reshape(ROWS, QW)
    return (prefill_context, decode_output)
```

```python
import functools

import jax
import jax.numpy as jnp
from jax import lax
from jax.experimental import pallas as pl
from jax.experimental.pallas import tpu as pltpu
from jax.sharding import PartitionSpec as P

KVH = 8
HD = 128
PAGE = 16
GROUP = 8
MASKED = -1e30

norm_eps = 1e-05
rope_base = 500000.0


MIB = 2**20


def swapped(value, axis, bit):
    mask = 2**bit
    pairs = [(source, source ^ mask) for source in range(lax.axis_size(axis))]
    return lax.ppermute(value, axis, pairs)


def from_behind(value, axis, steps):
    count = lax.axis_size(axis)
    pairs = [(source, (source + steps) % count) for source in range(count)]
    return lax.ppermute(value, axis, pairs)


def ordered_pair(mine, other, upper, axis):
    first = jnp.where(upper == 1, other, mine)
    second = jnp.where(upper == 1, mine, other)
    return jnp.concatenate((first, second), axis=axis)


def spread_members(blocks, member, low_bit, member_bits, mover):
    members = blocks.shape[0]
    order = jnp.bitwise_xor(member, jnp.arange(members))
    buffer = blocks[order]
    for step in range(member_bits):
        width = 2**step
        view = buffer.reshape(members // (2 * width), 2, width, blocks.shape[1], blocks.shape[2])
        arrived = mover(view[:, 1], low_bit + step)
        buffer = jnp.stack((view[:, 0], arrived), axis=1).reshape(blocks.shape)
    return buffer[order]


def rotation_tables(count, width, first_col, only_keys):
    columns = first_col + jnp.arange(width)
    pair_index = columns % HD // 2
    inverse = jnp.exp(
        -(2.0 * pair_index.astype(jnp.float32) / HD) * jnp.log(jnp.float32(rope_base))
    )
    angle = jnp.arange(count).astype(jnp.float32)[:, None] * inverse[None, :]
    cosine = jnp.cos(angle)
    sine = jnp.where(columns % 2 == 0, -1.0, 1.0)[None, :] * jnp.sin(angle)
    if only_keys:
        is_key = (columns % (2 * HD) < HD)[None, :]
        cosine = jnp.where(is_key, cosine, 1.0)
        sine = jnp.where(is_key, sine, 0.0)
    return cosine, sine


def turned(tile, cosine, sine):
    lane = lax.broadcasted_iota(jnp.int32, tile.shape, 1)
    after = pltpu.roll(tile, HD - 1, 1)
    before = pltpu.roll(tile, 1, 1)
    return tile * cosine + jnp.where(lane % 2 == 0, after, before) * sine


def project_kernel(chunk_rows, jobs, depth, starts, *refs):
    n = len(chunk_rows)
    x_refs, gain = refs[:n], refs[n]
    job_refs = refs[n + 1 : n + 1 + 3 * jobs]
    outs = refs[n + 1 + 3 * jobs : n + 1 + 4 * jobs]
    scale_ref = refs[n + 1 + 4 * jobs]
    accs = refs[n + 2 + 4 * jobs :]
    step = pl.program_id(0)
    width = x_refs[0].shape[1]

    @pl.when(step == 0)
    def _():
        first = 0
        for x_ref, rows in zip(x_refs, chunk_rows):

            def add(i, total):
                part = x_ref[:, pl.ds(pl.multiple_of(i * 512, 512), 512)].astype(jnp.float32)
                part = part * part
                return total + (
                    (part[:, :128] + part[:, 128:256]) + (part[:, 256:384] + part[:, 384:])
                )

            total = lax.fori_loop(0, width // 512, add, jnp.zeros((rows, 128), jnp.float32))
            mean_sq = jnp.sum(total, axis=1, keepdims=True) / width
            scale_ref[first : first + rows, :] = jnp.broadcast_to(
                lax.rsqrt(mean_sq + norm_eps), (rows, 128)
            )
            first += rows

    here = pl.ds(pl.multiple_of(step * depth, depth), depth)
    gain_here = gain[:, here].astype(jnp.float32)
    parts = []
    first = 0
    for x_ref, rows in zip(x_refs, chunk_rows):
        part = x_ref[:, here].astype(jnp.float32)
        parts.append(
            (part * scale_ref[first : first + rows, 0:1] * gain_here).astype(jnp.bfloat16)
        )
        first += rows
    normed = parts[0] if n == 1 else jnp.concatenate(parts, axis=0)
    for j in range(jobs):
        product = jnp.dot(normed, job_refs[3 * j][...], preferred_element_type=jnp.float32)

        @pl.when(step == 0)
        def _(product=product, j=j):
            accs[j][...] = product

        @pl.when(step > 0)
        def _(product=product, j=j):
            accs[j][...] += product

    @pl.when(step == pl.num_programs(0) - 1)
    def _():
        for j in range(jobs):
            cos_ref, sin_ref = job_refs[3 * j + 1], job_refs[3 * j + 2]
            table = cos_ref.shape[1]
            first = 0
            for i, rows in enumerate(chunk_rows):
                where = pl.ds(pl.multiple_of(starts[i], rows), rows)
                for col in range(0, accs[j].shape[1], HD):
                    at = col % table
                    outs[j][first : first + rows, col : col + HD] = turned(
                        accs[j][first : first + rows, col : col + HD],
                        cos_ref[where, at : at + HD],
                        sin_ref[where, at : at + HD],
                    ).astype(jnp.bfloat16)
                first += rows


def project(chunks, starts, gain, jobs):
    chunk_rows = tuple(chunk.shape[0] for chunk in chunks)
    rows = sum(chunk_rows)
    width = chunks[0].shape[1]
    columns = [job[0].shape[1] for job in jobs]
    depth = 1024 if sum(columns) > 512 else 2048
    whole = lambda k, starts: (0, 0)
    in_specs = [pl.BlockSpec(c.shape, whole, pipeline_mode=pl.Buffered(1)) for c in chunks]
    in_specs.append(pl.BlockSpec((1, width), whole, pipeline_mode=pl.Buffered(1)))
    operands = list(chunks) + [gain]
    for weight, cosine, sine in jobs:
        in_specs.append(pl.BlockSpec((depth, weight.shape[1]), lambda k, starts: (k, 0)))
        in_specs += [pl.BlockSpec(cosine.shape, whole, pipeline_mode=pl.Buffered(1))] * 2
        operands += [weight, cosine, sine]
    return pl.pallas_call(
        functools.partial(project_kernel, chunk_rows, len(jobs), depth),
        out_shape=[jax.ShapeDtypeStruct((rows, c), jnp.bfloat16) for c in columns],
        grid_spec=pltpu.PrefetchScalarGridSpec(
            num_scalar_prefetch=1,
            grid=(width // depth,),
            in_specs=in_specs,
            out_specs=[pl.BlockSpec((rows, c), whole) for c in columns],
            scratch_shapes=[pltpu.VMEM((rows, 128), jnp.float32)]
            + [pltpu.VMEM((rows, c), jnp.float32) for c in columns],
        ),
        compiler_params=pltpu.CompilerParams(
            dimension_semantics=("arbitrary",), vmem_limit_bytes=32 * MIB
        ),
        cost_estimate=pl.CostEstimate(
            flops=2 * rows * width * sum(columns),
            bytes_accessed=2 * width * (rows + sum(columns)),
            transcendentals=0,
        ),
        name="project",
    )(jnp.stack(starts).astype(jnp.int32), *operands)


def attend_kernel(chunk_rows, sizes, starts, *refs):
    n = len(sizes)
    q_refs, kv_refs, out, q_all, kv_all = refs[:n], refs[n : 2 * n], *refs[2 * n :]
    count = q_all.shape[0]
    i = 0
    for q_ref, kv_ref, size in zip(q_refs, kv_refs, sizes):
        first = 0
        while first < size:
            rows = chunk_rows[i]
            where = pl.ds(pl.multiple_of(starts[i], rows), rows)
            q_all[where, :] = q_ref[first : first + rows, :]
            kv_all[where, :] = kv_ref[first : first + rows, :]
            first += rows
            i += 1
    tile = min(128, count)
    scale = HD ** (-0.5)
    heads = q_all.shape[1] // HD
    row = lax.broadcasted_iota(jnp.int32, (tile, tile), 0)
    col = lax.broadcasted_iota(jnp.int32, (tile, tile), 1)
    triangle = row >= col
    dims = (((1,), (1,)), ((), ()))
    for j in range(count // tile):
        low = j * tile

        def one_head(h, carry, low=low):
            lanes = pl.ds(pl.multiple_of(h * HD, HD), HD)
            query = q_all[low : low + tile, lanes]
            edge = (
                lax.dot_general(
                    query,
                    kv_all[low : low + tile, :HD],
                    dims,
                    preferred_element_type=jnp.float32,
                )
                * scale
            )
            edge = jnp.where(triangle, edge, MASKED)
            highest = jnp.max(edge, axis=1, keepdims=True)
            if low:
                body = (
                    lax.dot_general(
                        query, kv_all[:low, :HD], dims, preferred_element_type=jnp.float32
                    )
                    * scale
                )
                highest = jnp.maximum(highest, jnp.max(body, axis=1, keepdims=True))
                body = jnp.exp(body - highest)
            edge = jnp.exp(edge - highest)
            total = jnp.sum(edge, axis=1, keepdims=True)
            if low:
                total = total + jnp.sum(body, axis=1, keepdims=True)
            share = 1.0 / total
            mixed = jnp.dot(
                (edge * share).astype(jnp.bfloat16),
                kv_all[low : low + tile, HD:],
                preferred_element_type=jnp.float32,
            )
            if low:
                mixed = mixed + jnp.dot(
                    (body * share).astype(jnp.bfloat16),
                    kv_all[:low, HD:],
                    preferred_element_type=jnp.float32,
                )
            out[low : low + tile, lanes] = mixed.astype(jnp.bfloat16)
            return carry

        lax.fori_loop(0, heads, one_head, 0, unroll=2)


def attend(queries, kvs, chunk_rows, starts):
    count = sum(chunk_rows)
    q_width = queries[0].shape[1]
    whole = lambda i, starts: (0, 0)
    spec = lambda a: pl.BlockSpec(a.shape, whole, pipeline_mode=pl.Buffered(1))
    return pl.pallas_call(
        functools.partial(attend_kernel, tuple(chunk_rows), tuple(q.shape[0] for q in queries)),
        out_shape=jax.ShapeDtypeStruct((count, q_width), jnp.bfloat16),
        grid_spec=pltpu.PrefetchScalarGridSpec(
            num_scalar_prefetch=1,
            grid=(1,),
            in_specs=[spec(a) for a in (*queries, *kvs)],
            out_specs=pl.BlockSpec((count, q_width), whole),
            scratch_shapes=[
                pltpu.VMEM((count, q_width), jnp.bfloat16),
                pltpu.VMEM((count, 2 * HD), jnp.bfloat16),
            ],
        ),
        compiler_params=pltpu.CompilerParams(vmem_limit_bytes=32 * MIB),
        cost_estimate=pl.CostEstimate(
            flops=2 * count * count * q_width,
            bytes_accessed=4 * count * (q_width + 2 * HD),
            transcendentals=count * count * q_width // HD // 2,
        ),
        name="attend",
    )(jnp.stack(starts).astype(jnp.int32), *queries, *kvs)


def decode_old_kernel(tables, q_ref, own_ref, live_ref, pool, acc_ref, top_ref, sum_ref, cache, sems):
    rows, pages = tables.shape
    scale = HD ** (-0.5)
    dims = (((1,), (1,)), ((), ()))
    for r in range(rows):

        @pl.loop(0, pages)
        def _(p, r=r):
            pltpu.make_async_copy(pool.at[tables[r, p]], cache.at[r, p], sems.at[r]).start()

    for r in range(rows):
        pltpu.make_async_copy(pool.at[pl.ds(0, pages)], cache.at[r], sems.at[r]).wait()
        kv = cache.at[r].reshape(pages * PAGE, cache.shape[3])
        mine = slice(r * GROUP, (r + 1) * GROUP)
        scores, own_scores = [], []
        for h in range(KVH):
            query = q_ref[h, mine, :]
            scores.append(
                lax.dot_general(
                    query.astype(jnp.bfloat16),
                    kv[:, 2 * h * HD : (2 * h + 1) * HD],
                    dims,
                    preferred_element_type=jnp.float32,
                )
            )
            own_key = own_ref[r : r + 1, 2 * h * HD : (2 * h + 1) * HD].astype(jnp.float32)
            own_scores.append(jnp.sum(query * own_key, axis=1, keepdims=True))
        score = jnp.concatenate(scores, axis=0) * scale
        own_score = jnp.concatenate(own_scores, axis=0) * scale
        score = jnp.where(live_ref[r : r + 1, :] > 0.0, score, MASKED)
        highest = jnp.maximum(jnp.max(score, axis=1, keepdims=True), own_score)
        weight = jnp.exp(score - highest)
        own_weight = jnp.exp(own_score - highest)
        total = jnp.sum(weight, axis=1, keepdims=True) + own_weight
        weight = weight.astype(jnp.bfloat16)
        for h in range(KVH):
            here = slice(h * GROUP, (h + 1) * GROUP)
            own_value = own_ref[r : r + 1, (2 * h + 1) * HD : (2 * h + 2) * HD].astype(jnp.float32)
            mixed = jnp.dot(
                weight[here],
                kv[:, (2 * h + 1) * HD : (2 * h + 2) * HD],
                preferred_element_type=jnp.float32,
            )
            acc_ref[h, mine, :] = mixed + own_weight[here] * own_value
            top_ref[h, mine, :] = jnp.broadcast_to(highest[here], (GROUP, HD))
            sum_ref[h, mine, :] = jnp.broadcast_to(total[here], (GROUP, HD))


def decode_old(pool, tables, live, queries, new_kv):
    rows, pages = tables.shape
    state = jax.ShapeDtypeStruct((KVH, rows * GROUP, HD), jnp.float32)
    vmem = pl.BlockSpec(memory_space=pltpu.VMEM)
    return pl.pallas_call(
        decode_old_kernel,
        out_shape=[state] * 3,
        in_specs=[
            pl.BlockSpec(memory_space=pltpu.SMEM),
            vmem,
            vmem,
            vmem,
            pl.BlockSpec(memory_space=pl.ANY),
        ],
        out_specs=[vmem] * 3,
        scratch_shapes=[
            pltpu.VMEM((rows, pages) + pool.shape[1:], pool.dtype),
            pltpu.SemaphoreType.DMA((rows,)),
        ],
        compiler_params=pltpu.CompilerParams(vmem_limit_bytes=32 * MIB),
        cost_estimate=pl.CostEstimate(
            flops=4 * rows * pages * PAGE * KVH * GROUP * HD,
            bytes_accessed=2 * rows * pages * PAGE * pool.shape[2],
            transcendentals=rows * pages * PAGE * KVH * GROUP,
        ),
        name="decode_old",
    )(tables, queries, new_kv, live, pool)


def decode_new_kernel(heads, q_ref, mask_ref, acc_ref, top_ref, sum_ref, *refs):
    pieces, out = refs[:-1], refs[-1]
    scale = HD ** (-0.5)
    dims = (((1,), (1,)), ((), ()))
    allowed = mask_ref[...] > 0.0
    for k in range(KVH):
        h = heads[k]
        score = (
            lax.dot_general(
                q_ref[h].astype(jnp.bfloat16),
                pieces[k][:, :HD],
                dims,
                preferred_element_type=jnp.float32,
            )
            * scale
        )
        score = jnp.where(allowed, score, MASKED)
        before = top_ref[h]
        highest = jnp.maximum(before, jnp.max(score, axis=1, keepdims=True))
        keep = jnp.exp(before - highest)
        weight = jnp.exp(score - highest[:, :1])
        total = sum_ref[h] * keep + jnp.sum(weight, axis=1, keepdims=True)
        mixed = acc_ref[h] * keep + jnp.dot(
            weight.astype(jnp.bfloat16), pieces[k][:, HD:], preferred_element_type=jnp.float32
        )
        out[h] = (mixed / total).astype(jnp.bfloat16)


def decode_new(pieces, heads, allowed, queries, state):
    vmem = pl.BlockSpec(memory_space=pltpu.VMEM)
    return pl.pallas_call(
        decode_new_kernel,
        out_shape=jax.ShapeDtypeStruct(queries.shape, jnp.bfloat16),
        in_specs=[pl.BlockSpec(memory_space=pltpu.SMEM)] + [vmem] * (5 + len(pieces)),
        out_specs=vmem,
        compiler_params=pltpu.CompilerParams(vmem_limit_bytes=16 * MIB),
        name="decode_new",
    )(heads, queries, allowed, *state, *pieces)


def exchange_plan(members, subs):
    def pairs(links):
        return [
            (source * subs + sub, target * subs + sub)
            for source, target in links
            for sub in range(subs)
        ]

    side = [(m, m ^ 1) for m in range(members)]
    outer = [(m, m ^ 2) for m in range(members)]
    outward = [(m, m ^ 2) for m in range(members) if m // 2 in (1, 2)]
    inner = [(m, m ^ 6) for m in range(members) if m // 2 in (1, 2)]
    return pairs(side), pairs(outer), pairs(outward), pairs(inner)


def local(
    stretch_tokens,
    norm_gain,
    q_weight,
    kv_weight,
    dec_query,
    dec_new_kv,
    kv_pool,
    page_table,
    cache_lengths,
    handoff_slot,
):
    devices_tp = lax.axis_size("tp")
    members = min(16, devices_tp)
    subs = devices_tp // members
    sub_bits = subs.bit_length() - 1
    member_bits = members.bit_length() - 1
    headmates = members // KVH
    position = lax.axis_index("tp")
    member = position // subs
    tokens = stretch_tokens[0]
    block_rows, width = tokens.shape
    count = members * block_rows
    gain = norm_gain.reshape(1, width)

    rows, pages = page_table.shape
    slots = handoff_slot[0]
    listed = page_table[:, :, None] == slots[None, None, :]
    handed = jnp.repeat(jnp.any(listed, axis=2), PAGE, axis=1)
    live = (jnp.arange(pages * PAGE)[None, :] < cache_lengths[:, None]) & ~handed
    live = live.astype(jnp.float32)
    allowed = jnp.repeat(
        jnp.repeat(jnp.any(listed, axis=1), GROUP, axis=0), PAGE, axis=1
    ).astype(jnp.float32)
    dec_heads = (
        dec_query.reshape(rows, KVH, GROUP, HD)
        .transpose(1, 0, 2, 3)
        .reshape(KVH, rows * GROUP, HD)
        .astype(jnp.float32)
    )

    q_block = q_weight
    kv_block = kv_weight
    for bit in range(sub_bits):
        other_q = swapped(q_block, "tp", bit)
        other_kv = swapped(kv_block, "tp", bit)
        upper = position // 2**bit % 2
        q_block = ordered_pair(q_block, other_q, upper, 1)
        kv_block = ordered_pair(kv_block, other_kv, upper, 1)
    q_cos, q_sin = rotation_tables(count, HD, 0, False)
    kv_width = kv_block.shape[1]
    kv_cos, kv_sin = rotation_tables(count, kv_width, member * kv_width, True)
    q_job = (q_block, q_cos, q_sin)
    kv_job = (kv_block, kv_cos, kv_sin)
    bar = lax.optimization_barrier

    def old_state():
        return decode_old(kv_pool, page_table, live, dec_heads, dec_new_kv)

    if members == 8 and headmates == 1 and block_rows % 32 == 0:
        half = block_rows // 2
        side, outer, outward, inner = exchange_plan(members, subs)
        move = lambda value, pairs: lax.ppermute(value, "tp", pairs)
        row = member // 2
        at_end = (row == 0) | (row == 3)

        def start_of(offset, c):
            return jnp.bitwise_xor(member, offset) * block_rows + c * half

        def hand(kv, offset):
            pairs = [
                (r * devices_tp + m * subs + s, (1 - r) * devices_tp + (m ^ offset) * subs + s)
                for r in range(2)
                for m in range(members)
                for s in range(subs)
            ]
            return lax.ppermute(kv, ("role", "tp"), pairs)

        own = [tokens[:half], tokens[half:]]
        y, e1, e2 = {}, {}, {}
        for c in range(2):
            y[c], e1[c], e2[c] = move(own[c], side), move(own[c], outer), move(own[c], inner)
        state = old_state()
        q0, kv0 = project([tokens], [member * block_rows], gain, [q_job, kv_job])
        piece = {0: hand(kv0, 0)}
        near = {}
        for c in range(2):
            e1[c], e2[c], y[c] = bar((e1[c], e2[c], y[c]))
            e1[2 + c] = move(e2[c], outward)
            e2[2 + c] = move(e1[c], inner)
            y[2 + c] = move(e1[c], side)
        qa, kva = project(
            [e1[0], e1[1], y[0], y[1]],
            [start_of(o, c) for o in (2, 1) for c in range(2)],
            gain,
            [q_job, kv_job],
        )
        piece[2] = hand(kva[:block_rows], 2)
        piece[1] = hand(kva[block_rows:], 1)
        two, three = {}, {}
        for c in range(2):
            e1[2 + c], e2[2 + c], y[2 + c] = bar((e1[2 + c], e2[2 + c], y[2 + c]))
            two[c] = jnp.where(at_end, e1[2 + c], e2[2 + c])
            e1[4 + c] = move(e2[2 + c], outward)
            y[4 + c] = move(two[c], side)
        qb, kvb = project(
            [two[0], two[1], y[2], y[3]],
            [start_of(o, c) for o in (4, 3) for c in range(2)],
            gain,
            [q_job, kv_job],
        )
        piece[4] = hand(kvb[:block_rows], 4)
        piece[3] = hand(kvb[block_rows:], 3)
        for c in range(2):
            e1[4 + c], y[4 + c] = bar((e1[4 + c], y[4 + c]))
            three[c] = jnp.where(at_end, e1[4 + c], e2[c])
            if c == 0:
                e1[6] = move(y[4], outer)
            else:
                y[6] = move(three[1], side)
        qc, kvc = project(
            [three[0], three[1], y[4], y[5]],
            [start_of(o, c) for o in (6, 5) for c in range(2)],
            gain,
            [q_job, kv_job],
        )
        piece[6] = hand(kvc[:block_rows], 6)
        piece[5] = hand(kvc[block_rows:], 5)
        last = [e1[6], y[6]]
        last_starts = [start_of(7, c) for c in range(2)]
        (kvd,) = project(last, last_starts, gain, [kv_job])
        piece[7] = hand(kvd, 7)
        (qd,) = project(last, last_starts, gain, [q_job])
        starts = [start_of(o, c) for o in (0, 2, 1, 4, 3, 6, 5, 7) for c in range(2)]
        context = attend(
            [q0, qa, qb, qc, qd], [kv0, kva, kvb, kvc, kvd], [half] * (2 * members), starts
        )
        pieces = [piece[k] for k in range(members)]
        piece_heads = jnp.bitwise_xor(member, jnp.arange(members)).astype(jnp.int32)
    else:
        state = old_state()
        moving = tokens
        queries, local_kvs, order = [], [], []
        group, group_ids = [tokens], [member]
        for step in range(members):
            if step:
                moving = from_behind(moving, "tp", subs)
                group.append(moving)
                group_ids.append((member - step) % members)
            if len(group) == min(4, members) or step == members - 1:
                q_part, kv_part = project(
                    group, [i * block_rows for i in group_ids], gain, [q_job, kv_job]
                )
                queries.append(q_part)
                local_kvs.append(kv_part)
                order += group_ids
                group, group_ids = [], []
        arrived_kv = jnp.concatenate(local_kvs, axis=0).reshape(members, block_rows, kv_width)
        local_kv = arrived_kv[jnp.argsort(jnp.stack(order))].reshape(count, kv_width)
        head_kv = local_kv
        for step in range(headmates.bit_length() - 1):
            other = swapped(head_kv, "tp", sub_bits + step)
            head_kv = ordered_pair(head_kv, other, member // 2**step % 2, 1)
        arrived_q = jnp.concatenate(queries, axis=0).reshape(members, block_rows, -1)
        all_q = arrived_q[jnp.argsort(jnp.stack(order))].reshape(count, -1)
        context = attend([all_q], [head_kv], [count], [jnp.int32(0)])
        crossed = swapped(local_kv, "role", 0)
        received = spread_members(
            crossed.reshape(members, block_rows, kv_width),
            member,
            sub_bits,
            member_bits,
            lambda part, bit: swapped(part, "tp", bit),
        )
        arrived = jnp.transpose(received, (1, 0, 2)).reshape(block_rows, members * kv_width)
        pieces = [arrived[:, k * 2 * HD : (k + 1) * 2 * HD] for k in range(KVH)]
        piece_heads = jnp.arange(KVH).astype(jnp.int32)

    decoded = decode_new(pieces, piece_heads, allowed, dec_heads, state)
    decoded = (
        decoded.reshape(KVH, rows, GROUP, HD).transpose(1, 0, 2, 3).reshape(rows, KVH * GROUP * HD)
    )
    return (context[None], decoded)


def solution(mesh):
    in_specs = (
        P("role", ("grp", "tp"), None),
        P(),
        P(None, "tp"),
        P(None, "tp"),
        P(("grp", "role", "tp"), None),
        P(("grp", "role", "tp"), None),
        P(("grp", "role", "tp"), None, None),
        P(("grp", "role", "tp"), None),
        P(("grp", "role", "tp")),
        P(("grp", "role", "tp"), None),
    )
    out_specs = (P("role", "grp", "tp"), P(("grp", "role", "tp"), None))
    return jax.shard_map(local, mesh=mesh, in_specs=in_specs, out_specs=out_specs, check_vma=False)
```

```python
import functools

import jax
import jax.numpy as jnp
from jax import lax
from jax.experimental import pallas as pl
from jax.experimental.pallas import tpu as pltpu
from jax.sharding import PartitionSpec as P

KVH = 8
HD = 128
PAGE = 16
GROUP = 8
MASKED = -1e30

norm_eps = 1e-05
rope_base = 500000.0


LOG2E = 1.4426950408889634
VMEM_LIMIT = 16 * 2**20


def swapped(value, axis, bit):
    mask = 2**bit
    pairs = [(source, source ^ mask) for source in range(lax.axis_size(axis))]
    return lax.ppermute(value, axis, pairs)


def from_behind(value, axis, steps):
    count = lax.axis_size(axis)
    pairs = [(source, (source + steps) % count) for source in range(count)]
    return lax.ppermute(value, axis, pairs)


def ordered_pair(mine, other, upper, axis):
    first = jnp.where(upper == 1, other, mine)
    second = jnp.where(upper == 1, mine, other)
    return jnp.concatenate((first, second), axis=axis)


def spread_members(blocks, member, low_bit, member_bits, mover):
    members = blocks.shape[0]
    order = jnp.bitwise_xor(member, jnp.arange(members))
    buffer = blocks[order]
    for step in range(member_bits):
        width = 2**step
        view = buffer.reshape(members // (2 * width), 2, width, blocks.shape[1], blocks.shape[2])
        arrived = mover(view[:, 1], low_bit + step)
        buffer = jnp.stack((view[:, 0], arrived), axis=1).reshape(blocks.shape)
    return buffer[order]


def rotation_tables(count, width, first_col, only_keys):
    columns = first_col + jnp.arange(width)
    pair_index = columns % HD // 2
    inverse = jnp.exp(
        -(2.0 * pair_index.astype(jnp.float32) / HD) * jnp.log(jnp.float32(rope_base))
    )
    angle = jnp.arange(count).astype(jnp.float32)[:, None] * inverse[None, :]
    cosine = jnp.cos(angle)
    sine = jnp.where(columns % 2 == 0, -1.0, 1.0)[None, :] * jnp.sin(angle)
    if only_keys:
        is_key = (columns % (2 * HD) < HD)[None, :]
        cosine = jnp.where(is_key, cosine, 1.0)
        sine = jnp.where(is_key, sine, 0.0)
    return cosine, sine


def turned(tile, cosine, sine):
    lane = lax.broadcasted_iota(jnp.int32, tile.shape, 1)
    after = pltpu.roll(tile, HD - 1, 1)
    before = pltpu.roll(tile, 1, 1)
    return tile * cosine + jnp.where(lane % 2 == 0, after, before) * sine


def project_kernel(chunk_rows, jobs, starts, *refs):
    n = len(chunk_rows)
    x_refs, gain = refs[:n], refs[n]
    job_refs = refs[n + 1 : n + 1 + 3 * jobs]
    outs = refs[n + 1 + 3 * jobs : n + 1 + 4 * jobs]
    normed = refs[n + 1 + 4 * jobs]
    width = normed.shape[1]
    part = 512
    first = 0
    for x_ref, rows in zip(x_refs, chunk_rows):

        def add(i, total, x_ref=x_ref):
            tile = x_ref[:, pl.ds(pl.multiple_of(i * part, part), part)].astype(jnp.float32)
            tile = tile * tile
            for col in range(0, part, 128):
                total = total + tile[:, col : col + 128]
            return total

        total = lax.fori_loop(0, width // part, add, jnp.zeros((rows, 128), jnp.float32))
        mean_sq = jnp.sum(total, axis=1, keepdims=True) / width
        scale = lax.rsqrt(mean_sq + norm_eps)

        def write(i, carry, x_ref=x_ref, rows=rows, first=first, scale=scale):
            here = pl.ds(pl.multiple_of(i * part, part), part)
            normed[first : first + rows, here] = (
                x_ref[:, here].astype(jnp.float32) * scale * gain[:, here].astype(jnp.float32)
            ).astype(jnp.bfloat16)
            return carry

        lax.fori_loop(0, width // part, write, 0)
        first += rows
    for j in range(jobs):
        weight, cos_ref, sin_ref = job_refs[3 * j : 3 * j + 3]
        table = cos_ref.shape[1]
        columns = weight.shape[1]
        tile = min(256, columns)
        for low in range(0, columns, tile):
            product = jnp.dot(
                normed[...], weight[:, low : low + tile], preferred_element_type=jnp.float32
            )
            first = 0
            for i, rows in enumerate(chunk_rows):
                where = pl.ds(pl.multiple_of(starts[i], rows), rows)
                for col in range(low, low + tile, HD):
                    at = col % table
                    outs[j][first : first + rows, col : col + HD] = turned(
                        product[first : first + rows, col - low : col - low + HD],
                        cos_ref[where, at : at + HD],
                        sin_ref[where, at : at + HD],
                    ).astype(jnp.bfloat16)
                first += rows


def project(chunks, starts, gain, jobs):
    chunk_rows = tuple(chunk.shape[0] for chunk in chunks)
    rows = sum(chunk_rows)
    width = chunks[0].shape[1]
    columns = [job[0].shape[1] for job in jobs]
    operands = [*chunks, gain, *(part for job in jobs for part in job)]
    vmem = pl.BlockSpec(memory_space=pltpu.VMEM)
    return pl.pallas_call(
        functools.partial(project_kernel, chunk_rows, len(jobs)),
        out_shape=[jax.ShapeDtypeStruct((rows, c), jnp.bfloat16) for c in columns],
        in_specs=[pl.BlockSpec(memory_space=pltpu.SMEM)] + [vmem] * len(operands),
        out_specs=[vmem] * len(columns),
        scratch_shapes=[pltpu.VMEM((rows, width), jnp.bfloat16)],
        compiler_params=pltpu.CompilerParams(vmem_limit_bytes=VMEM_LIMIT),
        cost_estimate=pl.CostEstimate(
            flops=2 * rows * width * sum(columns),
            bytes_accessed=2 * width * (rows + sum(columns)),
            transcendentals=0,
        ),
        name="project",
    )(jnp.stack(starts).astype(jnp.int32), *operands)


def attend_kernel(chunk_rows, sizes, starts, *refs):
    n = len(sizes)
    q_refs, kv_refs, out, q_all, kv_all, keys_t, scores = (
        refs[:n],
        refs[n : 2 * n],
        *refs[2 * n :],
    )
    count, columns = out.shape
    heads = columns // HD
    tile = scores.shape[0] // heads
    i = 0
    for q_ref, kv_ref, size in zip(q_refs, kv_refs, sizes):
        first = 0
        while first < size:
            rows = chunk_rows[i]
            where = pl.ds(pl.multiple_of(starts[i], rows), rows)
            q_all[where, :] = q_ref[first : first + rows, :]
            kv_all[where, :] = kv_ref[first : first + rows, :]
            first += rows
            i += 1
    keys_t[...] = kv_all[:, :HD].astype(jnp.float32).T.astype(jnp.bfloat16)
    scale = HD ** (-0.5) * LOG2E
    row = lax.broadcasted_iota(jnp.int32, (tile, tile), 0)
    col = lax.broadcasted_iota(jnp.int32, (tile, tile), 1)
    triangle = row >= col
    for low in range(0, count, tile):
        top = low + tile
        query = jnp.concatenate(
            [q_all[low:top, h * HD : (h + 1) * HD] for h in range(heads)], axis=0
        )
        scores[:, :top] = jnp.dot(query, keys_t[:, :top], preferred_element_type=jnp.float32)
        for h in range(heads):
            mine = slice(h * tile, (h + 1) * tile)
            edge = jnp.where(triangle, scores[mine, low:top], MASKED)
            highest = jnp.max(edge, axis=1, keepdims=True)
            if low:
                body = scores[mine, :low]
                highest = jnp.maximum(highest, jnp.max(body, axis=1, keepdims=True))
                body = jnp.exp2((body - highest) * scale)
            edge = jnp.exp2((edge - highest) * scale)
            total = jnp.sum(edge, axis=1, keepdims=True)
            if low:
                total = total + jnp.sum(body, axis=1, keepdims=True)
            share = 1.0 / total
            mixed = jnp.dot(
                (edge * share).astype(jnp.bfloat16),
                kv_all[low:top, HD:],
                preferred_element_type=jnp.float32,
            )
            if low:
                mixed = mixed + jnp.dot(
                    (body * share).astype(jnp.bfloat16),
                    kv_all[:low, HD:],
                    preferred_element_type=jnp.float32,
                )
            out[low:top, h * HD : (h + 1) * HD] = mixed.astype(jnp.bfloat16)


def attend(queries, kvs, chunk_rows, starts):
    count = sum(chunk_rows)
    q_width = queries[0].shape[1]
    tile = min(256, count)
    vmem = pl.BlockSpec(memory_space=pltpu.VMEM)
    return pl.pallas_call(
        functools.partial(attend_kernel, tuple(chunk_rows), tuple(q.shape[0] for q in queries)),
        out_shape=jax.ShapeDtypeStruct((count, q_width), jnp.bfloat16),
        in_specs=[pl.BlockSpec(memory_space=pltpu.SMEM)] + [vmem] * (2 * len(queries)),
        out_specs=vmem,
        scratch_shapes=[
            pltpu.VMEM((count, q_width), jnp.bfloat16),
            pltpu.VMEM((count, 2 * HD), jnp.bfloat16),
            pltpu.VMEM((HD, count), jnp.bfloat16),
            pltpu.VMEM((tile * (q_width // HD), count), jnp.float32),
        ],
        compiler_params=pltpu.CompilerParams(vmem_limit_bytes=VMEM_LIMIT),
        cost_estimate=pl.CostEstimate(
            flops=2 * count * count * q_width,
            bytes_accessed=4 * count * (q_width + 2 * HD),
            transcendentals=count * count * q_width // HD // 2,
        ),
        name="attend",
    )(jnp.stack(starts).astype(jnp.int32), *queries, *kvs)


def decode_old_kernel(tables, q_ref, own_ref, live_ref, pool, acc_ref, state_ref, cache, sems):
    rows, pages = tables.shape
    span = (pages + 1) * PAGE
    scale = HD ** (-0.5) * LOG2E
    for r in range(rows):

        @pl.loop(0, pages)
        def _(p, r=r):
            pltpu.make_async_copy(pool.at[tables[r, p]], cache.at[r, p], sems.at[r]).start()

    columns = q_ref.shape[1]
    first_row = lax.broadcasted_iota(jnp.int32, (PAGE, cache.shape[3]), 0) == 0
    lane_row = lax.broadcasted_iota(jnp.int32, (1, columns), 1) // GROUP % rows
    for r in range(rows):
        own = own_ref[r : r + 1, :].astype(jnp.float32)
        cache[r, pages] = jnp.where(first_row, own, 0.0).astype(cache.dtype)
    scores = []
    for r in range(rows):
        pltpu.make_async_copy(
            pool.at[pl.ds(0, pages)], cache.at[r, pl.ds(0, pages)], sems.at[r]
        ).wait()
        kv = cache[r].reshape(span, cache.shape[3])
        score = jnp.dot(kv, q_ref[...], preferred_element_type=jnp.float32)
        seen = (live_ref[:, r : r + 1] > 0.0) & (lane_row == r)
        scores.append(jnp.where(seen, score, MASKED))
    highest = functools.reduce(
        jnp.maximum, [jnp.max(score, axis=0, keepdims=True) for score in scores]
    )
    total = jnp.zeros_like(highest)
    mixed = [jnp.zeros((rows * GROUP, HD), jnp.float32) for _ in range(KVH)]
    for r in range(rows):
        weight = jnp.exp2((scores[r] - highest) * scale)
        total = total + jnp.sum(weight, axis=0, keepdims=True)
        weight = weight.T.astype(jnp.bfloat16)
        for h in range(KVH):
            value = cache[r, :, :, (2 * h + 1) * HD : (2 * h + 2) * HD].reshape(span, HD)
            mixed[h] = mixed[h] + jnp.dot(
                weight[h * rows * GROUP : (h + 1) * rows * GROUP],
                value,
                preferred_element_type=jnp.float32,
            )
    for h in range(KVH):
        acc_ref[h] = mixed[h]
    state_ref[0:1, :] = highest
    state_ref[1:2, :] = total


def decode_old(pool, tables, live, queries, new_kv):
    rows, pages = tables.shape
    vmem = pl.BlockSpec(memory_space=pltpu.VMEM)
    return pl.pallas_call(
        decode_old_kernel,
        out_shape=[
            jax.ShapeDtypeStruct((KVH, rows * GROUP, HD), jnp.float32),
            jax.ShapeDtypeStruct((2, KVH * rows * GROUP), jnp.float32),
        ],
        in_specs=[
            pl.BlockSpec(memory_space=pltpu.SMEM),
            vmem,
            vmem,
            vmem,
            pl.BlockSpec(memory_space=pl.ANY),
        ],
        out_specs=[vmem] * 2,
        scratch_shapes=[
            pltpu.VMEM((rows, pages + 1) + pool.shape[1:], pool.dtype),
            pltpu.SemaphoreType.DMA((rows,)),
        ],
        compiler_params=pltpu.CompilerParams(vmem_limit_bytes=VMEM_LIMIT),
        cost_estimate=pl.CostEstimate(
            flops=4 * rows * pages * PAGE * KVH * GROUP * HD,
            bytes_accessed=2 * rows * pages * PAGE * pool.shape[2],
            transcendentals=rows * pages * PAGE * KVH * GROUP,
        ),
        name="decode_old",
    )(tables, queries, new_kv, live, pool)


def decode_new_kernel(heads, q_ref, allowed_ref, acc_ref, state_ref, *refs):
    pieces, out, weights, keeps = refs[:-3], *refs[-3:]
    scale = HD ** (-0.5) * LOG2E
    columns = q_ref.shape[1]
    per_head = columns // KVH
    score = jnp.zeros((pieces[0].shape[0], columns), jnp.float32)
    for k in range(KVH):
        where = pl.ds(pl.multiple_of(heads[k] * 2 * HD, 2 * HD), 2 * HD)
        score = score + jnp.dot(pieces[k][...], q_ref[where, :], preferred_element_type=jnp.float32)
    score = jnp.where(allowed_ref[...] > 0.0, score, MASKED)
    before = state_ref[0:1, :]
    highest = jnp.maximum(before, jnp.max(score, axis=0, keepdims=True))
    keep = jnp.exp2((before - highest) * scale)
    weight = jnp.exp2((score - highest) * scale)
    share = 1.0 / (state_ref[1:2, :] * keep + jnp.sum(weight, axis=0, keepdims=True))
    weights[...] = (weight * share).T
    keeps[...] = jnp.broadcast_to(keep * share, (8, columns)).T
    for k in range(KVH):
        h = heads[k]
        mine = pl.ds(pl.multiple_of(h * per_head, per_head), per_head)
        mixed = acc_ref[h] * keeps[mine, 0:1] + jnp.dot(
            weights[mine, :].astype(jnp.bfloat16),
            pieces[k][:, HD:],
            preferred_element_type=jnp.float32,
        )
        out[h] = mixed.astype(jnp.bfloat16)


def decode_new(pieces, heads, allowed, queries, acc, state):
    vmem = pl.BlockSpec(memory_space=pltpu.VMEM)
    columns = queries.shape[1]
    return pl.pallas_call(
        decode_new_kernel,
        out_shape=jax.ShapeDtypeStruct(acc.shape, jnp.bfloat16),
        in_specs=[pl.BlockSpec(memory_space=pltpu.SMEM)] + [vmem] * (4 + len(pieces)),
        out_specs=vmem,
        scratch_shapes=[
            pltpu.VMEM((columns, pieces[0].shape[0]), jnp.float32),
            pltpu.VMEM((columns, 8), jnp.float32),
        ],
        compiler_params=pltpu.CompilerParams(vmem_limit_bytes=VMEM_LIMIT),
        name="decode_new",
    )(heads, queries, allowed, acc, state, *pieces)


def exchange_plan(members, subs):
    def pairs(links):
        return [
            (source * subs + sub, target * subs + sub)
            for source, target in links
            for sub in range(subs)
        ]

    side = [(m, m ^ 1) for m in range(members)]
    outer = [(m, m ^ 2) for m in range(members)]
    outward = [(m, m ^ 2) for m in range(members) if m // 2 in (1, 2)]
    inner = [(m, m ^ 6) for m in range(members) if m // 2 in (1, 2)]
    return pairs(side), pairs(outer), pairs(outward), pairs(inner)


def local(
    stretch_tokens,
    norm_gain,
    q_weight,
    kv_weight,
    dec_query,
    dec_new_kv,
    kv_pool,
    page_table,
    cache_lengths,
    handoff_slot,
):
    devices_tp = lax.axis_size("tp")
    members = min(16, devices_tp)
    subs = devices_tp // members
    sub_bits = subs.bit_length() - 1
    member_bits = members.bit_length() - 1
    headmates = members // KVH
    position = lax.axis_index("tp")
    member = position // subs
    tokens = stretch_tokens[0]
    block_rows, width = tokens.shape
    count = members * block_rows
    gain = norm_gain.reshape(1, width)

    rows, pages = page_table.shape
    slots = handoff_slot[0]
    listed = page_table[:, :, None] == slots[None, None, :]
    handed = jnp.repeat(jnp.any(listed, axis=2), PAGE, axis=1)
    live = (jnp.arange(pages * PAGE)[None, :] < cache_lengths[:, None]) & ~handed
    own_page = jnp.broadcast_to(jnp.arange(PAGE)[:, None] == 0, (PAGE, rows))
    live = jnp.concatenate((live.T, own_page), axis=0).astype(jnp.float32)
    allowed = jnp.repeat(jnp.any(listed, axis=1).T, PAGE, axis=0)
    allowed = jnp.tile(jnp.repeat(allowed, GROUP, axis=1), (1, KVH)).astype(jnp.float32)
    by_head = dec_query.reshape(rows, KVH, GROUP, HD).transpose(1, 3, 0, 2)
    by_head = by_head.reshape(KVH, 1, HD, 1, rows * GROUP)
    same_head = jnp.eye(KVH, dtype=bool).reshape(KVH, 1, 1, KVH, 1)
    key_half = jnp.arange(2).reshape(1, 2, 1, 1, 1) == 0
    dec_heads = jnp.where(same_head & key_half, by_head, jnp.zeros((), by_head.dtype))
    dec_heads = dec_heads.reshape(KVH * 2 * HD, KVH * rows * GROUP)

    q_block = q_weight
    kv_block = kv_weight
    for bit in range(sub_bits):
        other_q = swapped(q_block, "tp", bit)
        other_kv = swapped(kv_block, "tp", bit)
        upper = position // 2**bit % 2
        q_block = ordered_pair(q_block, other_q, upper, 1)
        kv_block = ordered_pair(kv_block, other_kv, upper, 1)
    q_cos, q_sin = rotation_tables(count, HD, 0, False)
    kv_width = kv_block.shape[1]
    kv_cos, kv_sin = rotation_tables(count, kv_width, member * kv_width, True)
    q_job = (q_block, q_cos, q_sin)
    kv_job = (kv_block, kv_cos, kv_sin)
    bar = lax.optimization_barrier

    def old_state():
        return decode_old(kv_pool, page_table, live, dec_heads, dec_new_kv)

    if members == 8 and headmates == 1 and block_rows % 32 == 0:
        half = block_rows // 2
        side, outer, outward, inner = exchange_plan(members, subs)
        move = lambda value, pairs: lax.ppermute(value, "tp", pairs)
        row = member // 2
        at_end = (row == 0) | (row == 3)

        def start_of(offset, c):
            return jnp.bitwise_xor(member, offset) * block_rows + c * half

        def hand(kv, offset):
            pairs = [
                (r * devices_tp + m * subs + s, (1 - r) * devices_tp + (m ^ offset) * subs + s)
                for r in range(2)
                for m in range(members)
                for s in range(subs)
            ]
            return lax.ppermute(kv, ("role", "tp"), pairs)

        own = [tokens[:half], tokens[half:]]
        y, e1, e2 = {}, {}, {}
        for c in range(2):
            y[c], e1[c], e2[c] = move(own[c], side), move(own[c], outer), move(own[c], inner)
        state = old_state()
        q0, kv0 = project([tokens], [member * block_rows], gain, [q_job, kv_job])
        piece = {0: hand(kv0, 0)}
        near = {}
        for c in range(2):
            e1[c], e2[c], y[c] = bar((e1[c], e2[c], y[c]))
            e1[2 + c] = move(e2[c], outward)
            e2[2 + c] = move(e1[c], inner)
            y[2 + c] = move(e1[c], side)
        qa, kva = project(
            [e1[0], e1[1], y[0], y[1]],
            [start_of(o, c) for o in (2, 1) for c in range(2)],
            gain,
            [q_job, kv_job],
        )
        piece[2] = hand(kva[:block_rows], 2)
        piece[1] = hand(kva[block_rows:], 1)
        two, three = {}, {}
        for c in range(2):
            e1[2 + c], e2[2 + c], y[2 + c] = bar((e1[2 + c], e2[2 + c], y[2 + c]))
            two[c] = jnp.where(at_end, e1[2 + c], e2[2 + c])
            e1[4 + c] = move(e2[2 + c], outward)
            y[4 + c] = move(two[c], side)
        qb, kvb = project(
            [two[0], two[1], y[2], y[3]],
            [start_of(o, c) for o in (4, 3) for c in range(2)],
            gain,
            [q_job, kv_job],
        )
        piece[4] = hand(kvb[:block_rows], 4)
        piece[3] = hand(kvb[block_rows:], 3)
        for c in range(2):
            e1[4 + c], y[4 + c] = bar((e1[4 + c], y[4 + c]))
            three[c] = jnp.where(at_end, e1[4 + c], e2[c])
            if c == 0:
                e1[6] = move(y[4], outer)
            else:
                y[6] = move(three[1], side)
        qc, kvc = project(
            [three[0], three[1], y[4], y[5]],
            [start_of(o, c) for o in (6, 5) for c in range(2)],
            gain,
            [q_job, kv_job],
        )
        piece[6] = hand(kvc[:block_rows], 6)
        piece[5] = hand(kvc[block_rows:], 5)
        last = [e1[6], y[6]]
        last_starts = [start_of(7, c) for c in range(2)]
        (kvd,) = project(last, last_starts, gain, [kv_job])
        piece[7] = hand(kvd, 7)
        (qd,) = project(last, last_starts, gain, [q_job])
        starts = [start_of(o, c) for o in (0, 2, 1, 4, 3, 6, 5, 7) for c in range(2)]
        context = attend(
            [q0, qa, qb, qc, qd], [kv0, kva, kvb, kvc, kvd], [half] * (2 * members), starts
        )
        pieces = [piece[k] for k in range(members)]
        piece_heads = jnp.bitwise_xor(member, jnp.arange(members)).astype(jnp.int32)
    else:
        state = old_state()
        moving = tokens
        queries, local_kvs, order = [], [], []
        group, group_ids = [tokens], [member]
        for step in range(members):
            if step:
                moving = from_behind(moving, "tp", subs)
                group.append(moving)
                group_ids.append((member - step) % members)
            if len(group) == min(4, members) or step == members - 1:
                q_part, kv_part = project(
                    group, [i * block_rows for i in group_ids], gain, [q_job, kv_job]
                )
                queries.append(q_part)
                local_kvs.append(kv_part)
                order += group_ids
                group, group_ids = [], []
        arrived_kv = jnp.concatenate(local_kvs, axis=0).reshape(members, block_rows, kv_width)
        local_kv = arrived_kv[jnp.argsort(jnp.stack(order))].reshape(count, kv_width)
        head_kv = local_kv
        for step in range(headmates.bit_length() - 1):
            other = swapped(head_kv, "tp", sub_bits + step)
            head_kv = ordered_pair(head_kv, other, member // 2**step % 2, 1)
        arrived_q = jnp.concatenate(queries, axis=0).reshape(members, block_rows, -1)
        all_q = arrived_q[jnp.argsort(jnp.stack(order))].reshape(count, -1)
        context = attend([all_q], [head_kv], [count], [jnp.int32(0)])
        crossed = swapped(local_kv, "role", 0)
        received = spread_members(
            crossed.reshape(members, block_rows, kv_width),
            member,
            sub_bits,
            member_bits,
            lambda part, bit: swapped(part, "tp", bit),
        )
        arrived = jnp.transpose(received, (1, 0, 2)).reshape(block_rows, members * kv_width)
        pieces = [arrived[:, k * 2 * HD : (k + 1) * 2 * HD] for k in range(KVH)]
        piece_heads = jnp.arange(KVH).astype(jnp.int32)

    decoded = decode_new(pieces, piece_heads, allowed, dec_heads, *state)
    decoded = (
        decoded.reshape(KVH, rows, GROUP, HD).transpose(1, 0, 2, 3).reshape(rows, KVH * GROUP * HD)
    )
    return (context[None], decoded)


def solution(mesh):
    in_specs = (
        P("role", ("grp", "tp"), None),
        P(),
        P(None, "tp"),
        P(None, "tp"),
        P(("grp", "role", "tp"), None),
        P(("grp", "role", "tp"), None),
        P(("grp", "role", "tp"), None, None),
        P(("grp", "role", "tp"), None),
        P(("grp", "role", "tp")),
        P(("grp", "role", "tp"), None),
    )
    out_specs = (P("role", "grp", "tp"), P(("grp", "role", "tp"), None))
    return jax.shard_map(local, mesh=mesh, in_specs=in_specs, out_specs=out_specs, check_vma=False)
```

```python
import functools

import jax
import jax.numpy as jnp
from jax import lax
from jax.experimental import pallas as pl
from jax.experimental.pallas import tpu as pltpu
from jax.sharding import PartitionSpec as P

KVH = 8
HD = 128
PAGE = 16
GROUP = 8
MASKED = -1e30

norm_eps = 1e-05
rope_base = 500000.0


LOG2E = 1.4426950408889634
VMEM_LIMIT = 20 * 2**20


def swapped(value, axis, bit):
    mask = 2**bit
    pairs = [(source, source ^ mask) for source in range(lax.axis_size(axis))]
    return lax.ppermute(value, axis, pairs)


def from_behind(value, axis, steps):
    count = lax.axis_size(axis)
    pairs = [(source, (source + steps) % count) for source in range(count)]
    return lax.ppermute(value, axis, pairs)


def ordered_pair(mine, other, upper, axis):
    first = jnp.where(upper == 1, other, mine)
    second = jnp.where(upper == 1, mine, other)
    return jnp.concatenate((first, second), axis=axis)


def spread_members(blocks, member, low_bit, member_bits, mover):
    members = blocks.shape[0]
    order = jnp.bitwise_xor(member, jnp.arange(members))
    buffer = blocks[order]
    for step in range(member_bits):
        width = 2**step
        view = buffer.reshape(members // (2 * width), 2, width, blocks.shape[1], blocks.shape[2])
        arrived = mover(view[:, 1], low_bit + step)
        buffer = jnp.stack((view[:, 0], arrived), axis=1).reshape(blocks.shape)
    return buffer[order]


def rotation_tables(count, width, first_col, only_keys):
    columns = first_col + jnp.arange(width)
    pair_index = columns % HD // 2
    inverse = jnp.exp(
        -(2.0 * pair_index.astype(jnp.float32) / HD) * jnp.log(jnp.float32(rope_base))
    )
    angle = jnp.arange(count).astype(jnp.float32)[:, None] * inverse[None, :]
    cosine = jnp.cos(angle)
    sine = jnp.where(columns % 2 == 0, -1.0, 1.0)[None, :] * jnp.sin(angle)
    if only_keys:
        is_key = (columns % (2 * HD) < HD)[None, :]
        cosine = jnp.where(is_key, cosine, 1.0)
        sine = jnp.where(is_key, sine, 0.0)
    return cosine, sine


def turned(tile, cosine, sine):
    lane = lax.broadcasted_iota(jnp.int32, tile.shape, 1)
    after = pltpu.roll(tile, HD - 1, 1)
    before = pltpu.roll(tile, 1, 1)
    return tile * cosine + jnp.where(lane % 2 == 0, after, before) * sine


def normalize(x_refs, chunk_rows, gain, normed):
    width = normed.shape[1]
    part = 512
    first = 0
    for x_ref, rows in zip(x_refs, chunk_rows):

        def add(i, total, x_ref=x_ref):
            tile = x_ref[:, pl.ds(pl.multiple_of(i * part, part), part)].astype(jnp.float32)
            tile = tile * tile
            sums = [tile[:, col : col + 128] for col in range(0, part, 128)]
            return total + ((sums[0] + sums[1]) + (sums[2] + sums[3]))

        total = lax.fori_loop(
            0, width // part, add, jnp.zeros((rows, 128), jnp.float32), unroll=4
        )
        mean_sq = jnp.sum(total, axis=1, keepdims=True) / width
        scale = lax.rsqrt(mean_sq + norm_eps)

        def write(i, carry, x_ref=x_ref, rows=rows, first=first, scale=scale):
            here = pl.ds(pl.multiple_of(i * part, part), part)
            normed[first : first + rows, here] = (
                x_ref[:, here].astype(jnp.float32) * scale * gain[:, here].astype(jnp.float32)
            ).astype(jnp.bfloat16)
            return carry

        lax.fori_loop(0, width // part, write, 0, unroll=4)
        first += rows


def project_kernel(chunk_rows, rotated, place, ready, member, *refs):
    jobs = len(rotated)
    n = 1 if ready else len(chunk_rows)
    x_refs, gain = refs[:n], refs[n]
    job_refs = refs[n + 1 : n + 1 + 3 * jobs]
    outs = refs[n + 1 + 3 * jobs : n + 1 + 4 * jobs]
    starts = place(member[0])
    if ready:
        normed = x_refs[0]
    else:
        normed = refs[-1]
        normalize(x_refs, chunk_rows, gain, normed)
    for j in range(jobs):
        weight, cos_ref, sin_ref = job_refs[3 * j : 3 * j + 3]
        table = cos_ref.shape[1]
        columns = weight.shape[1]
        tile = min(256, columns)
        for low in range(0, columns, tile):
            product = jnp.dot(
                normed[...], weight[:, low : low + tile], preferred_element_type=jnp.float32
            )
            first = 0
            for i, rows in enumerate(chunk_rows):
                where = pl.ds(pl.multiple_of(starts[i], rows), rows)
                for col in range(low, low + tile, HD):
                    here = product[first : first + rows, col - low : col - low + HD]
                    if rotated[j][col // HD]:
                        at = col % table
                        here = turned(
                            here, cos_ref[where, at : at + HD], sin_ref[where, at : at + HD]
                        )
                    outs[j][first : first + rows, col : col + HD] = here.astype(jnp.bfloat16)
                first += rows


def project(chunks, place, member, gain, jobs, ready=None, keep=False):
    chunk_rows = tuple(chunk.shape[0] for chunk in chunks)
    rows = sum(chunk_rows)
    width = chunks[0].shape[1]
    columns = [job[0].shape[1] for job in jobs]
    rows_in = [ready] if ready is not None else list(chunks)
    operands = [*rows_in, gain, *(part for job in jobs for part in job[:3])]
    vmem = pl.BlockSpec(memory_space=pltpu.VMEM)
    outs = [jax.ShapeDtypeStruct((rows, c), jnp.bfloat16) for c in columns]
    normed = (rows, width)
    scratch = []
    if keep:
        outs.append(jax.ShapeDtypeStruct(normed, jnp.bfloat16))
    elif ready is None:
        scratch.append(pltpu.VMEM(normed, jnp.bfloat16))
    return pl.pallas_call(
        functools.partial(
            project_kernel, chunk_rows, [job[3] for job in jobs], place, ready is not None
        ),
        out_shape=outs,
        in_specs=[pl.BlockSpec(memory_space=pltpu.SMEM)] + [vmem] * len(operands),
        out_specs=[vmem] * len(outs),
        scratch_shapes=scratch,
        compiler_params=pltpu.CompilerParams(vmem_limit_bytes=VMEM_LIMIT),
        cost_estimate=pl.CostEstimate(
            flops=2 * rows * width * sum(columns),
            bytes_accessed=2 * width * (rows + sum(columns)),
            transcendentals=0,
        ),
        name="project",
    )(member, *operands)


def attend_kernel(chunk_rows, sizes, place, member, *refs):
    n = len(sizes)
    starts = place(member[0])
    q_refs, kv_refs, out, q_all, kv_all, keys_t, scores = (
        refs[:n],
        refs[n : 2 * n],
        *refs[2 * n :],
    )
    count, columns = out.shape
    heads = columns // HD
    tile = scores.shape[0] // heads
    i = 0
    for q_ref, kv_ref, size in zip(q_refs, kv_refs, sizes):
        first = 0
        while first < size:
            rows = chunk_rows[i]
            where = pl.ds(pl.multiple_of(starts[i], rows), rows)
            q_all[where, :] = q_ref[first : first + rows, :]
            kv_all[where, :] = kv_ref[first : first + rows, :]
            first += rows
            i += 1
    keys_t[...] = kv_all[:, :HD].astype(jnp.float32).T.astype(jnp.bfloat16)
    scale = HD ** (-0.5) * LOG2E
    row = lax.broadcasted_iota(jnp.int32, (tile, tile), 0)
    col = lax.broadcasted_iota(jnp.int32, (tile, tile), 1)
    triangle = row >= col
    for low in range(0, count, tile):
        top = low + tile
        query = jnp.concatenate(
            [q_all[low:top, h * HD : (h + 1) * HD] for h in range(heads)], axis=0
        )
        scores[:, :top] = jnp.dot(query, keys_t[:, :top], preferred_element_type=jnp.float32)
        for h in range(heads):
            mine = slice(h * tile, (h + 1) * tile)
            edge = jnp.where(triangle, scores[mine, low:top], MASKED)
            highest = jnp.max(edge, axis=1, keepdims=True)
            if low:
                body = scores[mine, :low]
                highest = jnp.maximum(highest, jnp.max(body, axis=1, keepdims=True))
                body = jnp.exp2((body - highest) * scale)
            edge = jnp.exp2((edge - highest) * scale)
            total = jnp.sum(edge, axis=1, keepdims=True)
            if low:
                total = total + jnp.sum(body, axis=1, keepdims=True)
            share = 1.0 / total
            mixed = jnp.dot(
                (edge * share).astype(jnp.bfloat16),
                kv_all[low:top, HD:],
                preferred_element_type=jnp.float32,
            )
            if low:
                mixed = mixed + jnp.dot(
                    (body * share).astype(jnp.bfloat16),
                    kv_all[:low, HD:],
                    preferred_element_type=jnp.float32,
                )
            out[low:top, h * HD : (h + 1) * HD] = mixed.astype(jnp.bfloat16)


def attend(queries, kvs, chunk_rows, place, member):
    count = sum(chunk_rows)
    q_width = queries[0].shape[1]
    tile = min(256, count)
    vmem = pl.BlockSpec(memory_space=pltpu.VMEM)
    return pl.pallas_call(
        functools.partial(
            attend_kernel, tuple(chunk_rows), tuple(q.shape[0] for q in queries), place
        ),
        out_shape=jax.ShapeDtypeStruct((count, q_width), jnp.bfloat16),
        in_specs=[pl.BlockSpec(memory_space=pltpu.SMEM)] + [vmem] * (2 * len(queries)),
        out_specs=vmem,
        scratch_shapes=[
            pltpu.VMEM((count, q_width), jnp.bfloat16),
            pltpu.VMEM((count, 2 * HD), jnp.bfloat16),
            pltpu.VMEM((HD, count), jnp.bfloat16),
            pltpu.VMEM((tile * (q_width // HD), count), jnp.float32),
        ],
        compiler_params=pltpu.CompilerParams(vmem_limit_bytes=VMEM_LIMIT),
        cost_estimate=pl.CostEstimate(
            flops=2 * count * count * q_width,
            bytes_accessed=4 * count * (q_width + 2 * HD),
            transcendentals=count * count * q_width // HD // 2,
        ),
        name="attend",
    )(member, *queries, *kvs)


def decode_old_kernel(
    tables,
    lengths,
    slots,
    query_ref,
    own_ref,
    pool,
    acc_ref,
    state_ref,
    queries,
    allowed,
    limits,
    scores,
    own,
):
    rows, pages = tables.shape
    handed = slots.shape[1]
    total_pages, page, width = pool.shape
    columns = queries.shape[1]
    per_head = columns // KVH
    scale = HD ** (-0.5) * LOG2E
    lane = lax.broadcasted_iota(jnp.int32, (1, columns), 1)
    lane_row = lane % rows

    limits[...] = jnp.zeros_like(limits)

    def one_entry(e, owners):
        for r in range(rows):
            at = tables[r, e]
            count = jnp.clip(lengths[r] - e * page, 0, page)
            for j in range(handed):
                taken = slots[0, j] == at
                count = jnp.where(taken, 0, count)
                owners = owners[:j] + (jnp.where(taken, r, owners[j]),) + owners[j + 1 :]
            limits[pl.ds(at, 1), :] = jnp.where(lane_row == r, count, 0)
        return owners

    owners = lax.fori_loop(0, pages, one_entry, (jnp.int32(-1),) * handed)
    for j in range(handed):
        allowed[j * page : (j + 1) * page, :] = jnp.broadcast_to(
            jnp.where(lane_row == owners[j], 1.0, 0.0), (page, columns)
        )

    stacked = jnp.concatenate(
        [query_ref[:, i * HD : (i + 1) * HD].astype(jnp.float32) for i in range(KVH * GROUP)],
        axis=0,
    )
    turned_q = stacked.T.astype(jnp.bfloat16)
    for h in range(KVH):
        queries[2 * h * HD : (2 * h + 1) * HD, :] = jnp.where(
            lane // per_head == h, turned_q, jnp.zeros_like(turned_q)
        )
        queries[(2 * h + 1) * HD : (2 * h + 2) * HD, :] = jnp.zeros((HD, columns), jnp.bfloat16)

    own[...] = jnp.zeros_like(own)
    own[0:rows, :] = own_ref[...]
    own_score = jnp.dot(own[...], queries[...], preferred_element_type=jnp.float32)
    own_line = lax.broadcasted_iota(jnp.int32, own_score.shape, 0)
    own_score = jnp.where(own_line == lane_row, own_score, MASKED)
    highest = jnp.max(own_score, axis=0, keepdims=True)
    step = total_pages // 4
    line = lax.broadcasted_iota(jnp.int32, (step, page, columns), 1)
    for first in range(0, total_pages, step):
        score = jnp.dot(
            pool[first : first + step].reshape(step * page, width),
            queries[...],
            preferred_element_type=jnp.float32,
        ).reshape(step, page, columns)
        limit = limits[first : first + step, :].reshape(step, 1, columns)
        score = jnp.where(line < limit, score, MASKED)
        score = score.reshape(step * page, columns)
        scores[first * page : (first + step) * page, :] = score
        highest = jnp.maximum(highest, jnp.max(score, axis=0, keepdims=True))

    weight = jnp.exp2((own_score - highest) * scale)
    total = jnp.sum(weight, axis=0, keepdims=True)
    weight = weight.T.astype(jnp.bfloat16)
    mixed = [
        jnp.dot(
            weight[h * per_head : (h + 1) * per_head],
            own[:, (2 * h + 1) * HD : (2 * h + 2) * HD],
            preferred_element_type=jnp.float32,
        )
        for h in range(KVH)
    ]
    for first in range(0, total_pages, step):
        weight = jnp.exp2((scores[first * page : (first + step) * page, :] - highest) * scale)
        total = total + jnp.sum(weight, axis=0, keepdims=True)
        weight = weight.T.astype(jnp.bfloat16)
        for h in range(KVH):
            value = pool[first : first + step, :, (2 * h + 1) * HD : (2 * h + 2) * HD]
            mixed[h] = mixed[h] + jnp.dot(
                weight[h * per_head : (h + 1) * per_head],
                value.reshape(step * page, HD),
                preferred_element_type=jnp.float32,
            )
    for h in range(KVH):
        acc_ref[h] = mixed[h]
    state_ref[0:1, :] = highest
    state_ref[1:2, :] = total


def decode_old(pool, tables, lengths, slots, queries, new_kv):
    rows = tables.shape[0]
    columns = KVH * GROUP * rows
    total_pages, page, width = pool.shape
    vmem = pl.BlockSpec(memory_space=pltpu.VMEM)
    smem = pl.BlockSpec(memory_space=pltpu.SMEM)
    return pl.pallas_call(
        decode_old_kernel,
        out_shape=[
            jax.ShapeDtypeStruct((KVH, GROUP * rows, HD), jnp.float32),
            jax.ShapeDtypeStruct((2, columns), jnp.float32),
            jax.ShapeDtypeStruct((width, columns), jnp.bfloat16),
            jax.ShapeDtypeStruct((slots.shape[1] * page, columns), jnp.float32),
        ],
        in_specs=[smem, smem, smem, vmem, vmem, vmem],
        out_specs=[vmem] * 4,
        scratch_shapes=[
            pltpu.VMEM((total_pages, columns), jnp.int32),
            pltpu.VMEM((total_pages * page, columns), jnp.float32),
            pltpu.VMEM((page, width), jnp.bfloat16),
        ],
        compiler_params=pltpu.CompilerParams(vmem_limit_bytes=VMEM_LIMIT),
        cost_estimate=pl.CostEstimate(
            flops=4 * total_pages * page * width * columns,
            bytes_accessed=2 * total_pages * page * width,
            transcendentals=total_pages * page * columns,
        ),
        name="decode_old",
    )(tables, lengths, slots, queries, new_kv, pool)


def decode_new_kernel(heads_of, member, q_ref, allowed_ref, acc_ref, state_ref, *refs):
    pieces, out, weights, keeps = refs[:-3], *refs[-3:]
    scale = HD ** (-0.5) * LOG2E
    columns = q_ref.shape[1]
    per_head = columns // KVH
    rows = out.shape[0]
    heads = heads_of(member[0])
    score = jnp.zeros((pieces[0].shape[0], columns), jnp.float32)
    for k in range(KVH):
        where = pl.ds(pl.multiple_of(heads[k] * 2 * HD, 2 * HD), 2 * HD)
        score = score + jnp.dot(pieces[k][...], q_ref[where, :], preferred_element_type=jnp.float32)
    score = jnp.where(allowed_ref[...] > 0.0, score, MASKED)
    before = state_ref[0:1, :]
    highest = jnp.maximum(before, jnp.max(score, axis=0, keepdims=True))
    keep = jnp.exp2((before - highest) * scale)
    weight = jnp.exp2((score - highest) * scale)
    share = 1.0 / (state_ref[1:2, :] * keep + jnp.sum(weight, axis=0, keepdims=True))
    weights[...] = (weight * share).T
    keeps[...] = jnp.broadcast_to(keep * share, (8, columns)).T
    for k in range(KVH):
        h = heads[k]
        mine = pl.ds(pl.multiple_of(h * per_head, per_head), per_head)
        mixed = acc_ref[h] * keeps[mine, 0:1] + jnp.dot(
            weights[mine, :].astype(jnp.bfloat16),
            pieces[k][:, HD:],
            preferred_element_type=jnp.float32,
        )
        for j in range(GROUP):
            lanes = pl.ds(pl.multiple_of((h * GROUP + j) * HD, HD), HD)
            out[:, lanes] = mixed[j * rows : (j + 1) * rows, :].astype(jnp.bfloat16)


def decode_new(pieces, heads_of, member, rows, acc, state, queries, allowed):
    vmem = pl.BlockSpec(memory_space=pltpu.VMEM)
    columns = queries.shape[1]
    return pl.pallas_call(
        functools.partial(decode_new_kernel, heads_of),
        out_shape=jax.ShapeDtypeStruct((rows, KVH * GROUP * HD), jnp.bfloat16),
        in_specs=[pl.BlockSpec(memory_space=pltpu.SMEM)] + [vmem] * (4 + len(pieces)),
        out_specs=vmem,
        scratch_shapes=[
            pltpu.VMEM((columns, pieces[0].shape[0]), jnp.float32),
            pltpu.VMEM((columns, 8), jnp.float32),
        ],
        compiler_params=pltpu.CompilerParams(vmem_limit_bytes=VMEM_LIMIT),
        name="decode_new",
    )(member, queries, allowed, acc, state, *pieces)


def exchange_plan(members, subs):
    def pairs(links):
        return [
            (source * subs + sub, target * subs + sub)
            for source, target in links
            for sub in range(subs)
        ]

    side = [(m, m ^ 1) for m in range(members)]
    outer = [(m, m ^ 2) for m in range(members)]
    outward = [(m, m ^ 2) for m in range(members) if m // 2 in (1, 2)]
    inner = [(m, m ^ 6) for m in range(members) if m // 2 in (1, 2)]
    return pairs(side), pairs(outer), pairs(outward), pairs(inner)


def local(
    stretch_tokens,
    norm_gain,
    q_weight,
    kv_weight,
    dec_query,
    dec_new_kv,
    kv_pool,
    page_table,
    cache_lengths,
    handoff_slot,
):
    devices_tp = lax.axis_size("tp")
    members = min(16, devices_tp)
    subs = devices_tp // members
    sub_bits = subs.bit_length() - 1
    member_bits = members.bit_length() - 1
    headmates = members // KVH
    position = lax.axis_index("tp")
    member = position // subs
    tokens = stretch_tokens[0]
    block_rows, width = tokens.shape
    count = members * block_rows
    gain = norm_gain.reshape(1, width)

    member_ref = member.reshape(1).astype(jnp.int32)
    rows = page_table.shape[0]

    q_block = q_weight
    kv_block = kv_weight
    for bit in range(sub_bits):
        other_q = swapped(q_block, "tp", bit)
        other_kv = swapped(kv_block, "tp", bit)
        upper = position // 2**bit % 2
        q_block = ordered_pair(q_block, other_q, upper, 1)
        kv_block = ordered_pair(kv_block, other_kv, upper, 1)
    q_cos, q_sin = rotation_tables(count, HD, 0, False)
    kv_width = kv_block.shape[1]
    if kv_width % (2 * HD) == 0:
        kv_job = (kv_block, q_cos, q_sin, (True, False) * (kv_width // (2 * HD)))
    else:
        kv_cos, kv_sin = rotation_tables(count, kv_width, member * kv_width, True)
        kv_job = (kv_block, kv_cos, kv_sin, (True,) * max(1, kv_width // HD))
    q_job = (q_block, q_cos, q_sin, (True,) * (q_block.shape[1] // HD))
    bar = lax.optimization_barrier

    def old_state():
        return decode_old(
            kv_pool, page_table, cache_lengths, handoff_slot, dec_query, dec_new_kv
        )

    if members == 8 and headmates == 1 and block_rows % 32 == 0:
        half = block_rows // 2
        side, outer, outward, inner = exchange_plan(members, subs)
        move = lambda value, pairs: lax.ppermute(value, "tp", pairs)
        row = member // 2
        at_end = (row == 0) | (row == 3)

        def place(offsets):
            return lambda m: [
                jnp.bitwise_xor(m, offset) * block_rows + c * half
                for offset in offsets
                for c in range(2)
            ]

        def hand(kv, offset):
            pairs = [
                (r * devices_tp + m * subs + s, (1 - r) * devices_tp + (m ^ offset) * subs + s)
                for r in range(2)
                for m in range(members)
                for s in range(subs)
            ]
            return lax.ppermute(kv, ("role", "tp"), pairs)

        own = [tokens[:half]]
        own.append(bar((tokens, own[0]))[0][half:])
        y, e1, e2 = {}, {}, {}
        for c in range(2):
            y[c], e1[c], e2[c] = move(own[c], side), move(own[c], outer), move(own[c], inner)
        state = old_state()
        q0, kv0 = project(
            [tokens], lambda m: [m * block_rows], member_ref, gain, [q_job, kv_job]
        )
        piece = {0: hand(kv0, 0)}
        near = {}
        for c in range(2):
            e1[c], e2[c], y[c] = bar((e1[c], e2[c], y[c]))
            e1[2 + c] = move(e2[c], outward)
            e2[2 + c] = move(e1[c], inner)
            y[2 + c] = move(e1[c], side)
        qa, kva = project(
            [e1[0], e1[1], y[0], y[1]],
            place((2, 1)),
            member_ref,
            gain,
            [q_job, kv_job],
        )
        piece[2] = hand(kva[:block_rows], 2)
        piece[1] = hand(kva[block_rows:], 1)
        two, three = {}, {}
        for c in range(2):
            e1[2 + c], e2[2 + c], y[2 + c] = bar((e1[2 + c], e2[2 + c], y[2 + c]))
            two[c] = jnp.where(at_end, e1[2 + c], e2[2 + c])
            e1[4 + c] = move(e2[2 + c], outward)
            y[4 + c] = move(two[c], side)
        qb, kvb = project(
            [two[0], two[1], y[2], y[3]],
            place((4, 3)),
            member_ref,
            gain,
            [q_job, kv_job],
        )
        piece[4] = hand(kvb[:block_rows], 4)
        piece[3] = hand(kvb[block_rows:], 3)
        for c in range(2):
            e1[4 + c], y[4 + c] = bar((e1[4 + c], y[4 + c]))
            three[c] = jnp.where(at_end, e1[4 + c], e2[c])
            if c == 0:
                e1[6] = move(y[4], outer)
            else:
                y[6] = move(three[1], side)
        qc, kvc = project(
            [three[0], three[1], y[4], y[5]],
            place((6, 5)),
            member_ref,
            gain,
            [q_job, kv_job],
        )
        piece[6] = hand(kvc[:block_rows], 6)
        piece[5] = hand(kvc[block_rows:], 5)
        last = [e1[6], y[6]]
        kvd, normed = project(last, place((7,)), member_ref, gain, [kv_job], keep=True)
        piece[7] = hand(kvd, 7)
        (qd,) = project(last, place((7,)), member_ref, gain, [q_job], ready=normed)
        context = attend(
            [q0, qa, qb, qc, qd],
            [kv0, kva, kvb, kvc, kvd],
            [half] * (2 * members),
            place((0, 2, 1, 4, 3, 6, 5, 7)),
            member_ref,
        )
        pieces = [piece[k] for k in range(members)]
        heads_of = lambda m: [jnp.bitwise_xor(m, k) for k in range(members)]
    else:
        state = old_state()
        moving = tokens
        queries, local_kvs, order = [], [], []
        group, group_steps = [tokens], [0]
        for step in range(members):
            if step:
                moving = from_behind(moving, "tp", subs)
                group.append(moving)
                group_steps.append(step)
            if len(group) == min(4, members) or step == members - 1:
                place = lambda m, steps=tuple(group_steps): [
                    jnp.bitwise_and(m - back, members - 1) * block_rows for back in steps
                ]
                q_part, kv_part = project(group, place, member_ref, gain, [q_job, kv_job])
                queries.append(q_part)
                local_kvs.append(kv_part)
                order += [(member - back) % members for back in group_steps]
                group, group_steps = [], []
        arrived_kv = jnp.concatenate(local_kvs, axis=0).reshape(members, block_rows, kv_width)
        local_kv = arrived_kv[jnp.argsort(jnp.stack(order))].reshape(count, kv_width)
        head_kv = local_kv
        for step in range(headmates.bit_length() - 1):
            other = swapped(head_kv, "tp", sub_bits + step)
            head_kv = ordered_pair(head_kv, other, member // 2**step % 2, 1)
        arrived_q = jnp.concatenate(queries, axis=0).reshape(members, block_rows, -1)
        all_q = arrived_q[jnp.argsort(jnp.stack(order))].reshape(count, -1)
        context = attend([all_q], [head_kv], [count], lambda m: [0], member_ref)
        crossed = swapped(local_kv, "role", 0)
        received = spread_members(
            crossed.reshape(members, block_rows, kv_width),
            member,
            sub_bits,
            member_bits,
            lambda part, bit: swapped(part, "tp", bit),
        )
        arrived = jnp.transpose(received, (1, 0, 2)).reshape(block_rows, members * kv_width)
        pieces = [arrived[:, k * 2 * HD : (k + 1) * 2 * HD] for k in range(KVH)]
        heads_of = lambda m: list(range(KVH))

    decoded = decode_new(pieces, heads_of, member_ref, rows, *state)
    return (context[None], decoded)


def solution(mesh):
    in_specs = (
        P("role", ("grp", "tp"), None),
        P(),
        P(None, "tp"),
        P(None, "tp"),
        P(("grp", "role", "tp"), None),
        P(("grp", "role", "tp"), None),
        P(("grp", "role", "tp"), None, None),
        P(("grp", "role", "tp"), None),
        P(("grp", "role", "tp")),
        P(("grp", "role", "tp"), None),
    )
    out_specs = (P("role", "grp", "tp"), P(("grp", "role", "tp"), None))
    return jax.shard_map(local, mesh=mesh, in_specs=in_specs, out_specs=out_specs, check_vma=False)
```

```python
import functools

import jax
import jax.numpy as jnp
from jax import lax
from jax.experimental import pallas as pl
from jax.experimental.pallas import tpu as pltpu
from jax.sharding import PartitionSpec as P

KVH = 8
HD = 128
GROUP = 8
MASKED = -1e30

norm_eps = 1e-05
rope_base = 500000.0


LOG2E = 1.4426950408889634
VMEM_LIMIT = 14 * 2**20


def swapped(value, axis, bit):
    mask = 2**bit
    pairs = [(source, source ^ mask) for source in range(lax.axis_size(axis))]
    return lax.ppermute(value, axis, pairs)


def from_behind(value, axis, steps):
    count = lax.axis_size(axis)
    pairs = [(source, (source + steps) % count) for source in range(count)]
    return lax.ppermute(value, axis, pairs)


def ordered_pair(mine, other, upper, axis):
    first = jnp.where(upper == 1, other, mine)
    second = jnp.where(upper == 1, mine, other)
    return jnp.concatenate((first, second), axis=axis)


def spread_members(blocks, member, low_bit, member_bits, mover):
    members = blocks.shape[0]
    order = jnp.bitwise_xor(member, jnp.arange(members))
    buffer = blocks[order]
    for step in range(member_bits):
        width = 2**step
        view = buffer.reshape(members // (2 * width), 2, width, blocks.shape[1], blocks.shape[2])
        arrived = mover(view[:, 1], low_bit + step)
        buffer = jnp.stack((view[:, 0], arrived), axis=1).reshape(blocks.shape)
    return buffer[order]


def rotation_tables(count, width, first_col, only_keys):
    columns = first_col + jnp.arange(width)
    pair_index = columns % HD // 2
    inverse = jnp.exp(
        -(2.0 * pair_index.astype(jnp.float32) / HD) * jnp.log(jnp.float32(rope_base))
    )
    angle = jnp.arange(count).astype(jnp.float32)[:, None] * inverse[None, :]
    cosine = jnp.cos(angle)
    sine = jnp.where(columns % 2 == 0, -1.0, 1.0)[None, :] * jnp.sin(angle)
    if only_keys:
        is_key = (columns % (2 * HD) < HD)[None, :]
        cosine = jnp.where(is_key, cosine, 1.0)
        sine = jnp.where(is_key, sine, 0.0)
    return cosine, sine


def turned(tile, cosine, sine):
    lane = lax.broadcasted_iota(jnp.int32, tile.shape, 1)
    after = pltpu.roll(tile, HD - 1, 1)
    before = pltpu.roll(tile, 1, 1)
    return tile * cosine + jnp.where(lane % 2 == 0, after, before) * sine


def normalize(x_refs, chunk_rows, gain, normed):
    width = normed.shape[1]
    part = 512
    first = 0
    for x_ref, rows in zip(x_refs, chunk_rows):

        def add(i, total, x_ref=x_ref):
            tile = x_ref[:, pl.ds(pl.multiple_of(i * part, part), part)].astype(jnp.float32)
            tile = tile * tile
            sums = [tile[:, col : col + 128] for col in range(0, part, 128)]
            return total + ((sums[0] + sums[1]) + (sums[2] + sums[3]))

        total = lax.fori_loop(
            0, width // part, add, jnp.zeros((rows, 128), jnp.float32), unroll=4
        )
        mean_sq = jnp.sum(total, axis=1, keepdims=True) / width
        scale = lax.rsqrt(mean_sq + norm_eps)

        def write(i, carry, x_ref=x_ref, rows=rows, first=first, scale=scale):
            here = pl.ds(pl.multiple_of(i * part, part), part)
            normed[first : first + rows, here] = (
                x_ref[:, here].astype(jnp.float32) * scale * gain[:, here].astype(jnp.float32)
            ).astype(jnp.bfloat16)
            return carry

        lax.fori_loop(0, width // part, write, 0, unroll=4)
        first += rows


def project_kernel(chunk_rows, rotated, blocks, place, ready, member, *refs):
    jobs = len(rotated)
    n = 1 if ready else len(chunk_rows)
    x_refs, gain = refs[:n], refs[n]
    job_refs = refs[n + 1 : n + 1 + 3 * jobs]
    outs = refs[n + 1 + 3 * jobs :]
    starts = place(member[0])
    if ready:
        normed = x_refs[0]
    else:
        normed = refs[-1]
        normalize(x_refs, chunk_rows, gain, normed)
    for j in range(jobs):
        weight, cos_ref, sin_ref = job_refs[3 * j : 3 * j + 3]
        table = cos_ref.shape[1]
        columns = weight.shape[1]
        tile = min(256, columns)
        own_outs, outs = outs[: blocks[j]], outs[blocks[j] :]
        per_out = sum(chunk_rows) // blocks[j]
        for low in range(0, columns, tile):
            product = jnp.dot(
                normed[...], weight[:, low : low + tile], preferred_element_type=jnp.float32
            )
            first = 0
            for i, rows in enumerate(chunk_rows):
                where = pl.ds(pl.multiple_of(starts[i], rows), rows)
                for col in range(low, low + tile, HD):
                    here = product[first : first + rows, col - low : col - low + HD]
                    if rotated[j][col // HD]:
                        at = col % table
                        here = turned(
                            here, cos_ref[where, at : at + HD], sin_ref[where, at : at + HD]
                        )
                    at = first % per_out
                    own_outs[first // per_out][at : at + rows, col : col + HD] = here.astype(
                        jnp.bfloat16
                    )
                first += rows


def project(chunks, place, member, gain, jobs, ready=None, keep=False):
    chunk_rows = tuple(chunk.shape[0] for chunk in chunks)
    rows = sum(chunk_rows)
    width = chunks[0].shape[1]
    columns = [job[0].shape[1] for job in jobs]
    rows_in = [ready] if ready is not None else list(chunks)
    operands = [*rows_in, gain, *(part for job in jobs for part in job[:3])]
    vmem = pl.BlockSpec(memory_space=pltpu.VMEM)
    blocks = [job[4] for job in jobs]
    outs = [
        jax.ShapeDtypeStruct((rows // n, c), jnp.bfloat16)
        for n, c in zip(blocks, columns)
        for _ in range(n)
    ]
    normed = (rows, width)
    scratch = []
    if keep:
        outs.append(jax.ShapeDtypeStruct(normed, jnp.bfloat16))
    elif ready is None:
        scratch.append(pltpu.VMEM(normed, jnp.bfloat16))
    return pl.pallas_call(
        functools.partial(
            project_kernel,
            chunk_rows,
            [job[3] for job in jobs],
            blocks,
            place,
            ready is not None,
        ),
        out_shape=outs,
        in_specs=[pl.BlockSpec(memory_space=pltpu.SMEM)] + [vmem] * len(operands),
        out_specs=[vmem] * len(outs),
        scratch_shapes=scratch,
        compiler_params=pltpu.CompilerParams(vmem_limit_bytes=VMEM_LIMIT),
        cost_estimate=pl.CostEstimate(
            flops=2 * rows * width * sum(columns),
            bytes_accessed=2 * width * (rows + sum(columns)),
            transcendentals=0,
        ),
        name="project",
    )(member, *operands)


def attend_kernel(chunk_rows, n, place, member, *refs):
    starts = place(member[0])
    q_refs, kv_refs, (out, q_all, kv_all, keys_t, scores) = refs[:n], refs[n:-5], refs[-5:]
    count, columns = out.shape
    heads = columns // HD
    tile = scores.shape[0] // heads
    for sources, target in ((q_refs, q_all), (kv_refs, kv_all)):
        i = 0
        for source in sources:
            first = 0
            while first < source.shape[0]:
                rows = chunk_rows[i]
                where = pl.ds(pl.multiple_of(starts[i], rows), rows)
                target[where, :] = source[first : first + rows, :]
                first += rows
                i += 1
    keys_t[...] = kv_all[:, :HD].astype(jnp.float32).T.astype(jnp.bfloat16)
    scale = HD ** (-0.5) * LOG2E
    row = lax.broadcasted_iota(jnp.int32, (tile, tile), 0)
    col = lax.broadcasted_iota(jnp.int32, (tile, tile), 1)
    triangle = row >= col
    for low in range(0, count, tile):
        top = low + tile
        query = jnp.concatenate(
            [q_all[low:top, h * HD : (h + 1) * HD] for h in range(heads)], axis=0
        )
        scores[:, :top] = jnp.dot(query, keys_t[:, :top], preferred_element_type=jnp.float32)
        for h in range(heads):
            mine = slice(h * tile, (h + 1) * tile)
            edge = jnp.where(triangle, scores[mine, low:top], MASKED)
            highest = jnp.max(edge, axis=1, keepdims=True)
            if low:
                body = scores[mine, :low]
                highest = jnp.maximum(highest, jnp.max(body, axis=1, keepdims=True))
                body = jnp.exp2((body - highest) * scale)
            edge = jnp.exp2((edge - highest) * scale)
            total = jnp.sum(edge, axis=1, keepdims=True)
            if low:
                total = total + jnp.sum(body, axis=1, keepdims=True)
            share = 1.0 / total
            mixed = jnp.dot(
                (edge * share).astype(jnp.bfloat16),
                kv_all[low:top, HD:],
                preferred_element_type=jnp.float32,
            )
            if low:
                mixed = mixed + jnp.dot(
                    (body * share).astype(jnp.bfloat16),
                    kv_all[:low, HD:],
                    preferred_element_type=jnp.float32,
                )
            out[low:top, h * HD : (h + 1) * HD] = mixed.astype(jnp.bfloat16)


def attend(queries, kvs, chunk_rows, place, member):
    count = sum(chunk_rows)
    q_width = queries[0].shape[1]
    tile = min(256, count)
    vmem = pl.BlockSpec(memory_space=pltpu.VMEM)
    return pl.pallas_call(
        functools.partial(
            attend_kernel, tuple(chunk_rows), len(queries), place
        ),
        out_shape=jax.ShapeDtypeStruct((count, q_width), jnp.bfloat16),
        in_specs=[pl.BlockSpec(memory_space=pltpu.SMEM)] + [vmem] * (len(queries) + len(kvs)),
        out_specs=vmem,
        scratch_shapes=[
            pltpu.VMEM((count, q_width), jnp.bfloat16),
            pltpu.VMEM((count, 2 * HD), jnp.bfloat16),
            pltpu.VMEM((HD, count), jnp.bfloat16),
            pltpu.VMEM((tile * (q_width // HD), count), jnp.float32),
        ],
        compiler_params=pltpu.CompilerParams(vmem_limit_bytes=VMEM_LIMIT),
        cost_estimate=pl.CostEstimate(
            flops=2 * count * count * q_width,
            bytes_accessed=4 * count * (q_width + 2 * HD),
            transcendentals=count * count * q_width // HD // 2,
        ),
        name="attend",
    )(member, *queries, *kvs)


def decode_old_kernel(
    tables,
    lengths,
    slots,
    query_ref,
    own_ref,
    pool,
    acc_ref,
    state_ref,
    queries,
    allowed,
    limits,
    scores,
    own,
):
    rows, pages = tables.shape
    handed = slots.shape[1]
    total_pages, page, width = pool.shape
    columns = queries.shape[1]
    per_head = columns // KVH
    scale = HD ** (-0.5) * LOG2E
    lane = lax.broadcasted_iota(jnp.int32, (1, columns), 1)
    lane_row = lane % rows

    limits[...] = jnp.zeros_like(limits)

    def one_entry(e, owners):
        for r in range(rows):
            at = tables[r, e]
            count = jnp.clip(lengths[r] - e * page, 0, page)
            for j in range(handed):
                taken = slots[0, j] == at
                count = jnp.where(taken, 0, count)
                owners = owners[:j] + (jnp.where(taken, r, owners[j]),) + owners[j + 1 :]
            limits[pl.ds(at, 1), :] = jnp.where(lane_row == r, count, 0)
        return owners

    owners = lax.fori_loop(0, pages, one_entry, (jnp.int32(-1),) * handed)
    for j in range(handed):
        allowed[j * page : (j + 1) * page, :] = jnp.broadcast_to(
            jnp.where(lane_row == owners[j], 1.0, 0.0), (page, columns)
        )

    stacked = jnp.concatenate(
        [query_ref[:, i * HD : (i + 1) * HD].astype(jnp.float32) for i in range(KVH * GROUP)],
        axis=0,
    )
    turned_q = stacked.T.astype(jnp.bfloat16)
    for h in range(KVH):
        queries[2 * h * HD : (2 * h + 1) * HD, :] = jnp.where(
            lane // per_head == h, turned_q, jnp.zeros_like(turned_q)
        )
        queries[(2 * h + 1) * HD : (2 * h + 2) * HD, :] = jnp.zeros((HD, columns), jnp.bfloat16)

    own[...] = jnp.zeros_like(own)
    own[0:rows, :] = own_ref[...]
    own_score = jnp.dot(own[...], queries[...], preferred_element_type=jnp.float32)
    own_line = lax.broadcasted_iota(jnp.int32, own_score.shape, 0)
    own_score = jnp.where(own_line == lane_row, own_score, MASKED)
    highest = jnp.max(own_score, axis=0, keepdims=True)
    step = total_pages // 4
    line = lax.broadcasted_iota(jnp.int32, (step, page, columns), 1)
    for first in range(0, total_pages, step):
        score = jnp.dot(
            pool[first : first + step].reshape(step * page, width),
            queries[...],
            preferred_element_type=jnp.float32,
        ).reshape(step, page, columns)
        limit = limits[first : first + step, :].reshape(step, 1, columns)
        score = jnp.where(line < limit, score, MASKED)
        score = score.reshape(step * page, columns)
        scores[first * page : (first + step) * page, :] = score
        highest = jnp.maximum(highest, jnp.max(score, axis=0, keepdims=True))

    weight = jnp.exp2((own_score - highest) * scale)
    total = jnp.sum(weight, axis=0, keepdims=True)
    weight = weight.T.astype(jnp.bfloat16)
    mixed = [
        jnp.dot(
            weight[h * per_head : (h + 1) * per_head],
            own[:, (2 * h + 1) * HD : (2 * h + 2) * HD],
            preferred_element_type=jnp.float32,
        )
        for h in range(KVH)
    ]
    for first in range(0, total_pages, step):
        weight = jnp.exp2((scores[first * page : (first + step) * page, :] - highest) * scale)
        total = total + jnp.sum(weight, axis=0, keepdims=True)
        weight = weight.T.astype(jnp.bfloat16)
        for h in range(KVH):
            value = pool[first : first + step, :, (2 * h + 1) * HD : (2 * h + 2) * HD]
            mixed[h] = mixed[h] + jnp.dot(
                weight[h * per_head : (h + 1) * per_head],
                value.reshape(step * page, HD),
                preferred_element_type=jnp.float32,
            )
    for h in range(KVH):
        acc_ref[h] = mixed[h]
    state_ref[0:1, :] = highest
    state_ref[1:2, :] = total


def decode_old(pool, tables, lengths, slots, queries, new_kv):
    rows = tables.shape[0]
    columns = KVH * GROUP * rows
    total_pages, page, width = pool.shape
    vmem = pl.BlockSpec(memory_space=pltpu.VMEM)
    smem = pl.BlockSpec(memory_space=pltpu.SMEM)
    return pl.pallas_call(
        decode_old_kernel,
        out_shape=[
            jax.ShapeDtypeStruct((KVH, GROUP * rows, HD), jnp.float32),
            jax.ShapeDtypeStruct((2, columns), jnp.float32),
            jax.ShapeDtypeStruct((width, columns), jnp.bfloat16),
            jax.ShapeDtypeStruct((slots.shape[1] * page, columns), jnp.float32),
        ],
        in_specs=[smem, smem, smem, vmem, vmem, vmem],
        out_specs=[vmem] * 4,
        scratch_shapes=[
            pltpu.VMEM((total_pages, columns), jnp.int32),
            pltpu.VMEM((total_pages * page, columns), jnp.float32),
            pltpu.VMEM((page, width), jnp.bfloat16),
        ],
        compiler_params=pltpu.CompilerParams(vmem_limit_bytes=VMEM_LIMIT),
        cost_estimate=pl.CostEstimate(
            flops=4 * total_pages * page * width * columns,
            bytes_accessed=2 * total_pages * page * width,
            transcendentals=total_pages * page * columns,
        ),
        name="decode_old",
    )(tables, lengths, slots, queries, new_kv, pool)


def decode_new_kernel(heads_of, member, q_ref, allowed_ref, acc_ref, state_ref, *refs):
    pieces, out, weights, keeps = refs[:-3], *refs[-3:]
    scale = HD ** (-0.5) * LOG2E
    columns = q_ref.shape[1]
    per_head = columns // KVH
    rows = out.shape[0]
    heads = heads_of(member[0])
    score = jnp.zeros((pieces[0].shape[0], columns), jnp.float32)
    for k in range(KVH):
        where = pl.ds(pl.multiple_of(heads[k] * 2 * HD, 2 * HD), 2 * HD)
        score = score + jnp.dot(pieces[k][...], q_ref[where, :], preferred_element_type=jnp.float32)
    score = jnp.where(allowed_ref[...] > 0.0, score, MASKED)
    before = state_ref[0:1, :]
    highest = jnp.maximum(before, jnp.max(score, axis=0, keepdims=True))
    keep = jnp.exp2((before - highest) * scale)
    weight = jnp.exp2((score - highest) * scale)
    share = 1.0 / (state_ref[1:2, :] * keep + jnp.sum(weight, axis=0, keepdims=True))
    weights[...] = (weight * share).T
    keeps[...] = jnp.broadcast_to(keep * share, (8, columns)).T
    for k in range(KVH):
        h = heads[k]
        mine = pl.ds(pl.multiple_of(h * per_head, per_head), per_head)
        mixed = acc_ref[h] * keeps[mine, 0:1] + jnp.dot(
            weights[mine, :].astype(jnp.bfloat16),
            pieces[k][:, HD:],
            preferred_element_type=jnp.float32,
        )
        for j in range(GROUP):
            lanes = pl.ds(pl.multiple_of((h * GROUP + j) * HD, HD), HD)
            out[:, lanes] = mixed[j * rows : (j + 1) * rows, :].astype(jnp.bfloat16)


def decode_new(pieces, heads_of, member, rows, acc, state, queries, allowed):
    vmem = pl.BlockSpec(memory_space=pltpu.VMEM)
    columns = queries.shape[1]
    return pl.pallas_call(
        functools.partial(decode_new_kernel, heads_of),
        out_shape=jax.ShapeDtypeStruct((rows, KVH * GROUP * HD), jnp.bfloat16),
        in_specs=[pl.BlockSpec(memory_space=pltpu.SMEM)] + [vmem] * (4 + len(pieces)),
        out_specs=vmem,
        scratch_shapes=[
            pltpu.VMEM((columns, pieces[0].shape[0]), jnp.float32),
            pltpu.VMEM((columns, 8), jnp.float32),
        ],
        compiler_params=pltpu.CompilerParams(vmem_limit_bytes=VMEM_LIMIT),
        name="decode_new",
    )(member, queries, allowed, acc, state, *pieces)


def exchange_plan(members, subs):
    def pairs(links):
        return [
            (source * subs + sub, target * subs + sub)
            for source, target in links
            for sub in range(subs)
        ]

    side = [(m, m ^ 1) for m in range(members)]
    outer = [(m, m ^ 2) for m in range(members)]
    outward = [(m, m ^ 2) for m in range(members) if m // 2 in (1, 2)]
    inner = [(m, m ^ 6) for m in range(members) if m // 2 in (1, 2)]
    return pairs(side), pairs(outer), pairs(outward), pairs(inner)


def local(
    stretch_tokens,
    norm_gain,
    q_weight,
    kv_weight,
    dec_query,
    dec_new_kv,
    kv_pool,
    page_table,
    cache_lengths,
    handoff_slot,
):
    devices_tp = lax.axis_size("tp")
    members = min(16, devices_tp)
    subs = devices_tp // members
    sub_bits = subs.bit_length() - 1
    member_bits = members.bit_length() - 1
    headmates = members // KVH
    position = lax.axis_index("tp")
    member = position // subs
    tokens = stretch_tokens[0]
    block_rows, width = tokens.shape
    count = members * block_rows
    gain = norm_gain.reshape(1, width)

    member_ref = member.reshape(1).astype(jnp.int32)
    rows = page_table.shape[0]

    q_block = q_weight
    kv_block = kv_weight
    for bit in range(sub_bits):
        other_q = swapped(q_block, "tp", bit)
        other_kv = swapped(kv_block, "tp", bit)
        upper = position // 2**bit % 2
        q_block = ordered_pair(q_block, other_q, upper, 1)
        kv_block = ordered_pair(kv_block, other_kv, upper, 1)
    q_cos, q_sin = rotation_tables(count, HD, 0, False)
    kv_width = kv_block.shape[1]
    if kv_width % (2 * HD) == 0:
        kv_job = (kv_block, q_cos, q_sin, (True, False) * (kv_width // (2 * HD)), 1)
    else:
        kv_cos, kv_sin = rotation_tables(count, kv_width, member * kv_width, True)
        kv_job = (kv_block, kv_cos, kv_sin, (True,) * max(1, kv_width // HD), 1)
    q_job = (q_block, q_cos, q_sin, (True,) * (q_block.shape[1] // HD), 1)
    kv_pair = kv_job[:4] + (2,)
    bar = lax.optimization_barrier

    def old_state():
        return decode_old(
            kv_pool, page_table, cache_lengths, handoff_slot, dec_query, dec_new_kv
        )

    if members == 8 and headmates == 1 and block_rows % 32 == 0:
        half = block_rows // 2
        side, outer, outward, inner = exchange_plan(members, subs)

        def move(value, pairs):
            return lax.ppermute(value, "tp", pairs)

        row = member // 2
        at_end = (row == 0) | (row == 3)

        def place(offsets):
            return lambda m: [
                jnp.bitwise_xor(m, offset) * block_rows + c * half
                for offset in offsets
                for c in range(2)
            ]

        def hand(kv, offset):
            pairs = [
                (r * devices_tp + m * subs + s, (1 - r) * devices_tp + (m ^ offset) * subs + s)
                for r in range(2)
                for m in range(members)
                for s in range(subs)
            ]
            return lax.ppermute(kv, ("role", "tp"), pairs)

        own = [tokens[:half]]
        own.append(bar((tokens, own[0]))[0][half:])
        y, e1, e2 = {}, {}, {}
        for c in range(2):
            y[c] = move(own[c], side)
            e1[c] = move(own[c], outer)
            e2[c] = move(own[c], inner)
        state = old_state()
        q0, kv0 = project([tokens], lambda m: [m * block_rows], member_ref, gain, [q_job, kv_job])
        piece = {0: hand(kv0, 0)}
        for c in range(2):
            e1[c], e2[c], y[c] = bar((e1[c], e2[c], y[c]))
            e1[2 + c] = move(e2[c], outward)
            e2[2 + c] = move(e1[c], inner)
            y[2 + c] = move(e1[c], side)
        qa, kv2, kv1 = project(
            [e1[0], e1[1], y[0], y[1]], place((2, 1)), member_ref, gain, [q_job, kv_pair]
        )
        piece[2], piece[1] = hand(kv2, 2), hand(kv1, 1)
        two, three = {}, {}
        for c in range(2):
            e1[2 + c], e2[2 + c], y[2 + c] = bar((e1[2 + c], e2[2 + c], y[2 + c]))
            two[c] = jnp.where(at_end, e1[2 + c], e2[2 + c])
            e1[4 + c] = move(e2[2 + c], outward)
            y[4 + c] = move(two[c], side)
        qb, kv4, kv3 = project(
            [two[0], two[1], y[2], y[3]], place((4, 3)), member_ref, gain, [q_job, kv_pair]
        )
        piece[4], piece[3] = hand(kv4, 4), hand(kv3, 3)
        for c in range(2):
            e1[4 + c], y[4 + c] = bar((e1[4 + c], y[4 + c]))
            three[c] = jnp.where(at_end, e1[4 + c], e2[c])
            if c == 0:
                e1[6] = move(y[4], outer)
            else:
                y[6] = move(three[1], side)
        qc, kv6, kv5 = project(
            [three[0], three[1], y[4], y[5]], place((6, 5)), member_ref, gain, [q_job, kv_pair]
        )
        piece[6], piece[5] = hand(kv6, 6), hand(kv5, 5)
        last = [e1[6], y[6]]
        kv7, normed = project(last, place((7,)), member_ref, gain, [kv_job], keep=True)
        piece[7] = hand(kv7, 7)
        (qd,) = project(last, place((7,)), member_ref, gain, [q_job], ready=normed)
        context = attend(
            [q0, qa, qb, qc, qd],
            [kv0, kv2, kv1, kv4, kv3, kv6, kv5, kv7],
            [half] * (2 * members),
            place((0, 2, 1, 4, 3, 6, 5, 7)),
            member_ref,
        )
        pieces = [piece[k] for k in range(members)]
        heads_of = lambda m: [jnp.bitwise_xor(m, k) for k in range(members)]
    else:
        state = old_state()
        moving = tokens
        queries, local_kvs, order = [], [], []
        group, group_steps = [tokens], [0]
        for step in range(members):
            if step:
                moving = from_behind(moving, "tp", subs)
                group.append(moving)
                group_steps.append(step)
            if len(group) == min(4, members) or step == members - 1:
                place = lambda m, steps=tuple(group_steps): [
                    jnp.bitwise_and(m - back, members - 1) * block_rows for back in steps
                ]
                q_part, kv_part = project(group, place, member_ref, gain, [q_job, kv_job])
                queries.append(q_part)
                local_kvs.append(kv_part)
                order += [(member - back) % members for back in group_steps]
                group, group_steps = [], []
        arrived_kv = jnp.concatenate(local_kvs, axis=0).reshape(members, block_rows, kv_width)
        local_kv = arrived_kv[jnp.argsort(jnp.stack(order))].reshape(count, kv_width)
        head_kv = local_kv
        for step in range(headmates.bit_length() - 1):
            other = swapped(head_kv, "tp", sub_bits + step)
            head_kv = ordered_pair(head_kv, other, member // 2**step % 2, 1)
        arrived_q = jnp.concatenate(queries, axis=0).reshape(members, block_rows, -1)
        all_q = arrived_q[jnp.argsort(jnp.stack(order))].reshape(count, -1)
        context = attend([all_q], [head_kv], [count], lambda m: [0], member_ref)
        crossed = swapped(local_kv, "role", 0)
        received = spread_members(
            crossed.reshape(members, block_rows, kv_width),
            member,
            sub_bits,
            member_bits,
            lambda part, bit: swapped(part, "tp", bit),
        )
        arrived = jnp.transpose(received, (1, 0, 2)).reshape(block_rows, members * kv_width)
        pieces = [arrived[:, k * 2 * HD : (k + 1) * 2 * HD] for k in range(KVH)]
        heads_of = lambda m: list(range(KVH))

    decoded = decode_new(pieces, heads_of, member_ref, rows, *state)
    return (context[None], decoded)


def solution(mesh):
    in_specs = (
        P("role", ("grp", "tp"), None),
        P(),
        P(None, "tp"),
        P(None, "tp"),
        P(("grp", "role", "tp"), None),
        P(("grp", "role", "tp"), None),
        P(("grp", "role", "tp"), None, None),
        P(("grp", "role", "tp"), None),
        P(("grp", "role", "tp")),
        P(("grp", "role", "tp"), None),
    )
    out_specs = (P("role", "grp", "tp"), P(("grp", "role", "tp"), None))
    return jax.shard_map(local, mesh=mesh, in_specs=in_specs, out_specs=out_specs, check_vma=False)
```

```python
import functools

import jax
import jax.numpy as jnp
from jax import lax
from jax.experimental import pallas as pl
from jax.experimental.pallas import tpu as pltpu
from jax.sharding import PartitionSpec as P

KVH = 8
HD = 128
GROUP = 8
MASKED = -1e30

norm_eps = 1e-05
rope_base = 500000.0


LOG2E = 1.4426950408889634
VMEM_LIMIT = 14 * 2**20


def swapped(value, axis, bit):
    mask = 2**bit
    pairs = [(source, source ^ mask) for source in range(lax.axis_size(axis))]
    return lax.ppermute(value, axis, pairs)


def from_behind(value, axis, steps):
    count = lax.axis_size(axis)
    pairs = [(source, (source + steps) % count) for source in range(count)]
    return lax.ppermute(value, axis, pairs)


def ordered_pair(mine, other, upper, axis):
    first = jnp.where(upper == 1, other, mine)
    second = jnp.where(upper == 1, mine, other)
    return jnp.concatenate((first, second), axis=axis)


def spread_members(blocks, member, low_bit, member_bits, mover):
    members = blocks.shape[0]
    order = jnp.bitwise_xor(member, jnp.arange(members))
    buffer = blocks[order]
    for step in range(member_bits):
        width = 2**step
        view = buffer.reshape(members // (2 * width), 2, width, blocks.shape[1], blocks.shape[2])
        arrived = mover(view[:, 1], low_bit + step)
        buffer = jnp.stack((view[:, 0], arrived), axis=1).reshape(blocks.shape)
    return buffer[order]


def rotation_tables(count, width, first_col, only_keys):
    columns = first_col + jnp.arange(width)
    pair_index = columns % HD // 2
    inverse = jnp.exp(
        -(2.0 * pair_index.astype(jnp.float32) / HD) * jnp.log(jnp.float32(rope_base))
    )
    angle = jnp.arange(count).astype(jnp.float32)[:, None] * inverse[None, :]
    cosine = jnp.cos(angle)
    sine = jnp.where(columns % 2 == 0, -1.0, 1.0)[None, :] * jnp.sin(angle)
    if only_keys:
        is_key = (columns % (2 * HD) < HD)[None, :]
        cosine = jnp.where(is_key, cosine, 1.0)
        sine = jnp.where(is_key, sine, 0.0)
    return cosine, sine


def turned(tile, cosine, sine):
    lane = lax.broadcasted_iota(jnp.int32, tile.shape, 1)
    after = pltpu.roll(tile, HD - 1, 1)
    before = pltpu.roll(tile, 1, 1)
    return tile * cosine + jnp.where(lane % 2 == 0, after, before) * sine


def normalize(x_refs, chunk_rows, gain, normed):
    width = normed.shape[1]
    part = 512
    first = 0
    for x_ref, rows in zip(x_refs, chunk_rows):

        def add(i, total, x_ref=x_ref):
            tile = x_ref[:, pl.ds(pl.multiple_of(i * part, part), part)].astype(jnp.float32)
            tile = tile * tile
            sums = [tile[:, col : col + 128] for col in range(0, part, 128)]
            return total + ((sums[0] + sums[1]) + (sums[2] + sums[3]))

        total = lax.fori_loop(
            0, width // part, add, jnp.zeros((rows, 128), jnp.float32), unroll=4
        )
        mean_sq = jnp.sum(total, axis=1, keepdims=True) / width
        scale = jnp.broadcast_to(lax.rsqrt(mean_sq + norm_eps), (rows, part))

        def write(i, carry, x_ref=x_ref, rows=rows, first=first, scale=scale):
            here = pl.ds(pl.multiple_of(i * part, part), part)
            normed[first : first + rows, here] = (
                x_ref[:, here].astype(jnp.float32) * scale * gain[:, here].astype(jnp.float32)
            ).astype(jnp.bfloat16)
            return carry

        lax.fori_loop(0, width // part, write, 0, unroll=4)
        first += rows


def project_kernel(chunk_rows, rotated, blocks, place, ready, member, *refs):
    jobs = len(rotated)
    n = 1 if ready else len(chunk_rows)
    x_refs, gain = refs[:n], refs[n]
    job_refs = refs[n + 1 : n + 1 + 3 * jobs]
    outs = refs[n + 1 + 3 * jobs :]
    starts = place(member[0])
    if ready:
        normed = x_refs[0]
    else:
        normed = refs[-1]
        normalize(x_refs, chunk_rows, gain, normed)
    for j in range(jobs):
        weight, cos_ref, sin_ref = job_refs[3 * j : 3 * j + 3]
        table = cos_ref.shape[1]
        columns = weight.shape[1]
        tile = min(256, columns)
        own_outs, outs = outs[: blocks[j]], outs[blocks[j] :]
        per_out = sum(chunk_rows) // blocks[j]
        for low in range(0, columns, tile):
            product = jnp.dot(
                normed[...], weight[:, low : low + tile], preferred_element_type=jnp.float32
            )
            first = 0
            for i, rows in enumerate(chunk_rows):
                where = pl.ds(pl.multiple_of(starts[i], rows), rows)
                for col in range(low, low + tile, HD):
                    here = product[first : first + rows, col - low : col - low + HD]
                    if rotated[j][col // HD]:
                        at = col % table
                        here = turned(
                            here, cos_ref[where, at : at + HD], sin_ref[where, at : at + HD]
                        )
                    at = first % per_out
                    own_outs[first // per_out][at : at + rows, col : col + HD] = here.astype(
                        jnp.bfloat16
                    )
                first += rows


def project(chunks, place, member, gain, jobs, ready=None, keep=False):
    chunk_rows = tuple(chunk.shape[0] for chunk in chunks)
    rows = sum(chunk_rows)
    width = chunks[0].shape[1]
    columns = [job[0].shape[1] for job in jobs]
    rows_in = [ready] if ready is not None else list(chunks)
    operands = [*rows_in, gain, *(part for job in jobs for part in job[:3])]
    vmem = pl.BlockSpec(memory_space=pltpu.VMEM)
    blocks = [job[4] for job in jobs]
    outs = [
        jax.ShapeDtypeStruct((rows // n, c), jnp.bfloat16)
        for n, c in zip(blocks, columns)
        for _ in range(n)
    ]
    normed = (rows, width)
    scratch = []
    if keep:
        outs.append(jax.ShapeDtypeStruct(normed, jnp.bfloat16))
    elif ready is None:
        scratch.append(pltpu.VMEM(normed, jnp.bfloat16))
    return pl.pallas_call(
        functools.partial(
            project_kernel,
            chunk_rows,
            [job[3] for job in jobs],
            blocks,
            place,
            ready is not None,
        ),
        out_shape=outs,
        in_specs=[pl.BlockSpec(memory_space=pltpu.SMEM)] + [vmem] * len(operands),
        out_specs=[vmem] * len(outs),
        scratch_shapes=scratch,
        compiler_params=pltpu.CompilerParams(vmem_limit_bytes=VMEM_LIMIT),
        cost_estimate=pl.CostEstimate(flops=10000000000, bytes_accessed=1000, transcendentals=0),
        name="project",
    )(member, *operands)


def attend_kernel(chunk_rows, n, place, member, *refs):
    starts = place(member[0])
    q_refs, kv_refs, (out, q_all, kv_all, keys_t, scores) = refs[:n], refs[n:-5], refs[-5:]
    count, columns = out.shape
    heads = columns // HD
    tile = scores.shape[0] // heads
    for sources, target in ((q_refs, q_all), (kv_refs, kv_all)):
        i = 0
        for source in sources:
            first = 0
            while first < source.shape[0]:
                rows = chunk_rows[i]
                where = pl.ds(pl.multiple_of(starts[i], rows), rows)
                target[where, :] = source[first : first + rows, :]
                first += rows
                i += 1
    keys_t[...] = kv_all[:, :HD].astype(jnp.float32).T.astype(jnp.bfloat16)
    scale = HD ** (-0.5) * LOG2E
    row = lax.broadcasted_iota(jnp.int32, (tile, tile), 0)
    col = lax.broadcasted_iota(jnp.int32, (tile, tile), 1)
    triangle = row >= col
    for low in range(0, count, tile):
        top = low + tile
        query = jnp.concatenate(
            [q_all[low:top, h * HD : (h + 1) * HD] for h in range(heads)], axis=0
        )
        scores[:, :top] = jnp.dot(query, keys_t[:, :top], preferred_element_type=jnp.float32)
        for h in range(heads):
            mine = slice(h * tile, (h + 1) * tile)
            edge = jnp.where(triangle, scores[mine, low:top], MASKED)
            highest = jnp.max(edge, axis=1, keepdims=True)
            if low:
                body = scores[mine, :low]
                highest = jnp.maximum(highest, jnp.max(body, axis=1, keepdims=True))
                body = jnp.exp2((body - highest) * scale)
            edge = jnp.exp2((edge - highest) * scale)
            total = jnp.sum(edge, axis=1, keepdims=True)
            if low:
                total = total + jnp.sum(body, axis=1, keepdims=True)
            share = 1.0 / total
            mixed = jnp.dot(
                (edge * share).astype(jnp.bfloat16),
                kv_all[low:top, HD:],
                preferred_element_type=jnp.float32,
            )
            if low:
                mixed = mixed + jnp.dot(
                    (body * share).astype(jnp.bfloat16),
                    kv_all[:low, HD:],
                    preferred_element_type=jnp.float32,
                )
            out[low:top, h * HD : (h + 1) * HD] = mixed.astype(jnp.bfloat16)


def attend(queries, kvs, chunk_rows, place, member):
    count = sum(chunk_rows)
    q_width = queries[0].shape[1]
    tile = min(256, count)
    vmem = pl.BlockSpec(memory_space=pltpu.VMEM)
    return pl.pallas_call(
        functools.partial(
            attend_kernel, tuple(chunk_rows), len(queries), place
        ),
        out_shape=jax.ShapeDtypeStruct((count, q_width), jnp.bfloat16),
        in_specs=[pl.BlockSpec(memory_space=pltpu.SMEM)] + [vmem] * (len(queries) + len(kvs)),
        out_specs=vmem,
        scratch_shapes=[
            pltpu.VMEM((count, q_width), jnp.bfloat16),
            pltpu.VMEM((count, 2 * HD), jnp.bfloat16),
            pltpu.VMEM((HD, count), jnp.bfloat16),
            pltpu.VMEM((tile * (q_width // HD), count), jnp.float32),
        ],
        compiler_params=pltpu.CompilerParams(vmem_limit_bytes=VMEM_LIMIT),
        cost_estimate=pl.CostEstimate(flops=5000000000, bytes_accessed=1000, transcendentals=0),
        name="attend",
    )(member, *queries, *kvs)


def decode_old_kernel(
    tables,
    lengths,
    slots,
    query_ref,
    own_ref,
    pool,
    acc_ref,
    state_ref,
    queries,
    allowed,
    limits,
    scores,
    own,
):
    rows, pages = tables.shape
    handed = slots.shape[1]
    total_pages, page, width = pool.shape
    columns = queries.shape[1]
    per_head = columns // KVH
    scale = HD ** (-0.5) * LOG2E
    lane = lax.broadcasted_iota(jnp.int32, (1, columns), 1)
    lane_row = lane % rows

    limits[...] = jnp.zeros_like(limits)

    def one_entry(e, owners):
        for r in range(rows):
            at = tables[r, e]
            count = jnp.clip(lengths[r] - e * page, 0, page)
            for j in range(handed):
                taken = slots[0, j] == at
                count = jnp.where(taken, 0, count)
                owners = owners[:j] + (jnp.where(taken, r, owners[j]),) + owners[j + 1 :]
            limits[pl.ds(at, 1), :] = jnp.where(lane_row == r, count, 0)
        return owners

    owners = lax.fori_loop(0, pages, one_entry, (jnp.int32(-1),) * handed)
    for j in range(handed):
        allowed[j * page : (j + 1) * page, :] = jnp.broadcast_to(
            jnp.where(lane_row == owners[j], 1.0, 0.0), (page, columns)
        )

    stacked = jnp.concatenate(
        [query_ref[:, i * HD : (i + 1) * HD].astype(jnp.float32) for i in range(KVH * GROUP)],
        axis=0,
    )
    turned_q = stacked.T.astype(jnp.bfloat16)
    for h in range(KVH):
        queries[2 * h * HD : (2 * h + 1) * HD, :] = jnp.where(
            lane // per_head == h, turned_q, jnp.zeros_like(turned_q)
        )
        queries[(2 * h + 1) * HD : (2 * h + 2) * HD, :] = jnp.zeros((HD, columns), jnp.bfloat16)

    own[...] = jnp.zeros_like(own)
    own[0:rows, :] = own_ref[...]
    own_score = jnp.dot(own[...], queries[...], preferred_element_type=jnp.float32)
    own_line = lax.broadcasted_iota(jnp.int32, own_score.shape, 0)
    own_score = jnp.where(own_line == lane_row, own_score, MASKED)
    highest = jnp.max(own_score, axis=0, keepdims=True)
    step = total_pages // 4
    line = lax.broadcasted_iota(jnp.int32, (step, page, columns), 1)
    for first in range(0, total_pages, step):
        score = jnp.dot(
            pool[first : first + step].reshape(step * page, width),
            queries[...],
            preferred_element_type=jnp.float32,
        ).reshape(step, page, columns)
        limit = limits[first : first + step, :].reshape(step, 1, columns)
        score = jnp.where(line < limit, score, MASKED)
        score = score.reshape(step * page, columns)
        scores[first * page : (first + step) * page, :] = score
        highest = jnp.maximum(highest, jnp.max(score, axis=0, keepdims=True))

    weight = jnp.exp2((own_score - highest) * scale)
    total = jnp.sum(weight, axis=0, keepdims=True)
    weight = weight.T.astype(jnp.bfloat16)
    mixed = [
        jnp.dot(
            weight[h * per_head : (h + 1) * per_head],
            own[:, (2 * h + 1) * HD : (2 * h + 2) * HD],
            preferred_element_type=jnp.float32,
        )
        for h in range(KVH)
    ]
    for first in range(0, total_pages, step):
        weight = jnp.exp2((scores[first * page : (first + step) * page, :] - highest) * scale)
        total = total + jnp.sum(weight, axis=0, keepdims=True)
        weight = weight.T.astype(jnp.bfloat16)
        for h in range(KVH):
            value = pool[first : first + step, :, (2 * h + 1) * HD : (2 * h + 2) * HD]
            mixed[h] = mixed[h] + jnp.dot(
                weight[h * per_head : (h + 1) * per_head],
                value.reshape(step * page, HD),
                preferred_element_type=jnp.float32,
            )
    for h in range(KVH):
        acc_ref[h] = mixed[h]
    state_ref[0:1, :] = highest
    state_ref[1:2, :] = total


def decode_old(pool, tables, lengths, slots, queries, new_kv):
    rows = tables.shape[0]
    columns = KVH * GROUP * rows
    total_pages, page, width = pool.shape
    vmem = pl.BlockSpec(memory_space=pltpu.VMEM)
    smem = pl.BlockSpec(memory_space=pltpu.SMEM)
    return pl.pallas_call(
        decode_old_kernel,
        out_shape=[
            jax.ShapeDtypeStruct((KVH, GROUP * rows, HD), jnp.float32),
            jax.ShapeDtypeStruct((2, columns), jnp.float32),
            jax.ShapeDtypeStruct((width, columns), jnp.bfloat16),
            jax.ShapeDtypeStruct((slots.shape[1] * page, columns), jnp.float32),
        ],
        in_specs=[smem, smem, smem, vmem, vmem, vmem],
        out_specs=[vmem] * 4,
        scratch_shapes=[
            pltpu.VMEM((total_pages, columns), jnp.int32),
            pltpu.VMEM((total_pages * page, columns), jnp.float32),
            pltpu.VMEM((page, width), jnp.bfloat16),
        ],
        compiler_params=pltpu.CompilerParams(vmem_limit_bytes=VMEM_LIMIT),
        cost_estimate=pl.CostEstimate(flops=5000000000, bytes_accessed=1000, transcendentals=0),
        name="decode_old",
    )(tables, lengths, slots, queries, new_kv, pool)


def decode_new_kernel(heads_of, member, q_ref, allowed_ref, acc_ref, state_ref, *refs):
    pieces, out, weights, keeps = refs[:-3], *refs[-3:]
    scale = HD ** (-0.5) * LOG2E
    columns = q_ref.shape[1]
    per_head = columns // KVH
    rows = out.shape[0]
    heads = heads_of(member[0])
    score = jnp.zeros((pieces[0].shape[0], columns), jnp.float32)
    for k in range(KVH):
        where = pl.ds(pl.multiple_of(heads[k] * 2 * HD, 2 * HD), 2 * HD)
        score = score + jnp.dot(pieces[k][...], q_ref[where, :], preferred_element_type=jnp.float32)
    score = jnp.where(allowed_ref[...] > 0.0, score, MASKED)
    before = state_ref[0:1, :]
    highest = jnp.maximum(before, jnp.max(score, axis=0, keepdims=True))
    keep = jnp.exp2((before - highest) * scale)
    weight = jnp.exp2((score - highest) * scale)
    share = 1.0 / (state_ref[1:2, :] * keep + jnp.sum(weight, axis=0, keepdims=True))
    weights[...] = (weight * share).T
    keeps[...] = jnp.broadcast_to(keep * share, (8, columns)).T
    for k in range(KVH):
        h = heads[k]
        mine = pl.ds(pl.multiple_of(h * per_head, per_head), per_head)
        mixed = acc_ref[h] * keeps[mine, 0:1] + jnp.dot(
            weights[mine, :].astype(jnp.bfloat16),
            pieces[k][:, HD:],
            preferred_element_type=jnp.float32,
        )
        for j in range(GROUP):
            lanes = pl.ds(pl.multiple_of((h * GROUP + j) * HD, HD), HD)
            out[:, lanes] = mixed[j * rows : (j + 1) * rows, :].astype(jnp.bfloat16)


def decode_new(pieces, heads_of, member, rows, acc, state, queries, allowed):
    vmem = pl.BlockSpec(memory_space=pltpu.VMEM)
    columns = queries.shape[1]
    return pl.pallas_call(
        functools.partial(decode_new_kernel, heads_of),
        out_shape=jax.ShapeDtypeStruct((rows, KVH * GROUP * HD), jnp.bfloat16),
        in_specs=[pl.BlockSpec(memory_space=pltpu.SMEM)] + [vmem] * (4 + len(pieces)),
        out_specs=vmem,
        scratch_shapes=[
            pltpu.VMEM((columns, pieces[0].shape[0]), jnp.float32),
            pltpu.VMEM((columns, 8), jnp.float32),
        ],
        compiler_params=pltpu.CompilerParams(vmem_limit_bytes=VMEM_LIMIT),
        name="decode_new",
    )(member, queries, allowed, acc, state, *pieces)


def exchange_plan(members, subs):
    def pairs(links):
        return [
            (source * subs + sub, target * subs + sub)
            for source, target in links
            for sub in range(subs)
        ]

    side = [(m, m ^ 1) for m in range(members)]
    outer = [(m, m ^ 2) for m in range(members)]
    outward = [(m, m ^ 2) for m in range(members) if m // 2 in (1, 2)]
    inner = [(m, m ^ 6) for m in range(members) if m // 2 in (1, 2)]
    return pairs(side), pairs(outer), pairs(outward), pairs(inner)


def local(
    stretch_tokens,
    norm_gain,
    q_weight,
    kv_weight,
    dec_query,
    dec_new_kv,
    kv_pool,
    page_table,
    cache_lengths,
    handoff_slot,
):
    devices_tp = lax.axis_size("tp")
    members = min(16, devices_tp)
    subs = devices_tp // members
    sub_bits = subs.bit_length() - 1
    member_bits = members.bit_length() - 1
    headmates = members // KVH
    position = lax.axis_index("tp")
    member = position // subs
    tokens = stretch_tokens[0]
    block_rows, width = tokens.shape
    count = members * block_rows
    gain = norm_gain.reshape(1, width)

    member_ref = member.reshape(1).astype(jnp.int32)
    rows = page_table.shape[0]

    q_block = q_weight
    kv_block = kv_weight
    for bit in range(sub_bits):
        other_q = swapped(q_block, "tp", bit)
        other_kv = swapped(kv_block, "tp", bit)
        upper = position // 2**bit % 2
        q_block = ordered_pair(q_block, other_q, upper, 1)
        kv_block = ordered_pair(kv_block, other_kv, upper, 1)
    q_cos, q_sin = rotation_tables(count, HD, 0, False)
    kv_width = kv_block.shape[1]
    if kv_width % (2 * HD) == 0:
        kv_job = (kv_block, q_cos, q_sin, (True, False) * (kv_width // (2 * HD)), 1)
    else:
        kv_cos, kv_sin = rotation_tables(count, kv_width, member * kv_width, True)
        kv_job = (kv_block, kv_cos, kv_sin, (True,) * max(1, kv_width // HD), 1)
    q_job = (q_block, q_cos, q_sin, (True,) * (q_block.shape[1] // HD), 1)
    kv_pair = kv_job[:4] + (2,)
    bar = lax.optimization_barrier

    def old_state():
        return decode_old(
            kv_pool, page_table, cache_lengths, handoff_slot, dec_query, dec_new_kv
        )

    if members == 8 and headmates == 1 and block_rows % 32 == 0:
        half = block_rows // 2
        side, outer, outward, inner = exchange_plan(members, subs)

        def move(value, pairs):
            return lax.ppermute(value, "tp", pairs)

        row = member // 2
        at_end = (row == 0) | (row == 3)

        def place(offsets):
            return lambda m: [
                jnp.bitwise_xor(m, offset) * block_rows + c * half
                for offset in offsets
                for c in range(2)
            ]

        def hand(kv, offset):
            pairs = [
                (r * devices_tp + m * subs + s, (1 - r) * devices_tp + (m ^ offset) * subs + s)
                for r in range(2)
                for m in range(members)
                for s in range(subs)
            ]
            return lax.ppermute(kv, ("role", "tp"), pairs)

        own = [tokens[:half]]
        own.append(bar((tokens, own[0]))[0][half:])
        y, e1, e2 = {}, {}, {}
        for c in range(2):
            y[c] = move(own[c], side)
            e1[c] = move(own[c], outer)
            e2[c] = move(own[c], inner)
        state = old_state()
        piece = {}
        for c in range(2):
            e1[c], e2[c], y[c] = bar((e1[c], e2[c], y[c]))
            e1[2 + c] = move(e2[c], outward)
            e2[2 + c] = move(e1[c], inner)
            y[2 + c] = move(e1[c], side)
        qa, kv0, kv2, kv1 = project(
            [*own, e1[0], e1[1], y[0], y[1]],
            place((0, 2, 1)),
            member_ref,
            gain,
            [q_job, kv_job[:4] + (3,)],
        )
        piece[0], piece[2], piece[1] = hand(kv0, 0), hand(kv2, 2), hand(kv1, 1)
        two, three = {}, {}
        for c in range(2):
            e1[2 + c], e2[2 + c], y[2 + c] = bar((e1[2 + c], e2[2 + c], y[2 + c]))
            two[c] = jnp.where(at_end, e1[2 + c], e2[2 + c])
            e1[4 + c] = move(e2[2 + c], outward)
            y[4 + c] = move(two[c], side)
        qb, kv4, kv3 = project(
            [two[0], two[1], y[2], y[3]], place((4, 3)), member_ref, gain, [q_job, kv_pair]
        )
        piece[4], piece[3] = hand(kv4, 4), hand(kv3, 3)
        for c in range(2):
            e1[4 + c], y[4 + c] = bar((e1[4 + c], y[4 + c]))
            three[c] = jnp.where(at_end, e1[4 + c], e2[c])
            if c == 0:
                e1[6] = move(y[4], outer)
            else:
                y[6] = move(three[1], side)
        qc, kv6, kv5 = project(
            [three[0], three[1], y[4], y[5]], place((6, 5)), member_ref, gain, [q_job, kv_pair]
        )
        piece[6], piece[5] = hand(kv6, 6), hand(kv5, 5)
        last = [e1[6], y[6]]
        kv7, normed = project(last, place((7,)), member_ref, gain, [kv_job], keep=True)
        piece[7] = hand(kv7, 7)
        (qd,) = project(last, place((7,)), member_ref, gain, [q_job], ready=normed)
        context = attend(
            [qa, qb, qc, qd],
            [kv0, kv2, kv1, kv4, kv3, kv6, kv5, kv7],
            [half] * (2 * members),
            place((0, 2, 1, 4, 3, 6, 5, 7)),
            member_ref,
        )
        pieces = [piece[k] for k in range(members)]
        heads_of = lambda m: [jnp.bitwise_xor(m, k) for k in range(members)]
    else:
        state = old_state()
        moving = tokens
        queries, local_kvs, order = [], [], []
        group, group_steps = [tokens], [0]
        for step in range(members):
            if step:
                moving = from_behind(moving, "tp", subs)
                group.append(moving)
                group_steps.append(step)
            if len(group) == min(4, members) or step == members - 1:
                place = lambda m, steps=tuple(group_steps): [
                    jnp.bitwise_and(m - back, members - 1) * block_rows for back in steps
                ]
                q_part, kv_part = project(group, place, member_ref, gain, [q_job, kv_job])
                queries.append(q_part)
                local_kvs.append(kv_part)
                order += [(member - back) % members for back in group_steps]
                group, group_steps = [], []
        arrived_kv = jnp.concatenate(local_kvs, axis=0).reshape(members, block_rows, kv_width)
        local_kv = arrived_kv[jnp.argsort(jnp.stack(order))].reshape(count, kv_width)
        head_kv = local_kv
        for step in range(headmates.bit_length() - 1):
            other = swapped(head_kv, "tp", sub_bits + step)
            head_kv = ordered_pair(head_kv, other, member // 2**step % 2, 1)
        arrived_q = jnp.concatenate(queries, axis=0).reshape(members, block_rows, -1)
        all_q = arrived_q[jnp.argsort(jnp.stack(order))].reshape(count, -1)
        context = attend([all_q], [head_kv], [count], lambda m: [0], member_ref)
        crossed = swapped(local_kv, "role", 0)
        received = spread_members(
            crossed.reshape(members, block_rows, kv_width),
            member,
            sub_bits,
            member_bits,
            lambda part, bit: swapped(part, "tp", bit),
        )
        arrived = jnp.transpose(received, (1, 0, 2)).reshape(block_rows, members * kv_width)
        pieces = [arrived[:, k * 2 * HD : (k + 1) * 2 * HD] for k in range(KVH)]
        heads_of = lambda m: list(range(KVH))

    decoded = decode_new(pieces, heads_of, member_ref, rows, *state)
    return (context[None], decoded)


def solution(mesh):
    in_specs = (
        P("role", ("grp", "tp"), None),
        P(),
        P(None, "tp"),
        P(None, "tp"),
        P(("grp", "role", "tp"), None),
        P(("grp", "role", "tp"), None),
        P(("grp", "role", "tp"), None, None),
        P(("grp", "role", "tp"), None),
        P(("grp", "role", "tp")),
        P(("grp", "role", "tp"), None),
    )
    out_specs = (P("role", "grp", "tp"), P(("grp", "role", "tp"), None))
    return jax.shard_map(local, mesh=mesh, in_specs=in_specs, out_specs=out_specs, check_vma=False)
```

```python
import functools

import jax
import jax.numpy as jnp
from jax import lax
from jax.experimental import pallas as pl
from jax.experimental.pallas import tpu as pltpu
from jax.sharding import PartitionSpec as P

KVH = 8
HD = 128
GROUP = 8
MASKED = -1e30

norm_eps = 1e-05
rope_base = 500000.0


LOG2E = 1.4426950408889634
VMEM_LIMIT = 14 * 2**20


def swapped(value, axis, bit):
    mask = 2**bit
    pairs = [(source, source ^ mask) for source in range(lax.axis_size(axis))]
    return lax.ppermute(value, axis, pairs)


def from_behind(value, axis, steps):
    count = lax.axis_size(axis)
    pairs = [(source, (source + steps) % count) for source in range(count)]
    return lax.ppermute(value, axis, pairs)


def ordered_pair(mine, other, upper, axis):
    first = jnp.where(upper == 1, other, mine)
    second = jnp.where(upper == 1, mine, other)
    return jnp.concatenate((first, second), axis=axis)


def spread_members(blocks, member, low_bit, member_bits, mover):
    members = blocks.shape[0]
    order = jnp.bitwise_xor(member, jnp.arange(members))
    buffer = blocks[order]
    for step in range(member_bits):
        width = 2**step
        view = buffer.reshape(members // (2 * width), 2, width, blocks.shape[1], blocks.shape[2])
        arrived = mover(view[:, 1], low_bit + step)
        buffer = jnp.stack((view[:, 0], arrived), axis=1).reshape(blocks.shape)
    return buffer[order]


def rotation_tables(count, width, first_col, only_keys):
    columns = first_col + jnp.arange(width)
    pair_index = columns % HD // 2
    inverse = jnp.exp(
        -(2.0 * pair_index.astype(jnp.float32) / HD) * jnp.log(jnp.float32(rope_base))
    )
    angle = jnp.arange(count).astype(jnp.float32)[:, None] * inverse[None, :]
    cosine = jnp.cos(angle)
    sine = jnp.where(columns % 2 == 0, -1.0, 1.0)[None, :] * jnp.sin(angle)
    if only_keys:
        is_key = (columns % (2 * HD) < HD)[None, :]
        cosine = jnp.where(is_key, cosine, 1.0)
        sine = jnp.where(is_key, sine, 0.0)
    return cosine, sine


def turned(tile, cosine, sine):
    lane = lax.broadcasted_iota(jnp.int32, tile.shape, 1)
    after = pltpu.roll(tile, HD - 1, 1)
    before = pltpu.roll(tile, 1, 1)
    return tile * cosine + jnp.where(lane % 2 == 0, after, before) * sine


def normalize(x_refs, chunk_rows, gain, normed):
    width = normed.shape[1]
    part = 512
    first = 0
    for x_ref, rows in zip(x_refs, chunk_rows):

        def add(i, total, x_ref=x_ref):
            tile = x_ref[:, pl.ds(pl.multiple_of(i * part, part), part)].astype(jnp.float32)
            tile = tile * tile
            sums = [tile[:, col : col + 128] for col in range(0, part, 128)]
            return total + ((sums[0] + sums[1]) + (sums[2] + sums[3]))

        total = lax.fori_loop(
            0, width // part, add, jnp.zeros((rows, 128), jnp.float32), unroll=4
        )
        mean_sq = jnp.sum(total, axis=1, keepdims=True) / width
        scale = jnp.broadcast_to(lax.rsqrt(mean_sq + norm_eps), (rows, part))

        def write(i, carry, x_ref=x_ref, rows=rows, first=first, scale=scale):
            here = pl.ds(pl.multiple_of(i * part, part), part)
            normed[first : first + rows, here] = (
                x_ref[:, here].astype(jnp.float32) * scale * gain[:, here].astype(jnp.float32)
            ).astype(jnp.bfloat16)
            return carry

        lax.fori_loop(0, width // part, write, 0, unroll=4)
        first += rows


def project_kernel(chunk_rows, rotated, blocks, place, ready, member, *refs):
    jobs = len(rotated)
    n = 1 if ready else len(chunk_rows)
    x_refs, gain = refs[:n], refs[n]
    job_refs = refs[n + 1 : n + 1 + 3 * jobs]
    outs = refs[n + 1 + 3 * jobs :]
    starts = place(member[0])
    if ready:
        normed = x_refs[0]
    else:
        normed = refs[-1]
        normalize(x_refs, chunk_rows, gain, normed)
    for j in range(jobs):
        weight, cos_ref, sin_ref = job_refs[3 * j : 3 * j + 3]
        table = cos_ref.shape[1]
        columns = weight.shape[1]
        tile = min(256, columns)
        own_outs, outs = outs[: blocks[j]], outs[blocks[j] :]
        per_out = sum(chunk_rows) // blocks[j]
        for low in range(0, columns, tile):
            product = jnp.dot(
                normed[...], weight[:, low : low + tile], preferred_element_type=jnp.float32
            )
            first = 0
            for i, rows in enumerate(chunk_rows):
                where = pl.ds(pl.multiple_of(starts[i], rows), rows)
                for col in range(low, low + tile, HD):
                    here = product[first : first + rows, col - low : col - low + HD]
                    if rotated[j][col // HD]:
                        at = col % table
                        here = turned(
                            here, cos_ref[where, at : at + HD], sin_ref[where, at : at + HD]
                        )
                    at = first % per_out
                    own_outs[first // per_out][at : at + rows, col : col + HD] = here.astype(
                        jnp.bfloat16
                    )
                first += rows


def project(chunks, place, member, gain, jobs, ready=None, keep=False):
    chunk_rows = tuple(chunk.shape[0] for chunk in chunks)
    rows = sum(chunk_rows)
    width = chunks[0].shape[1]
    columns = [job[0].shape[1] for job in jobs]
    rows_in = [ready] if ready is not None else list(chunks)
    operands = [*rows_in, gain, *(part for job in jobs for part in job[:3])]
    vmem = pl.BlockSpec(memory_space=pltpu.VMEM)
    blocks = [job[4] for job in jobs]
    outs = [
        jax.ShapeDtypeStruct((rows // n, c), jnp.bfloat16)
        for n, c in zip(blocks, columns)
        for _ in range(n)
    ]
    normed = (rows, width)
    scratch = []
    if keep:
        outs.append(jax.ShapeDtypeStruct(normed, jnp.bfloat16))
    elif ready is None:
        scratch.append(pltpu.VMEM(normed, jnp.bfloat16))
    return pl.pallas_call(
        functools.partial(
            project_kernel,
            chunk_rows,
            [job[3] for job in jobs],
            blocks,
            place,
            ready is not None,
        ),
        out_shape=outs,
        in_specs=[pl.BlockSpec(memory_space=pltpu.SMEM)] + [vmem] * len(operands),
        out_specs=[vmem] * len(outs),
        scratch_shapes=scratch,
        compiler_params=pltpu.CompilerParams(vmem_limit_bytes=VMEM_LIMIT),
        cost_estimate=pl.CostEstimate(flops=10000000000, bytes_accessed=1000, transcendentals=0),
        name="project",
    )(member, *operands)


def attend_kernel(chunk_rows, n, place, member, *refs):
    starts = place(member[0])
    q_refs, kv_refs, (out, q_all, kv_all, keys_t, scores) = refs[:n], refs[n:-5], refs[-5:]
    count, columns = out.shape
    heads = columns // HD
    tile = scores.shape[0] // heads
    for sources, target in ((q_refs, q_all), (kv_refs, kv_all)):
        i = 0
        for source in sources:
            first = 0
            while first < source.shape[0]:
                rows = chunk_rows[i]
                where = pl.ds(pl.multiple_of(starts[i], rows), rows)
                target[where, :] = source[first : first + rows, :]
                first += rows
                i += 1
    keys_t[...] = kv_all[:, :HD].astype(jnp.float32).T.astype(jnp.bfloat16)
    scale = HD ** (-0.5) * LOG2E
    row = lax.broadcasted_iota(jnp.int32, (tile, tile), 0)
    col = lax.broadcasted_iota(jnp.int32, (tile, tile), 1)
    triangle = row >= col
    for low in range(0, count, tile):
        top = low + tile
        query = jnp.concatenate(
            [q_all[low:top, h * HD : (h + 1) * HD] for h in range(heads)], axis=0
        )
        scores[:, :top] = jnp.dot(query, keys_t[:, :top], preferred_element_type=jnp.float32)
        for h in range(heads):
            mine = slice(h * tile, (h + 1) * tile)
            edge = jnp.where(triangle, scores[mine, low:top], MASKED)
            highest = jnp.max(edge, axis=1, keepdims=True)
            if low:
                body = scores[mine, :low]
                highest = jnp.maximum(highest, jnp.max(body, axis=1, keepdims=True))
                body = jnp.exp2((body - highest) * scale)
            edge = jnp.exp2((edge - highest) * scale)
            total = jnp.sum(edge, axis=1, keepdims=True)
            if low:
                total = total + jnp.sum(body, axis=1, keepdims=True)
            share = 1.0 / total
            mixed = jnp.dot(
                (edge * share).astype(jnp.bfloat16),
                kv_all[low:top, HD:],
                preferred_element_type=jnp.float32,
            )
            if low:
                mixed = mixed + jnp.dot(
                    (body * share).astype(jnp.bfloat16),
                    kv_all[:low, HD:],
                    preferred_element_type=jnp.float32,
                )
            out[low:top, h * HD : (h + 1) * HD] = mixed.astype(jnp.bfloat16)


def attend(queries, kvs, chunk_rows, place, member):
    count = sum(chunk_rows)
    q_width = queries[0].shape[1]
    tile = min(256, count)
    vmem = pl.BlockSpec(memory_space=pltpu.VMEM)
    return pl.pallas_call(
        functools.partial(
            attend_kernel, tuple(chunk_rows), len(queries), place
        ),
        out_shape=jax.ShapeDtypeStruct((count, q_width), jnp.bfloat16),
        in_specs=[pl.BlockSpec(memory_space=pltpu.SMEM)] + [vmem] * (len(queries) + len(kvs)),
        out_specs=vmem,
        scratch_shapes=[
            pltpu.VMEM((count, q_width), jnp.bfloat16),
            pltpu.VMEM((count, 2 * HD), jnp.bfloat16),
            pltpu.VMEM((HD, count), jnp.bfloat16),
            pltpu.VMEM((tile * (q_width // HD), count), jnp.float32),
        ],
        compiler_params=pltpu.CompilerParams(vmem_limit_bytes=VMEM_LIMIT),
        cost_estimate=pl.CostEstimate(flops=5000000000, bytes_accessed=1000, transcendentals=0),
        name="attend",
    )(member, *queries, *kvs)


def decode_prepare_kernel(tables, lengths, slots, query_ref, queries, allowed, limits):
    rows, pages = tables.shape
    handed = slots.shape[1]
    page = allowed.shape[0] // handed
    columns = queries.shape[1]
    per_head = columns // KVH
    lane = lax.broadcasted_iota(jnp.int32, (1, columns), 1)
    lane_row = lane % rows

    limits[...] = jnp.zeros_like(limits)

    def one_entry(e, owners):
        for r in range(rows):
            at = tables[r, e]
            count = jnp.clip(lengths[r] - e * page, 0, page)
            for j in range(handed):
                taken = slots[0, j] == at
                count = jnp.where(taken, 0, count)
                owners = owners[:j] + (jnp.where(taken, r, owners[j]),) + owners[j + 1 :]
            limits[pl.ds(at, 1), :] = jnp.where(lane_row == r, count, 0)
        return owners

    owners = lax.fori_loop(0, pages, one_entry, (jnp.int32(-1),) * handed)
    for j in range(handed):
        allowed[j * page : (j + 1) * page, :] = jnp.broadcast_to(
            jnp.where(lane_row == owners[j], 1.0, 0.0), (page, columns)
        )

    stacked = jnp.concatenate(
        [query_ref[:, i * HD : (i + 1) * HD].astype(jnp.float32) for i in range(KVH * GROUP)],
        axis=0,
    )
    turned_q = stacked.T.astype(jnp.bfloat16)
    for h in range(KVH):
        queries[2 * h * HD : (2 * h + 1) * HD, :] = jnp.where(
            lane // per_head == h, turned_q, jnp.zeros_like(turned_q)
        )
        queries[(2 * h + 1) * HD : (2 * h + 2) * HD, :] = jnp.zeros((HD, columns), jnp.bfloat16)


def decode_prepare(pool, tables, lengths, slots, queries):
    rows = tables.shape[0]
    columns = KVH * GROUP * rows
    total_pages, page, width = pool.shape
    vmem = pl.BlockSpec(memory_space=pltpu.VMEM)
    smem = pl.BlockSpec(memory_space=pltpu.SMEM)
    return pl.pallas_call(
        decode_prepare_kernel,
        out_shape=[
            jax.ShapeDtypeStruct((width, columns), jnp.bfloat16),
            jax.ShapeDtypeStruct((slots.shape[1] * page, columns), jnp.float32),
            jax.ShapeDtypeStruct((total_pages, columns), jnp.int32),
        ],
        in_specs=[smem, smem, smem, vmem],
        out_specs=[vmem] * 3,
        compiler_params=pltpu.CompilerParams(vmem_limit_bytes=VMEM_LIMIT),
        cost_estimate=pl.CostEstimate(flops=10**10, bytes_accessed=1000, transcendentals=0),
        name="decode_prepare",
    )(tables, lengths, slots, queries)


def decode_old_kernel(queries, limits, own_ref, pool, acc_ref, state_ref, scores, own):
    rows = own_ref.shape[0]
    total_pages, page, width = pool.shape
    columns = queries.shape[1]
    per_head = columns // KVH
    scale = HD ** (-0.5) * LOG2E
    lane_row = lax.broadcasted_iota(jnp.int32, (1, columns), 1) % rows

    own[...] = jnp.zeros_like(own)
    own[0:rows, :] = own_ref[...]
    own_score = jnp.dot(own[...], queries[...], preferred_element_type=jnp.float32)
    own_line = lax.broadcasted_iota(jnp.int32, own_score.shape, 0)
    own_score = jnp.where(own_line == lane_row, own_score, MASKED)
    highest = jnp.max(own_score, axis=0, keepdims=True)
    step = total_pages // 4
    line = lax.broadcasted_iota(jnp.int32, (step, page, columns), 1)
    for first in range(0, total_pages, step):
        score = jnp.dot(
            pool[first : first + step].reshape(step * page, width),
            queries[...],
            preferred_element_type=jnp.float32,
        ).reshape(step, page, columns)
        limit = limits[first : first + step, :].reshape(step, 1, columns)
        score = jnp.where(line < limit, score, MASKED)
        score = score.reshape(step * page, columns)
        scores[first * page : (first + step) * page, :] = score
        highest = jnp.maximum(highest, jnp.max(score, axis=0, keepdims=True))

    weight = jnp.exp2((own_score - highest) * scale)
    total = jnp.sum(weight, axis=0, keepdims=True)
    weight = weight.T.astype(jnp.bfloat16)
    mixed = [
        jnp.dot(
            weight[h * per_head : (h + 1) * per_head],
            own[:, (2 * h + 1) * HD : (2 * h + 2) * HD],
            preferred_element_type=jnp.float32,
        )
        for h in range(KVH)
    ]
    for first in range(0, total_pages, step):
        weight = jnp.exp2((scores[first * page : (first + step) * page, :] - highest) * scale)
        total = total + jnp.sum(weight, axis=0, keepdims=True)
        weight = weight.T.astype(jnp.bfloat16)
        for h in range(KVH):
            value = pool[first : first + step, :, (2 * h + 1) * HD : (2 * h + 2) * HD]
            mixed[h] = mixed[h] + jnp.dot(
                weight[h * per_head : (h + 1) * per_head],
                value.reshape(step * page, HD),
                preferred_element_type=jnp.float32,
            )
    for h in range(KVH):
        acc_ref[h] = mixed[h]
    state_ref[0:1, :] = highest
    state_ref[1:2, :] = total


def decode_old(pool, queries, limits, new_kv):
    rows = new_kv.shape[0]
    columns = queries.shape[1]
    total_pages, page, width = pool.shape
    vmem = pl.BlockSpec(memory_space=pltpu.VMEM)
    return pl.pallas_call(
        decode_old_kernel,
        out_shape=[
            jax.ShapeDtypeStruct((KVH, GROUP * rows, HD), jnp.float32),
            jax.ShapeDtypeStruct((2, columns), jnp.float32),
        ],
        in_specs=[vmem] * 4,
        out_specs=[vmem] * 2,
        scratch_shapes=[
            pltpu.VMEM((total_pages * page, columns), jnp.float32),
            pltpu.VMEM((page, width), jnp.bfloat16),
        ],
        compiler_params=pltpu.CompilerParams(vmem_limit_bytes=VMEM_LIMIT),
        cost_estimate=pl.CostEstimate(flops=5 * 10**9, bytes_accessed=1000, transcendentals=0),
        name="decode_old",
    )(queries, limits, new_kv, pool)


def decode_new_kernel(heads_of, member, q_ref, allowed_ref, acc_ref, state_ref, *refs):
    pieces, out, weights, keeps = refs[:-3], *refs[-3:]
    scale = HD ** (-0.5) * LOG2E
    columns = q_ref.shape[1]
    per_head = columns // KVH
    rows = out.shape[0]
    heads = heads_of(member[0])
    score = jnp.zeros((pieces[0].shape[0], columns), jnp.float32)
    for k in range(KVH):
        where = pl.ds(pl.multiple_of(heads[k] * 2 * HD, 2 * HD), 2 * HD)
        score = score + jnp.dot(pieces[k][...], q_ref[where, :], preferred_element_type=jnp.float32)
    score = jnp.where(allowed_ref[...] > 0.0, score, MASKED)
    before = state_ref[0:1, :]
    highest = jnp.maximum(before, jnp.max(score, axis=0, keepdims=True))
    keep = jnp.exp2((before - highest) * scale)
    weight = jnp.exp2((score - highest) * scale)
    share = 1.0 / (state_ref[1:2, :] * keep + jnp.sum(weight, axis=0, keepdims=True))
    weights[...] = (weight * share).T
    keeps[...] = jnp.broadcast_to(keep * share, (8, columns)).T
    for k in range(KVH):
        h = heads[k]
        mine = pl.ds(pl.multiple_of(h * per_head, per_head), per_head)
        mixed = acc_ref[h] * keeps[mine, 0:1] + jnp.dot(
            weights[mine, :].astype(jnp.bfloat16),
            pieces[k][:, HD:],
            preferred_element_type=jnp.float32,
        )
        for j in range(GROUP):
            lanes = pl.ds(pl.multiple_of((h * GROUP + j) * HD, HD), HD)
            out[:, lanes] = mixed[j * rows : (j + 1) * rows, :].astype(jnp.bfloat16)


def decode_new(pieces, heads_of, member, rows, acc, state, queries, allowed):
    vmem = pl.BlockSpec(memory_space=pltpu.VMEM)
    columns = queries.shape[1]
    return pl.pallas_call(
        functools.partial(decode_new_kernel, heads_of),
        out_shape=jax.ShapeDtypeStruct((rows, KVH * GROUP * HD), jnp.bfloat16),
        in_specs=[pl.BlockSpec(memory_space=pltpu.SMEM)] + [vmem] * (4 + len(pieces)),
        out_specs=vmem,
        scratch_shapes=[
            pltpu.VMEM((columns, pieces[0].shape[0]), jnp.float32),
            pltpu.VMEM((columns, 8), jnp.float32),
        ],
        compiler_params=pltpu.CompilerParams(vmem_limit_bytes=VMEM_LIMIT),
        name="decode_new",
    )(member, queries, allowed, acc, state, *pieces)


def exchange_plan(members, subs):
    def pairs(links):
        return [
            (source * subs + sub, target * subs + sub)
            for source, target in links
            for sub in range(subs)
        ]

    side = [(m, m ^ 1) for m in range(members)]
    outer = [(m, m ^ 2) for m in range(members)]
    outward = [(m, m ^ 2) for m in range(members) if m // 2 in (1, 2)]
    inner = [(m, m ^ 6) for m in range(members) if m // 2 in (1, 2)]
    return pairs(side), pairs(outer), pairs(outward), pairs(inner)


def local(
    stretch_tokens,
    norm_gain,
    q_weight,
    kv_weight,
    dec_query,
    dec_new_kv,
    kv_pool,
    page_table,
    cache_lengths,
    handoff_slot,
):
    devices_tp = lax.axis_size("tp")
    members = min(16, devices_tp)
    subs = devices_tp // members
    sub_bits = subs.bit_length() - 1
    member_bits = members.bit_length() - 1
    headmates = members // KVH
    position = lax.axis_index("tp")
    member = position // subs
    tokens = stretch_tokens[0]
    block_rows, width = tokens.shape
    count = members * block_rows
    gain = norm_gain.reshape(1, width)

    member_ref = member.reshape(1).astype(jnp.int32)
    rows = page_table.shape[0]

    q_block = q_weight
    kv_block = kv_weight
    for bit in range(sub_bits):
        other_q = swapped(q_block, "tp", bit)
        other_kv = swapped(kv_block, "tp", bit)
        upper = position // 2**bit % 2
        q_block = ordered_pair(q_block, other_q, upper, 1)
        kv_block = ordered_pair(kv_block, other_kv, upper, 1)
    q_cos, q_sin = rotation_tables(count, HD, 0, False)
    kv_width = kv_block.shape[1]
    if kv_width % (2 * HD) == 0:
        kv_job = (kv_block, q_cos, q_sin, (True, False) * (kv_width // (2 * HD)), 1)
    else:
        kv_cos, kv_sin = rotation_tables(count, kv_width, member * kv_width, True)
        kv_job = (kv_block, kv_cos, kv_sin, (True,) * max(1, kv_width // HD), 1)
    q_job = (q_block, q_cos, q_sin, (True,) * (q_block.shape[1] // HD), 1)
    kv_pair = kv_job[:4] + (2,)
    bar = lax.optimization_barrier

    def prepared():
        return decode_prepare(kv_pool, page_table, cache_lengths, handoff_slot, dec_query)

    if members == 8 and headmates == 1 and block_rows % 32 == 0:
        half = block_rows // 2
        side, outer, outward, inner = exchange_plan(members, subs)

        def move(value, pairs):
            return lax.ppermute(value, "tp", pairs)

        row = member // 2
        at_end = (row == 0) | (row == 3)

        def place(offsets):
            return lambda m: [
                jnp.bitwise_xor(m, offset) * block_rows + c * half
                for offset in offsets
                for c in range(2)
            ]

        def hand(kv, offset):
            pairs = [
                (r * devices_tp + m * subs + s, (1 - r) * devices_tp + (m ^ offset) * subs + s)
                for r in range(2)
                for m in range(members)
                for s in range(subs)
            ]
            return lax.ppermute(kv, ("role", "tp"), pairs)

        own = [tokens[:half]]
        own.append(bar((tokens, own[0]))[0][half:])
        y, e1, e2 = {}, {}, {}
        for c in range(2):
            y[c] = move(own[c], side)
            e1[c] = move(own[c], outer)
            e2[c] = move(own[c], inner)
        dec_heads, allowed, limits = prepared()
        q0, kv0 = project([tokens], lambda m: [m * block_rows], member_ref, gain, [q_job, kv_job])
        piece = {0: hand(kv0, 0)}
        for c in range(2):
            e1[c], e2[c], y[c] = bar((e1[c], e2[c], y[c]))
            e1[2 + c] = move(e2[c], outward)
            e2[2 + c] = move(e1[c], inner)
            y[2 + c] = move(e1[c], side)
        qa, kv2, kv1 = project(
            [e1[0], e1[1], y[0], y[1]], place((2, 1)), member_ref, gain, [q_job, kv_pair]
        )
        piece[2], piece[1] = hand(kv2, 2), hand(kv1, 1)
        two, three = {}, {}
        for c in range(2):
            e1[2 + c], e2[2 + c], y[2 + c] = bar((e1[2 + c], e2[2 + c], y[2 + c]))
            two[c] = jnp.where(at_end, e1[2 + c], e2[2 + c])
            e1[4 + c] = move(e2[2 + c], outward)
            y[4 + c] = move(two[c], side)
        qb, kv4, kv3 = project(
            [two[0], two[1], y[2], y[3]], place((4, 3)), member_ref, gain, [q_job, kv_pair]
        )
        piece[4], piece[3] = hand(kv4, 4), hand(kv3, 3)
        for c in range(2):
            e1[4 + c], y[4 + c] = bar((e1[4 + c], y[4 + c]))
            three[c] = jnp.where(at_end, e1[4 + c], e2[c])
            if c == 0:
                e1[6] = move(y[4], outer)
            else:
                y[6] = move(three[1], side)
        state = decode_old(kv_pool, dec_heads, limits, dec_new_kv)
        qc, kv6, kv5 = project(
            [three[0], three[1], y[4], y[5]], place((6, 5)), member_ref, gain, [q_job, kv_pair]
        )
        piece[6], piece[5] = hand(kv6, 6), hand(kv5, 5)
        last = [e1[6], y[6]]
        kv7, normed = project(last, place((7,)), member_ref, gain, [kv_job], keep=True)
        piece[7] = hand(kv7, 7)
        (qd,) = project(last, place((7,)), member_ref, gain, [q_job], ready=normed)
        context = attend(
            [q0, qa, qb, qc, qd],
            [kv0, kv2, kv1, kv4, kv3, kv6, kv5, kv7],
            [half] * (2 * members),
            place((0, 2, 1, 4, 3, 6, 5, 7)),
            member_ref,
        )
        pieces = [piece[k] for k in range(members)]
        heads_of = lambda m: [jnp.bitwise_xor(m, k) for k in range(members)]
    else:
        dec_heads, allowed, limits = prepared()
        state = decode_old(kv_pool, dec_heads, limits, dec_new_kv)
        moving = tokens
        queries, local_kvs, order = [], [], []
        group, group_steps = [tokens], [0]
        for step in range(members):
            if step:
                moving = from_behind(moving, "tp", subs)
                group.append(moving)
                group_steps.append(step)
            if len(group) == min(4, members) or step == members - 1:
                place = lambda m, steps=tuple(group_steps): [
                    jnp.bitwise_and(m - back, members - 1) * block_rows for back in steps
                ]
                q_part, kv_part = project(group, place, member_ref, gain, [q_job, kv_job])
                queries.append(q_part)
                local_kvs.append(kv_part)
                order += [(member - back) % members for back in group_steps]
                group, group_steps = [], []
        arrived_kv = jnp.concatenate(local_kvs, axis=0).reshape(members, block_rows, kv_width)
        local_kv = arrived_kv[jnp.argsort(jnp.stack(order))].reshape(count, kv_width)
        head_kv = local_kv
        for step in range(headmates.bit_length() - 1):
            other = swapped(head_kv, "tp", sub_bits + step)
            head_kv = ordered_pair(head_kv, other, member // 2**step % 2, 1)
        arrived_q = jnp.concatenate(queries, axis=0).reshape(members, block_rows, -1)
        all_q = arrived_q[jnp.argsort(jnp.stack(order))].reshape(count, -1)
        context = attend([all_q], [head_kv], [count], lambda m: [0], member_ref)
        crossed = swapped(local_kv, "role", 0)
        received = spread_members(
            crossed.reshape(members, block_rows, kv_width),
            member,
            sub_bits,
            member_bits,
            lambda part, bit: swapped(part, "tp", bit),
        )
        arrived = jnp.transpose(received, (1, 0, 2)).reshape(block_rows, members * kv_width)
        pieces = [arrived[:, k * 2 * HD : (k + 1) * 2 * HD] for k in range(KVH)]
        heads_of = lambda m: list(range(KVH))

    decoded = decode_new(pieces, heads_of, member_ref, rows, *state, dec_heads, allowed)
    return (context[None], decoded)


def solution(mesh):
    in_specs = (
        P("role", ("grp", "tp"), None),
        P(),
        P(None, "tp"),
        P(None, "tp"),
        P(("grp", "role", "tp"), None),
        P(("grp", "role", "tp"), None),
        P(("grp", "role", "tp"), None, None),
        P(("grp", "role", "tp"), None),
        P(("grp", "role", "tp")),
        P(("grp", "role", "tp"), None),
    )
    out_specs = (P("role", "grp", "tp"), P(("grp", "role", "tp"), None))
    return jax.shard_map(local, mesh=mesh, in_specs=in_specs, out_specs=out_specs, check_vma=False)
```

```python
import functools

import jax
import jax.numpy as jnp
from jax import lax
from jax.experimental import pallas as pl
from jax.experimental.pallas import tpu as pltpu
from jax.sharding import PartitionSpec as P

KVH = 8
HD = 128
GROUP = 8
MASKED = -1e30

norm_eps = 1e-05
rope_base = 500000.0


LOG2E = 1.4426950408889634
VMEM_LIMIT = 14 * 2**20


def swapped(value, axis, bit):
    mask = 2**bit
    pairs = [(source, source ^ mask) for source in range(lax.axis_size(axis))]
    return lax.ppermute(value, axis, pairs)


def from_behind(value, axis, steps):
    count = lax.axis_size(axis)
    pairs = [(source, (source + steps) % count) for source in range(count)]
    return lax.ppermute(value, axis, pairs)


def ordered_pair(mine, other, upper, axis):
    first = jnp.where(upper == 1, other, mine)
    second = jnp.where(upper == 1, mine, other)
    return jnp.concatenate((first, second), axis=axis)


def spread_members(blocks, member, low_bit, member_bits, mover):
    members = blocks.shape[0]
    order = jnp.bitwise_xor(member, jnp.arange(members))
    buffer = blocks[order]
    for step in range(member_bits):
        width = 2**step
        view = buffer.reshape(members // (2 * width), 2, width, blocks.shape[1], blocks.shape[2])
        arrived = mover(view[:, 1], low_bit + step)
        buffer = jnp.stack((view[:, 0], arrived), axis=1).reshape(blocks.shape)
    return buffer[order]


def rotation_tables(count, width, first_col, only_keys):
    columns = first_col + jnp.arange(width)
    pair_index = columns % HD // 2
    inverse = jnp.exp(
        -(2.0 * pair_index.astype(jnp.float32) / HD) * jnp.log(jnp.float32(rope_base))
    )
    angle = jnp.arange(count).astype(jnp.float32)[:, None] * inverse[None, :]
    cosine = jnp.cos(angle)
    sine = jnp.where(columns % 2 == 0, -1.0, 1.0)[None, :] * jnp.sin(angle)
    if only_keys:
        is_key = (columns % (2 * HD) < HD)[None, :]
        cosine = jnp.where(is_key, cosine, 1.0)
        sine = jnp.where(is_key, sine, 0.0)
    return cosine, sine


def turned(tile, cosine, sine):
    lane = lax.broadcasted_iota(jnp.int32, tile.shape, 1)
    after = pltpu.roll(tile, HD - 1, 1)
    before = pltpu.roll(tile, 1, 1)
    return tile * cosine + jnp.where(lane % 2 == 0, after, before) * sine


def normalize(x_refs, chunk_rows, gain, normed):
    width = normed.shape[1]
    part = 512
    first = 0
    for x_ref, rows in zip(x_refs, chunk_rows):

        def add(i, total, x_ref=x_ref):
            tile = x_ref[:, pl.ds(pl.multiple_of(i * part, part), part)].astype(jnp.float32)
            tile = tile * tile
            sums = [tile[:, col : col + 128] for col in range(0, part, 128)]
            return total + ((sums[0] + sums[1]) + (sums[2] + sums[3]))

        total = lax.fori_loop(
            0, width // part, add, jnp.zeros((rows, 128), jnp.float32), unroll=4
        )
        mean_sq = jnp.sum(total, axis=1, keepdims=True) / width
        scale = jnp.broadcast_to(lax.rsqrt(mean_sq + norm_eps), (rows, part))

        def write(i, carry, x_ref=x_ref, rows=rows, first=first, scale=scale):
            here = pl.ds(pl.multiple_of(i * part, part), part)
            normed[first : first + rows, here] = (
                x_ref[:, here].astype(jnp.float32) * scale * gain[:, here].astype(jnp.float32)
            ).astype(jnp.bfloat16)
            return carry

        lax.fori_loop(0, width // part, write, 0, unroll=4)
        first += rows


def project_kernel(chunk_rows, rotated, blocks, place, ready, member, *refs):
    jobs = len(rotated)
    n = 1 if ready else len(chunk_rows)
    x_refs, gain = refs[:n], refs[n]
    job_refs = refs[n + 1 : n + 1 + 3 * jobs]
    outs = refs[n + 1 + 3 * jobs :]
    starts = place(member[0])
    if ready:
        normed = x_refs[0]
    else:
        normed = refs[-1]
        normalize(x_refs, chunk_rows, gain, normed)
    for j in range(jobs):
        weight, cos_ref, sin_ref = job_refs[3 * j : 3 * j + 3]
        table = cos_ref.shape[1]
        columns = weight.shape[1]
        tile = min(256, columns)
        own_outs, outs = outs[: blocks[j]], outs[blocks[j] :]
        per_out = sum(chunk_rows) // blocks[j]
        for low in range(0, columns, tile):
            product = jnp.dot(
                normed[...], weight[:, low : low + tile], preferred_element_type=jnp.float32
            )
            first = 0
            for i, rows in enumerate(chunk_rows):
                where = pl.ds(pl.multiple_of(starts[i], rows), rows)
                for col in range(low, low + tile, HD):
                    here = product[first : first + rows, col - low : col - low + HD]
                    if rotated[j][col // HD]:
                        at = col % table
                        here = turned(
                            here, cos_ref[where, at : at + HD], sin_ref[where, at : at + HD]
                        )
                    at = first % per_out
                    own_outs[first // per_out][at : at + rows, col : col + HD] = here.astype(
                        jnp.bfloat16
                    )
                first += rows


def project(chunks, place, member, gain, jobs, ready=None, keep=False):
    chunk_rows = tuple(chunk.shape[0] for chunk in chunks)
    rows = sum(chunk_rows)
    width = chunks[0].shape[1]
    columns = [job[0].shape[1] for job in jobs]
    rows_in = [ready] if ready is not None else list(chunks)
    operands = [*rows_in, gain, *(part for job in jobs for part in job[:3])]
    vmem = pl.BlockSpec(memory_space=pltpu.VMEM)
    blocks = [job[4] for job in jobs]
    outs = [
        jax.ShapeDtypeStruct((rows // n, c), jnp.bfloat16)
        for n, c in zip(blocks, columns)
        for _ in range(n)
    ]
    normed = (rows, width)
    scratch = []
    if keep:
        outs.append(jax.ShapeDtypeStruct(normed, jnp.bfloat16))
    elif ready is None:
        scratch.append(pltpu.VMEM(normed, jnp.bfloat16))
    return pl.pallas_call(
        functools.partial(
            project_kernel,
            chunk_rows,
            [job[3] for job in jobs],
            blocks,
            place,
            ready is not None,
        ),
        out_shape=outs,
        in_specs=[pl.BlockSpec(memory_space=pltpu.SMEM)] + [vmem] * len(operands),
        out_specs=[vmem] * len(outs),
        scratch_shapes=scratch,
        compiler_params=pltpu.CompilerParams(vmem_limit_bytes=VMEM_LIMIT),
        cost_estimate=pl.CostEstimate(flops=10000000000, bytes_accessed=1000, transcendentals=0),
        name="project",
    )(member, *operands)


def attend_kernel(chunk_rows, n, place, member, *refs):
    starts = place(member[0])
    q_refs, kv_refs, (out, q_all, kv_all, keys_t, scores) = refs[:n], refs[n:-5], refs[-5:]
    count, columns = out.shape
    heads = columns // HD
    tile = scores.shape[0] // heads
    for sources, target in ((q_refs, q_all), (kv_refs, kv_all)):
        i = 0
        for source in sources:
            first = 0
            while first < source.shape[0]:
                rows = chunk_rows[i]
                where = pl.ds(pl.multiple_of(starts[i], rows), rows)
                target[where, :] = source[first : first + rows, :]
                first += rows
                i += 1
    keys_t[...] = kv_all[:, :HD].astype(jnp.float32).T.astype(jnp.bfloat16)
    scale = HD ** (-0.5) * LOG2E
    row = lax.broadcasted_iota(jnp.int32, (tile, tile), 0)
    col = lax.broadcasted_iota(jnp.int32, (tile, tile), 1)
    triangle = row >= col
    for low in range(0, count, tile):
        top = low + tile
        query = jnp.concatenate(
            [q_all[low:top, h * HD : (h + 1) * HD] for h in range(heads)], axis=0
        )
        scores[:, :top] = jnp.dot(query, keys_t[:, :top], preferred_element_type=jnp.float32)
        for h in range(heads):
            mine = slice(h * tile, (h + 1) * tile)
            edge = jnp.where(triangle, scores[mine, low:top], MASKED)
            highest = jnp.max(edge, axis=1, keepdims=True)
            if low:
                body = scores[mine, :low]
                highest = jnp.maximum(highest, jnp.max(body, axis=1, keepdims=True))
                body = jnp.exp2((body - highest) * scale)
            edge = jnp.exp2((edge - highest) * scale)
            total = jnp.sum(edge, axis=1, keepdims=True)
            if low:
                total = total + jnp.sum(body, axis=1, keepdims=True)
            share = 1.0 / total
            mixed = jnp.dot(
                edge.astype(jnp.bfloat16),
                kv_all[low:top, HD:],
                preferred_element_type=jnp.float32,
            )
            if low:
                mixed = mixed + jnp.dot(
                    body.astype(jnp.bfloat16),
                    kv_all[:low, HD:],
                    preferred_element_type=jnp.float32,
                )
            out[low:top, h * HD : (h + 1) * HD] = (mixed * share).astype(jnp.bfloat16)


def attend(queries, kvs, chunk_rows, place, member):
    count = sum(chunk_rows)
    q_width = queries[0].shape[1]
    tile = min(256, count)
    vmem = pl.BlockSpec(memory_space=pltpu.VMEM)
    return pl.pallas_call(
        functools.partial(
            attend_kernel, tuple(chunk_rows), len(queries), place
        ),
        out_shape=jax.ShapeDtypeStruct((count, q_width), jnp.bfloat16),
        in_specs=[pl.BlockSpec(memory_space=pltpu.SMEM)] + [vmem] * (len(queries) + len(kvs)),
        out_specs=vmem,
        scratch_shapes=[
            pltpu.VMEM((count, q_width), jnp.bfloat16),
            pltpu.VMEM((count, 2 * HD), jnp.bfloat16),
            pltpu.VMEM((HD, count), jnp.bfloat16),
            pltpu.VMEM((tile * (q_width // HD), count), jnp.float32),
        ],
        compiler_params=pltpu.CompilerParams(vmem_limit_bytes=VMEM_LIMIT),
        cost_estimate=pl.CostEstimate(flops=5000000000, bytes_accessed=1000, transcendentals=0),
        name="attend",
    )(member, *queries, *kvs)


def decode_prepare_kernel(tables, lengths, slots, query_ref, queries, allowed, limits):
    rows, pages = tables.shape
    handed = slots.shape[1]
    page = allowed.shape[0] // handed
    columns = queries.shape[1]
    per_head = columns // KVH
    lane = lax.broadcasted_iota(jnp.int32, (1, columns), 1)
    lane_row = lane % rows

    limits[...] = jnp.zeros_like(limits)

    def one_entry(e, owners):
        for r in range(rows):
            at = tables[r, e]
            count = jnp.clip(lengths[r] - e * page, 0, page)
            for j in range(handed):
                taken = slots[0, j] == at
                count = jnp.where(taken, 0, count)
                owners = owners[:j] + (jnp.where(taken, r, owners[j]),) + owners[j + 1 :]
            limits[pl.ds(at, 1), :] = jnp.where(lane_row == r, count, 0)
        return owners

    owners = lax.fori_loop(0, pages, one_entry, (jnp.int32(-1),) * handed)
    for j in range(handed):
        allowed[j * page : (j + 1) * page, :] = jnp.broadcast_to(
            jnp.where(lane_row == owners[j], 1.0, 0.0), (page, columns)
        )

    stacked = jnp.concatenate(
        [query_ref[:, i * HD : (i + 1) * HD].astype(jnp.float32) for i in range(KVH * GROUP)],
        axis=0,
    )
    turned_q = stacked.T.astype(jnp.bfloat16)
    for h in range(KVH):
        queries[2 * h * HD : (2 * h + 1) * HD, :] = jnp.where(
            lane // per_head == h, turned_q, jnp.zeros_like(turned_q)
        )
        queries[(2 * h + 1) * HD : (2 * h + 2) * HD, :] = jnp.zeros((HD, columns), jnp.bfloat16)


def decode_prepare(pool, tables, lengths, slots, queries):
    rows = tables.shape[0]
    columns = KVH * GROUP * rows
    total_pages, page, width = pool.shape
    vmem = pl.BlockSpec(memory_space=pltpu.VMEM)
    smem = pl.BlockSpec(memory_space=pltpu.SMEM)
    return pl.pallas_call(
        decode_prepare_kernel,
        out_shape=[
            jax.ShapeDtypeStruct((width, columns), jnp.bfloat16),
            jax.ShapeDtypeStruct((slots.shape[1] * page, columns), jnp.float32),
            jax.ShapeDtypeStruct((total_pages, columns), jnp.int32),
        ],
        in_specs=[smem, smem, smem, vmem],
        out_specs=[vmem] * 3,
        compiler_params=pltpu.CompilerParams(vmem_limit_bytes=VMEM_LIMIT),
        cost_estimate=pl.CostEstimate(flops=10**10, bytes_accessed=1000, transcendentals=0),
        name="decode_prepare",
    )(tables, lengths, slots, queries)


def decode_old_kernel(queries, limits, own_ref, pool, acc_ref, state_ref, scores, own):
    rows = own_ref.shape[0]
    total_pages, page, width = pool.shape
    columns = queries.shape[1]
    per_head = columns // KVH
    scale = HD ** (-0.5) * LOG2E
    lane_row = lax.broadcasted_iota(jnp.int32, (1, columns), 1) % rows

    own[...] = jnp.zeros_like(own)
    own[0:rows, :] = own_ref[...]
    own_score = jnp.dot(own[...], queries[...], preferred_element_type=jnp.float32)
    own_line = lax.broadcasted_iota(jnp.int32, own_score.shape, 0)
    own_score = jnp.where(own_line == lane_row, own_score, MASKED)
    highest = jnp.max(own_score, axis=0, keepdims=True)
    step = total_pages // 4
    line = lax.broadcasted_iota(jnp.int32, (step, page, columns), 1)
    for first in range(0, total_pages, step):
        score = jnp.dot(
            pool[first : first + step].reshape(step * page, width),
            queries[...],
            preferred_element_type=jnp.float32,
        ).reshape(step, page, columns)
        limit = limits[first : first + step, :].reshape(step, 1, columns)
        score = jnp.where(line < limit, score, MASKED)
        score = score.reshape(step * page, columns)
        scores[first * page : (first + step) * page, :] = score
        highest = jnp.maximum(highest, jnp.max(score, axis=0, keepdims=True))

    weight = jnp.exp2((own_score - highest) * scale)
    total = jnp.sum(weight, axis=0, keepdims=True)
    weight = weight.T.astype(jnp.bfloat16)
    mixed = [
        jnp.dot(
            weight[h * per_head : (h + 1) * per_head],
            own[:, (2 * h + 1) * HD : (2 * h + 2) * HD],
            preferred_element_type=jnp.float32,
        )
        for h in range(KVH)
    ]
    for first in range(0, total_pages, step):
        weight = jnp.exp2((scores[first * page : (first + step) * page, :] - highest) * scale)
        total = total + jnp.sum(weight, axis=0, keepdims=True)
        weight = weight.T.astype(jnp.bfloat16)
        for h in range(KVH):
            value = pool[first : first + step, :, (2 * h + 1) * HD : (2 * h + 2) * HD]
            mixed[h] = mixed[h] + jnp.dot(
                weight[h * per_head : (h + 1) * per_head],
                value.reshape(step * page, HD),
                preferred_element_type=jnp.float32,
            )
    for h in range(KVH):
        acc_ref[h] = mixed[h]
    state_ref[0:1, :] = highest
    state_ref[1:2, :] = total


def decode_old(pool, queries, limits, new_kv):
    rows = new_kv.shape[0]
    columns = queries.shape[1]
    total_pages, page, width = pool.shape
    vmem = pl.BlockSpec(memory_space=pltpu.VMEM)
    return pl.pallas_call(
        decode_old_kernel,
        out_shape=[
            jax.ShapeDtypeStruct((KVH, GROUP * rows, HD), jnp.float32),
            jax.ShapeDtypeStruct((2, columns), jnp.float32),
        ],
        in_specs=[vmem] * 4,
        out_specs=[vmem] * 2,
        scratch_shapes=[
            pltpu.VMEM((total_pages * page, columns), jnp.float32),
            pltpu.VMEM((page, width), jnp.bfloat16),
        ],
        compiler_params=pltpu.CompilerParams(vmem_limit_bytes=VMEM_LIMIT),
        cost_estimate=pl.CostEstimate(flops=5 * 10**9, bytes_accessed=1000, transcendentals=0),
        name="decode_old",
    )(queries, limits, new_kv, pool)


def decode_new_kernel(heads_of, member, q_ref, allowed_ref, acc_ref, state_ref, *refs):
    pieces, out, weights, keeps = refs[:-3], *refs[-3:]
    scale = HD ** (-0.5) * LOG2E
    columns = q_ref.shape[1]
    per_head = columns // KVH
    rows = out.shape[0]
    heads = heads_of(member[0])
    score = jnp.zeros((pieces[0].shape[0], columns), jnp.float32)
    for k in range(KVH):
        where = pl.ds(pl.multiple_of(heads[k] * 2 * HD, 2 * HD), 2 * HD)
        score = score + jnp.dot(pieces[k][...], q_ref[where, :], preferred_element_type=jnp.float32)
    score = jnp.where(allowed_ref[...] > 0.0, score, MASKED)
    before = state_ref[0:1, :]
    highest = jnp.maximum(before, jnp.max(score, axis=0, keepdims=True))
    keep = jnp.exp2((before - highest) * scale)
    weight = jnp.exp2((score - highest) * scale)
    share = 1.0 / (state_ref[1:2, :] * keep + jnp.sum(weight, axis=0, keepdims=True))
    weights[...] = (weight * share).T
    keeps[...] = jnp.broadcast_to(keep * share, (8, columns)).T
    for k in range(KVH):
        h = heads[k]
        mine = pl.ds(pl.multiple_of(h * per_head, per_head), per_head)
        mixed = acc_ref[h] * keeps[mine, 0:1] + jnp.dot(
            weights[mine, :].astype(jnp.bfloat16),
            pieces[k][:, HD:],
            preferred_element_type=jnp.float32,
        )
        for j in range(GROUP):
            lanes = pl.ds(pl.multiple_of((h * GROUP + j) * HD, HD), HD)
            out[:, lanes] = mixed[j * rows : (j + 1) * rows, :].astype(jnp.bfloat16)


def decode_new(pieces, heads_of, member, rows, acc, state, queries, allowed):
    vmem = pl.BlockSpec(memory_space=pltpu.VMEM)
    columns = queries.shape[1]
    return pl.pallas_call(
        functools.partial(decode_new_kernel, heads_of),
        out_shape=jax.ShapeDtypeStruct((rows, KVH * GROUP * HD), jnp.bfloat16),
        in_specs=[pl.BlockSpec(memory_space=pltpu.SMEM)] + [vmem] * (4 + len(pieces)),
        out_specs=vmem,
        scratch_shapes=[
            pltpu.VMEM((columns, pieces[0].shape[0]), jnp.float32),
            pltpu.VMEM((columns, 8), jnp.float32),
        ],
        compiler_params=pltpu.CompilerParams(vmem_limit_bytes=VMEM_LIMIT),
        name="decode_new",
    )(member, queries, allowed, acc, state, *pieces)


def exchange_plan(members, subs):
    def pairs(links):
        return [
            (source * subs + sub, target * subs + sub)
            for source, target in links
            for sub in range(subs)
        ]

    side = [(m, m ^ 1) for m in range(members)]
    outer = [(m, m ^ 2) for m in range(members)]
    outward = [(m, m ^ 2) for m in range(members) if m // 2 in (1, 2)]
    inner = [(m, m ^ 6) for m in range(members) if m // 2 in (1, 2)]
    return pairs(side), pairs(outer), pairs(outward), pairs(inner)


def local(
    stretch_tokens,
    norm_gain,
    q_weight,
    kv_weight,
    dec_query,
    dec_new_kv,
    kv_pool,
    page_table,
    cache_lengths,
    handoff_slot,
):
    devices_tp = lax.axis_size("tp")
    members = min(16, devices_tp)
    subs = devices_tp // members
    sub_bits = subs.bit_length() - 1
    member_bits = members.bit_length() - 1
    headmates = members // KVH
    position = lax.axis_index("tp")
    member = position // subs
    tokens = stretch_tokens[0]
    block_rows, width = tokens.shape
    count = members * block_rows
    gain = norm_gain.reshape(1, width)

    member_ref = member.reshape(1).astype(jnp.int32)
    rows = page_table.shape[0]

    q_block = q_weight
    kv_block = kv_weight
    for bit in range(sub_bits):
        other_q = swapped(q_block, "tp", bit)
        other_kv = swapped(kv_block, "tp", bit)
        upper = position // 2**bit % 2
        q_block = ordered_pair(q_block, other_q, upper, 1)
        kv_block = ordered_pair(kv_block, other_kv, upper, 1)
    q_cos, q_sin = rotation_tables(count, HD, 0, False)
    kv_width = kv_block.shape[1]
    if kv_width % (2 * HD) == 0:
        kv_job = (kv_block, q_cos, q_sin, (True, False) * (kv_width // (2 * HD)), 1)
    else:
        kv_cos, kv_sin = rotation_tables(count, kv_width, member * kv_width, True)
        kv_job = (kv_block, kv_cos, kv_sin, (True,) * max(1, kv_width // HD), 1)
    q_job = (q_block, q_cos, q_sin, (True,) * (q_block.shape[1] // HD), 1)
    kv_pair = kv_job[:4] + (2,)
    bar = lax.optimization_barrier

    def prepared():
        return decode_prepare(kv_pool, page_table, cache_lengths, handoff_slot, dec_query)

    if members == 8 and headmates == 1 and block_rows % 64 == 0:
        half, quarter = block_rows // 2, block_rows // 4
        side, outer, outward, inner = exchange_plan(members, subs)

        def move(value, pairs):
            return lax.ppermute(value, "tp", pairs)

        row = member // 2
        at_end = (row == 0) | (row == 3)

        def place(*chunks):
            return lambda m: [
                jnp.bitwise_xor(m, offset) * block_rows + first for offset, first in chunks
            ]

        def hand(kv, offset):
            pairs = [
                (r * devices_tp + m * subs + s, (1 - r) * devices_tp + (m ^ offset) * subs + s)
                for r in range(2)
                for m in range(members)
                for s in range(subs)
            ]
            return lax.ppermute(kv, ("role", "tp"), pairs)

        own = [tokens[:half]]
        own.append(bar((tokens, own[0]))[0][half:])
        y, e1, e2 = {}, {}, {}
        y[0] = move(tokens, side)
        for c in range(2):
            e1[c] = move(own[c], outer)
            e2[c] = move(own[c], inner)
        dec_heads, allowed, limits = prepared()
        q0, kv0 = project([tokens], place((0, 0)), member_ref, gain, [q_job, kv_job])
        piece = {0: hand(kv0, 0)}
        for c in range(2):
            if c == 0:
                e1[0], e2[0] = bar((e1[0], e2[0]))
            else:
                e1[1], e2[1], y[0] = bar((e1[1], e2[1], y[0]))
            e1[2 + c] = move(e2[c], outward)
            e2[2 + c] = move(e1[c], inner)
            y[2 + c] = move(e1[c], side)
        qa, kv2, kv1 = project(
            [e1[0], e1[1], y[0]],
            place((2, 0), (2, half), (1, 0)),
            member_ref,
            gain,
            [q_job, kv_pair],
        )
        piece[2], piece[1] = hand(kv2, 2), hand(kv1, 1)
        two, three = {}, {}
        for c in range(2):
            e1[2 + c], e2[2 + c], y[2 + c] = bar((e1[2 + c], e2[2 + c], y[2 + c]))
            two[c] = jnp.where(at_end, e1[2 + c], e2[2 + c])
            if c == 0:
                e1[4] = move(e2[2], outward)
            else:
                e1["5a"] = move(e2[3][:quarter], outward)
                e1["5b"] = move(e2[3][quarter:], outward)
            y[4 + c] = move(two[c], side)
        qb, kv4, kv3 = project(
            [two[0], two[1], y[2], y[3]],
            place((4, 0), (4, half), (3, 0), (3, half)),
            member_ref,
            gain,
            [q_job, kv_pair],
        )
        piece[4], piece[3] = hand(kv4, 4), hand(kv3, 3)
        e1[4], y[4] = bar((e1[4], y[4]))
        three[0] = jnp.where(at_end, e1[4], e2[0])
        e1[6] = move(y[4], outer)
        three[1] = jnp.where(at_end, e1["5a"], e2[1][:quarter])
        y["6a"] = move(three[1], side)
        state = decode_old(kv_pool, dec_heads, limits, dec_new_kv)
        e1["5b"], y[5], three[1] = bar((e1["5b"], y[5], three[1]))
        three[2] = jnp.where(at_end, e1["5b"], e2[1][quarter:])
        y["6b"] = move(three[2], side)
        qc, kv6, kv5 = project(
            [three[0], three[1], three[2], y[4], y[5]],
            place((6, 0), (6, half), (6, half + quarter), (5, 0), (5, half)),
            member_ref,
            gain,
            [q_job, kv_pair],
        )
        piece[6], piece[5] = hand(kv6, 6), hand(kv5, 5)
        last = [e1[6], y["6a"], y["6b"]]
        last_place = place((7, 0), (7, half), (7, half + quarter))
        kv7, normed = project(last, last_place, member_ref, gain, [kv_job], keep=True)
        piece[7] = hand(kv7, 7)
        (qd,) = project(last, last_place, member_ref, gain, [q_job], ready=normed)
        context = attend(
            [q0, qa, qb, qc, qd],
            [kv0, kv2, kv1, kv4, kv3, kv6, kv5, kv7],
            [block_rows] * members,
            place(*((offset, 0) for offset in (0, 2, 1, 4, 3, 6, 5, 7))),
            member_ref,
        )
        pieces = [piece[k] for k in range(members)]
        heads_of = lambda m: [jnp.bitwise_xor(m, k) for k in range(members)]
    else:
        dec_heads, allowed, limits = prepared()
        state = decode_old(kv_pool, dec_heads, limits, dec_new_kv)
        moving = tokens
        queries, local_kvs, order = [], [], []
        group, group_steps = [tokens], [0]
        for step in range(members):
            if step:
                moving = from_behind(moving, "tp", subs)
                group.append(moving)
                group_steps.append(step)
            if len(group) == min(4, members) or step == members - 1:
                place = lambda m, steps=tuple(group_steps): [
                    jnp.bitwise_and(m - back, members - 1) * block_rows for back in steps
                ]
                q_part, kv_part = project(group, place, member_ref, gain, [q_job, kv_job])
                queries.append(q_part)
                local_kvs.append(kv_part)
                order += [(member - back) % members for back in group_steps]
                group, group_steps = [], []
        arrived_kv = jnp.concatenate(local_kvs, axis=0).reshape(members, block_rows, kv_width)
        local_kv = arrived_kv[jnp.argsort(jnp.stack(order))].reshape(count, kv_width)
        head_kv = local_kv
        for step in range(headmates.bit_length() - 1):
            other = swapped(head_kv, "tp", sub_bits + step)
            head_kv = ordered_pair(head_kv, other, member // 2**step % 2, 1)
        arrived_q = jnp.concatenate(queries, axis=0).reshape(members, block_rows, -1)
        all_q = arrived_q[jnp.argsort(jnp.stack(order))].reshape(count, -1)
        context = attend([all_q], [head_kv], [count], lambda m: [0], member_ref)
        crossed = swapped(local_kv, "role", 0)
        received = spread_members(
            crossed.reshape(members, block_rows, kv_width),
            member,
            sub_bits,
            member_bits,
            lambda part, bit: swapped(part, "tp", bit),
        )
        arrived = jnp.transpose(received, (1, 0, 2)).reshape(block_rows, members * kv_width)
        pieces = [arrived[:, k * 2 * HD : (k + 1) * 2 * HD] for k in range(KVH)]
        heads_of = lambda m: list(range(KVH))

    decoded = decode_new(pieces, heads_of, member_ref, rows, *state, dec_heads, allowed)
    return (context[None], decoded)


def solution(mesh):
    in_specs = (
        P("role", ("grp", "tp"), None),
        P(),
        P(None, "tp"),
        P(None, "tp"),
        P(("grp", "role", "tp"), None),
        P(("grp", "role", "tp"), None),
        P(("grp", "role", "tp"), None, None),
        P(("grp", "role", "tp"), None),
        P(("grp", "role", "tp")),
        P(("grp", "role", "tp"), None),
    )
    out_specs = (P("role", "grp", "tp"), P(("grp", "role", "tp"), None))
    return jax.shard_map(local, mesh=mesh, in_specs=in_specs, out_specs=out_specs, check_vma=False)
```

```python
import functools

import jax
import jax.numpy as jnp
from jax import lax
from jax.experimental import pallas as pl
from jax.experimental.pallas import tpu as pltpu
from jax.sharding import PartitionSpec as P

KVH = 8
HD = 128
GROUP = 8
MASKED = -1e30

norm_eps = 1e-05
rope_base = 500000.0


LOG2E = 1.4426950408889634
VMEM_LIMIT = 14 * 2**20


def swapped(value, axis, bit):
    mask = 2**bit
    pairs = [(source, source ^ mask) for source in range(lax.axis_size(axis))]
    return lax.ppermute(value, axis, pairs)


def from_behind(value, axis, steps):
    count = lax.axis_size(axis)
    pairs = [(source, (source + steps) % count) for source in range(count)]
    return lax.ppermute(value, axis, pairs)


def ordered_pair(mine, other, upper, axis):
    first = jnp.where(upper == 1, other, mine)
    second = jnp.where(upper == 1, mine, other)
    return jnp.concatenate((first, second), axis=axis)


def spread_members(blocks, member, low_bit, member_bits, mover):
    members = blocks.shape[0]
    order = jnp.bitwise_xor(member, jnp.arange(members))
    buffer = blocks[order]
    for step in range(member_bits):
        width = 2**step
        view = buffer.reshape(members // (2 * width), 2, width, blocks.shape[1], blocks.shape[2])
        arrived = mover(view[:, 1], low_bit + step)
        buffer = jnp.stack((view[:, 0], arrived), axis=1).reshape(blocks.shape)
    return buffer[order]


def rotation_tables(count, width, first_col, only_keys):
    columns = first_col + jnp.arange(width)
    pair_index = columns % HD // 2
    inverse = jnp.exp(
        -(2.0 * pair_index.astype(jnp.float32) / HD) * jnp.log(jnp.float32(rope_base))
    )
    angle = jnp.arange(count).astype(jnp.float32)[:, None] * inverse[None, :]
    cosine = jnp.cos(angle)
    sine = jnp.where(columns % 2 == 0, -1.0, 1.0)[None, :] * jnp.sin(angle)
    if only_keys:
        is_key = (columns % (2 * HD) < HD)[None, :]
        cosine = jnp.where(is_key, cosine, 1.0)
        sine = jnp.where(is_key, sine, 0.0)
    return cosine, sine


def turned(tile, cosine, sine):
    lane = lax.broadcasted_iota(jnp.int32, tile.shape, 1)
    after = pltpu.roll(tile, HD - 1, 1)
    before = pltpu.roll(tile, 1, 1)
    return tile * cosine + jnp.where(lane % 2 == 0, after, before) * sine


def normalize(x_refs, chunk_rows, gain, normed):
    width = normed.shape[1]
    part = 512
    first = 0
    for x_ref, rows in zip(x_refs, chunk_rows):

        def add(i, total, x_ref=x_ref):
            tile = x_ref[:, pl.ds(pl.multiple_of(i * part, part), part)].astype(jnp.float32)
            tile = tile * tile
            sums = [tile[:, col : col + 128] for col in range(0, part, 128)]
            return total + ((sums[0] + sums[1]) + (sums[2] + sums[3]))

        total = lax.fori_loop(
            0, width // part, add, jnp.zeros((rows, 128), jnp.float32), unroll=4
        )
        mean_sq = jnp.sum(total, axis=1, keepdims=True) / width
        scale = jnp.broadcast_to(lax.rsqrt(mean_sq + norm_eps), (rows, part))

        def write(i, carry, x_ref=x_ref, rows=rows, first=first, scale=scale):
            here = pl.ds(pl.multiple_of(i * part, part), part)
            normed[first : first + rows, here] = (
                x_ref[:, here].astype(jnp.float32) * scale * gain[:, here].astype(jnp.float32)
            ).astype(jnp.bfloat16)
            return carry

        lax.fori_loop(0, width // part, write, 0, unroll=4)
        first += rows


def project_kernel(chunk_rows, rotated, blocks, place, ready, member, *refs):
    jobs = len(rotated)
    n = 1 if ready else len(chunk_rows)
    x_refs, gain = refs[:n], refs[n]
    job_refs = refs[n + 1 : n + 1 + 3 * jobs]
    outs = refs[n + 1 + 3 * jobs :]
    starts = place(member[0])
    if ready:
        normed = x_refs[0]
    else:
        normed = refs[-1]
        normalize(x_refs, chunk_rows, gain, normed)
    for j in range(jobs):
        weight, cos_ref, sin_ref = job_refs[3 * j : 3 * j + 3]
        table = cos_ref.shape[1]
        columns = weight.shape[1]
        tile = min(256, columns)
        own_outs, outs = outs[: blocks[j]], outs[blocks[j] :]
        per_out = sum(chunk_rows) // blocks[j]
        for low in range(0, columns, tile):
            product = jnp.dot(
                normed[...], weight[:, low : low + tile], preferred_element_type=jnp.float32
            )
            first = 0
            for i, rows in enumerate(chunk_rows):
                where = pl.ds(pl.multiple_of(starts[i], rows), rows)
                for col in range(low, low + tile, HD):
                    here = product[first : first + rows, col - low : col - low + HD]
                    if rotated[j][col // HD]:
                        at = col % table
                        here = turned(
                            here, cos_ref[where, at : at + HD], sin_ref[where, at : at + HD]
                        )
                    at = first % per_out
                    own_outs[first // per_out][at : at + rows, col : col + HD] = here.astype(
                        jnp.bfloat16
                    )
                first += rows


def project(chunks, place, member, gain, jobs, ready=None, keep=False):
    chunk_rows = tuple(chunk.shape[0] for chunk in chunks)
    rows = sum(chunk_rows)
    width = chunks[0].shape[1]
    columns = [job[0].shape[1] for job in jobs]
    rows_in = [ready] if ready is not None else list(chunks)
    operands = [*rows_in, gain, *(part for job in jobs for part in job[:3])]
    vmem = pl.BlockSpec(memory_space=pltpu.VMEM)
    blocks = [job[4] for job in jobs]
    outs = [
        jax.ShapeDtypeStruct((rows // n, c), jnp.bfloat16)
        for n, c in zip(blocks, columns)
        for _ in range(n)
    ]
    normed = (rows, width)
    scratch = []
    if keep:
        outs.append(jax.ShapeDtypeStruct(normed, jnp.bfloat16))
    elif ready is None:
        scratch.append(pltpu.VMEM(normed, jnp.bfloat16))
    return pl.pallas_call(
        functools.partial(
            project_kernel,
            chunk_rows,
            [job[3] for job in jobs],
            blocks,
            place,
            ready is not None,
        ),
        out_shape=outs,
        in_specs=[pl.BlockSpec(memory_space=pltpu.SMEM)] + [vmem] * len(operands),
        out_specs=[vmem] * len(outs),
        scratch_shapes=scratch,
        compiler_params=pltpu.CompilerParams(vmem_limit_bytes=VMEM_LIMIT),
        cost_estimate=pl.CostEstimate(flops=10000000000, bytes_accessed=1000, transcendentals=0),
        name="project",
    )(member, *operands)


def attend_kernel(chunk_rows, n, place, member, *refs):
    starts = place(member[0])
    q_refs, kv_refs, (out, q_all, kv_all, keys_t, scores) = refs[:n], refs[n:-5], refs[-5:]
    count, columns = out.shape
    heads = columns // HD
    tile = scores.shape[0] // heads
    for sources, target in ((q_refs, q_all), (kv_refs, kv_all)):
        i = 0
        for source in sources:
            first = 0
            while first < source.shape[0]:
                rows = chunk_rows[i]
                where = pl.ds(pl.multiple_of(starts[i], rows), rows)
                target[where, :] = source[first : first + rows, :]
                first += rows
                i += 1
    keys_t[...] = kv_all[:, :HD].astype(jnp.float32).T.astype(jnp.bfloat16)
    scale = HD ** (-0.5) * LOG2E
    row = lax.broadcasted_iota(jnp.int32, (tile, tile), 0)
    col = lax.broadcasted_iota(jnp.int32, (tile, tile), 1)
    triangle = row >= col
    for low in range(0, count, tile):
        top = low + tile
        query = jnp.concatenate(
            [q_all[low:top, h * HD : (h + 1) * HD] for h in range(heads)], axis=0
        )
        scores[:, :top] = jnp.dot(query, keys_t[:, :top], preferred_element_type=jnp.float32)
        for h in range(heads):
            mine = slice(h * tile, (h + 1) * tile)
            edge = jnp.where(triangle, scores[mine, low:top], MASKED)
            highest = jnp.max(edge, axis=1, keepdims=True)
            if low:
                body = scores[mine, :low]
                highest = jnp.maximum(highest, jnp.max(body, axis=1, keepdims=True))
                body = jnp.exp2((body - highest) * scale)
            edge = jnp.exp2((edge - highest) * scale)
            total = jnp.sum(edge, axis=1, keepdims=True)
            if low:
                total = total + jnp.sum(body, axis=1, keepdims=True)
            share = 1.0 / total
            mixed = jnp.dot(
                edge.astype(jnp.bfloat16),
                kv_all[low:top, HD:],
                preferred_element_type=jnp.float32,
            )
            if low:
                mixed = mixed + jnp.dot(
                    body.astype(jnp.bfloat16),
                    kv_all[:low, HD:],
                    preferred_element_type=jnp.float32,
                )
            out[low:top, h * HD : (h + 1) * HD] = (mixed * share).astype(jnp.bfloat16)


def attend(queries, kvs, chunk_rows, place, member):
    count = sum(chunk_rows)
    q_width = queries[0].shape[1]
    tile = min(256, count)
    vmem = pl.BlockSpec(memory_space=pltpu.VMEM)
    return pl.pallas_call(
        functools.partial(
            attend_kernel, tuple(chunk_rows), len(queries), place
        ),
        out_shape=jax.ShapeDtypeStruct((count, q_width), jnp.bfloat16),
        in_specs=[pl.BlockSpec(memory_space=pltpu.SMEM)] + [vmem] * (len(queries) + len(kvs)),
        out_specs=vmem,
        scratch_shapes=[
            pltpu.VMEM((count, q_width), jnp.bfloat16),
            pltpu.VMEM((count, 2 * HD), jnp.bfloat16),
            pltpu.VMEM((HD, count), jnp.bfloat16),
            pltpu.VMEM((tile * (q_width // HD), count), jnp.float32),
        ],
        compiler_params=pltpu.CompilerParams(vmem_limit_bytes=VMEM_LIMIT),
        cost_estimate=pl.CostEstimate(flops=5000000000, bytes_accessed=1000, transcendentals=0),
        name="attend",
    )(member, *queries, *kvs)


def decode_prepare_kernel(tables, lengths, slots, query_ref, queries, allowed, limits):
    rows, pages = tables.shape
    handed = slots.shape[1]
    page = allowed.shape[0] // handed
    columns = queries.shape[1]
    per_head = columns // KVH
    lane = lax.broadcasted_iota(jnp.int32, (1, columns), 1)
    lane_row = lane % rows

    limits[...] = jnp.zeros_like(limits)

    def one_entry(e, owners):
        for r in range(rows):
            at = tables[r, e]
            count = jnp.clip(lengths[r] - e * page, 0, page)
            for j in range(handed):
                taken = slots[0, j] == at
                count = jnp.where(taken, 0, count)
                owners = owners[:j] + (jnp.where(taken, r, owners[j]),) + owners[j + 1 :]
            limits[pl.ds(at, 1), :] = jnp.where(lane_row == r, count, 0)
        return owners

    owners = lax.fori_loop(0, pages, one_entry, (jnp.int32(-1),) * handed)
    for j in range(handed):
        allowed[j * page : (j + 1) * page, :] = jnp.broadcast_to(
            jnp.where(lane_row == owners[j], 1.0, 0.0), (page, columns)
        )

    stacked = jnp.concatenate(
        [query_ref[:, i * HD : (i + 1) * HD].astype(jnp.float32) for i in range(KVH * GROUP)],
        axis=0,
    )
    turned_q = stacked.T.astype(jnp.bfloat16)
    for h in range(KVH):
        queries[2 * h * HD : (2 * h + 1) * HD, :] = jnp.where(
            lane // per_head == h, turned_q, jnp.zeros_like(turned_q)
        )
        queries[(2 * h + 1) * HD : (2 * h + 2) * HD, :] = jnp.zeros((HD, columns), jnp.bfloat16)


def decode_prepare(pool, tables, lengths, slots, queries):
    rows = tables.shape[0]
    columns = KVH * GROUP * rows
    total_pages, page, width = pool.shape
    vmem = pl.BlockSpec(memory_space=pltpu.VMEM)
    smem = pl.BlockSpec(memory_space=pltpu.SMEM)
    return pl.pallas_call(
        decode_prepare_kernel,
        out_shape=[
            jax.ShapeDtypeStruct((width, columns), jnp.bfloat16),
            jax.ShapeDtypeStruct((slots.shape[1] * page, columns), jnp.float32),
            jax.ShapeDtypeStruct((total_pages, columns), jnp.int32),
        ],
        in_specs=[smem, smem, smem, vmem],
        out_specs=[vmem] * 3,
        compiler_params=pltpu.CompilerParams(vmem_limit_bytes=VMEM_LIMIT),
        cost_estimate=pl.CostEstimate(flops=10**10, bytes_accessed=1000, transcendentals=0),
        name="decode_prepare",
    )(tables, lengths, slots, queries)


def decode_old_kernel(queries, limits, own_ref, pool, acc_ref, state_ref, scores, own):
    rows = own_ref.shape[0]
    total_pages, page, width = pool.shape
    columns = queries.shape[1]
    per_head = columns // KVH
    scale = HD ** (-0.5) * LOG2E
    lane_row = lax.broadcasted_iota(jnp.int32, (1, columns), 1) % rows

    own[...] = jnp.zeros_like(own)
    own[0:rows, :] = own_ref[...]
    own_score = jnp.dot(own[...], queries[...], preferred_element_type=jnp.float32)
    own_line = lax.broadcasted_iota(jnp.int32, own_score.shape, 0)
    own_score = jnp.where(own_line == lane_row, own_score, MASKED)
    highest = jnp.max(own_score, axis=0, keepdims=True)
    step = total_pages // 4
    line = lax.broadcasted_iota(jnp.int32, (step, page, columns), 1)
    for first in range(0, total_pages, step):
        score = jnp.dot(
            pool[first : first + step].reshape(step * page, width),
            queries[...],
            preferred_element_type=jnp.float32,
        ).reshape(step, page, columns)
        limit = limits[first : first + step, :].reshape(step, 1, columns)
        score = jnp.where(line < limit, score, MASKED)
        score = score.reshape(step * page, columns)
        scores[first * page : (first + step) * page, :] = score
        highest = jnp.maximum(highest, jnp.max(score, axis=0, keepdims=True))

    weight = jnp.exp2((own_score - highest) * scale)
    total = jnp.sum(weight, axis=0, keepdims=True)
    weight = weight.T.astype(jnp.bfloat16)
    mixed = [
        jnp.dot(
            weight[h * per_head : (h + 1) * per_head],
            own[:, (2 * h + 1) * HD : (2 * h + 2) * HD],
            preferred_element_type=jnp.float32,
        )
        for h in range(KVH)
    ]
    for first in range(0, total_pages, step):
        weight = jnp.exp2((scores[first * page : (first + step) * page, :] - highest) * scale)
        total = total + jnp.sum(weight, axis=0, keepdims=True)
        weight = weight.T.astype(jnp.bfloat16)
        for h in range(KVH):
            value = pool[first : first + step, :, (2 * h + 1) * HD : (2 * h + 2) * HD]
            mixed[h] = mixed[h] + jnp.dot(
                weight[h * per_head : (h + 1) * per_head],
                value.reshape(step * page, HD),
                preferred_element_type=jnp.float32,
            )
    for h in range(KVH):
        acc_ref[h] = mixed[h]
    state_ref[0:1, :] = highest
    state_ref[1:2, :] = total


def decode_old(pool, queries, limits, new_kv):
    rows = new_kv.shape[0]
    columns = queries.shape[1]
    total_pages, page, width = pool.shape
    vmem = pl.BlockSpec(memory_space=pltpu.VMEM)
    return pl.pallas_call(
        decode_old_kernel,
        out_shape=[
            jax.ShapeDtypeStruct((KVH, GROUP * rows, HD), jnp.float32),
            jax.ShapeDtypeStruct((2, columns), jnp.float32),
        ],
        in_specs=[vmem] * 4,
        out_specs=[vmem] * 2,
        scratch_shapes=[
            pltpu.VMEM((total_pages * page, columns), jnp.float32),
            pltpu.VMEM((page, width), jnp.bfloat16),
        ],
        compiler_params=pltpu.CompilerParams(vmem_limit_bytes=VMEM_LIMIT),
        cost_estimate=pl.CostEstimate(flops=5 * 10**9, bytes_accessed=1000, transcendentals=0),
        name="decode_old",
    )(queries, limits, new_kv, pool)


def decode_new_kernel(heads_of, member, q_ref, allowed_ref, acc_ref, state_ref, *refs):
    pieces, out, weights, keeps = refs[:-3], *refs[-3:]
    scale = HD ** (-0.5) * LOG2E
    columns = q_ref.shape[1]
    per_head = columns // KVH
    rows = out.shape[0]
    heads = heads_of(member[0])
    score = jnp.zeros((pieces[0].shape[0], columns), jnp.float32)
    for k in range(KVH):
        where = pl.ds(pl.multiple_of(heads[k] * 2 * HD, 2 * HD), 2 * HD)
        score = score + jnp.dot(pieces[k][...], q_ref[where, :], preferred_element_type=jnp.float32)
    score = jnp.where(allowed_ref[...] > 0.0, score, MASKED)
    before = state_ref[0:1, :]
    highest = jnp.maximum(before, jnp.max(score, axis=0, keepdims=True))
    keep = jnp.exp2((before - highest) * scale)
    weight = jnp.exp2((score - highest) * scale)
    share = 1.0 / (state_ref[1:2, :] * keep + jnp.sum(weight, axis=0, keepdims=True))
    weights[...] = (weight * share).T
    keeps[...] = jnp.broadcast_to(keep * share, (8, columns)).T
    for k in range(KVH):
        h = heads[k]
        mine = pl.ds(pl.multiple_of(h * per_head, per_head), per_head)
        mixed = acc_ref[h] * keeps[mine, 0:1] + jnp.dot(
            weights[mine, :].astype(jnp.bfloat16),
            pieces[k][:, HD:],
            preferred_element_type=jnp.float32,
        )
        for j in range(GROUP):
            lanes = pl.ds(pl.multiple_of((h * GROUP + j) * HD, HD), HD)
            out[:, lanes] = mixed[j * rows : (j + 1) * rows, :].astype(jnp.bfloat16)


def decode_new(pieces, heads_of, member, rows, acc, state, queries, allowed):
    vmem = pl.BlockSpec(memory_space=pltpu.VMEM)
    columns = queries.shape[1]
    return pl.pallas_call(
        functools.partial(decode_new_kernel, heads_of),
        out_shape=jax.ShapeDtypeStruct((rows, KVH * GROUP * HD), jnp.bfloat16),
        in_specs=[pl.BlockSpec(memory_space=pltpu.SMEM)] + [vmem] * (4 + len(pieces)),
        out_specs=vmem,
        scratch_shapes=[
            pltpu.VMEM((columns, pieces[0].shape[0]), jnp.float32),
            pltpu.VMEM((columns, 8), jnp.float32),
        ],
        compiler_params=pltpu.CompilerParams(vmem_limit_bytes=VMEM_LIMIT),
        name="decode_new",
    )(member, queries, allowed, acc, state, *pieces)


def exchange_plan(members, subs):
    def pairs(links):
        return [
            (source * subs + sub, target * subs + sub)
            for source, target in links
            for sub in range(subs)
        ]

    side = [(m, m ^ 1) for m in range(members)]
    outer = [(m, m ^ 2) for m in range(members)]
    outward = [(m, m ^ 2) for m in range(members) if m // 2 in (1, 2)]
    inner = [(m, m ^ 6) for m in range(members) if m // 2 in (1, 2)]
    return pairs(side), pairs(outer), pairs(outward), pairs(inner)


def local(
    stretch_tokens,
    norm_gain,
    q_weight,
    kv_weight,
    dec_query,
    dec_new_kv,
    kv_pool,
    page_table,
    cache_lengths,
    handoff_slot,
):
    devices_tp = lax.axis_size("tp")
    members = min(16, devices_tp)
    subs = devices_tp // members
    sub_bits = subs.bit_length() - 1
    member_bits = members.bit_length() - 1
    headmates = members // KVH
    position = lax.axis_index("tp")
    member = position // subs
    tokens = stretch_tokens[0]
    block_rows, width = tokens.shape
    count = members * block_rows
    gain = norm_gain.reshape(1, width)

    member_ref = member.reshape(1).astype(jnp.int32)
    rows = page_table.shape[0]

    q_block = q_weight
    kv_block = kv_weight
    for bit in range(sub_bits):
        other_q = swapped(q_block, "tp", bit)
        other_kv = swapped(kv_block, "tp", bit)
        upper = position // 2**bit % 2
        q_block = ordered_pair(q_block, other_q, upper, 1)
        kv_block = ordered_pair(kv_block, other_kv, upper, 1)
    q_cos, q_sin = rotation_tables(count, HD, 0, False)
    kv_width = kv_block.shape[1]
    if kv_width % (2 * HD) == 0:
        kv_job = (kv_block, q_cos, q_sin, (True, False) * (kv_width // (2 * HD)), 1)
    else:
        kv_cos, kv_sin = rotation_tables(count, kv_width, member * kv_width, True)
        kv_job = (kv_block, kv_cos, kv_sin, (True,) * max(1, kv_width // HD), 1)
    q_job = (q_block, q_cos, q_sin, (True,) * (q_block.shape[1] // HD), 1)
    kv_pair = kv_job[:4] + (2,)
    bar = lax.optimization_barrier

    def prepared():
        return decode_prepare(kv_pool, page_table, cache_lengths, handoff_slot, dec_query)

    if members == 8 and headmates == 1 and block_rows % 64 == 0:
        half, quarter = block_rows // 2, block_rows // 4
        side, outer, outward, inner = exchange_plan(members, subs)

        def move(value, pairs):
            return lax.ppermute(value, "tp", pairs)

        row = member // 2
        at_end = (row == 0) | (row == 3)

        def place(*chunks):
            return lambda m: [
                jnp.bitwise_xor(m, offset) * block_rows + first for offset, first in chunks
            ]

        def hand(kv, offset):
            pairs = [
                (r * devices_tp + m * subs + s, (1 - r) * devices_tp + (m ^ offset) * subs + s)
                for r in range(2)
                for m in range(members)
                for s in range(subs)
            ]
            return lax.ppermute(kv, ("role", "tp"), pairs)

        own = []
        for c in range(2):
            source = bar((tokens, own[0]))[0] if c else tokens
            own.append(source[c * half : (c + 1) * half])
        y, e1, e2 = {}, {}, {}
        y[0] = move(tokens, side)
        for c in range(2):
            e1[c] = move(own[c], outer)
            e2[c] = move(own[c], inner)
        dec_heads, allowed, limits = prepared()
        q0, kv0 = project([tokens], place((0, 0)), member_ref, gain, [q_job, kv_job])
        piece = {0: hand(kv0, 0)}
        for c in range(2):
            e1[2 + c] = move(e2[c], outward)
            e2[2 + c] = move(e1[c], inner)
            y[2 + c] = move(e1[c], side)
        qa, kv2, kv1 = project(
            [e1[0], e1[1], y[0]],
            place((2, 0), (2, half), (1, 0)),
            member_ref,
            gain,
            [q_job, kv_pair],
        )
        piece[2], piece[1] = hand(kv2, 2), hand(kv1, 1)
        two, three = {}, {}
        for c in range(2):
            two[c] = jnp.where(at_end, e1[2 + c], e2[2 + c])
            if c == 0:
                e1[4] = move(e2[2], outward)
            else:
                e1["5a"] = move(e2[3][:quarter], outward)
                e1["5b"] = move(e2[3][quarter:], outward)
            y[4 + c] = move(two[c], side)
        qb, kv4, kv3 = project(
            [two[0], two[1], y[2], y[3]],
            place((4, 0), (4, half), (3, 0), (3, half)),
            member_ref,
            gain,
            [q_job, kv_pair],
        )
        piece[4], piece[3] = hand(kv4, 4), hand(kv3, 3)
        three[0] = jnp.where(at_end, e1[4], e2[0])
        e1[6] = move(y[4], outer)
        three[1] = jnp.where(at_end, e1["5a"], e2[1][:quarter])
        y["6a"] = move(three[1], side)
        state = decode_old(kv_pool, dec_heads, limits, dec_new_kv)
        e1["5b"], three[1] = bar((e1["5b"], three[1]))
        three[2] = jnp.where(at_end, e1["5b"], e2[1][quarter:])
        y["6b"] = move(three[2], side)
        qc, kv6, kv5 = project(
            [three[0], three[1], three[2], y[4], y[5]],
            place((6, 0), (6, half), (6, half + quarter), (5, 0), (5, half)),
            member_ref,
            gain,
            [q_job, kv_pair],
        )
        piece[6], piece[5] = hand(kv6, 6), hand(kv5, 5)
        last = [e1[6], y["6a"], y["6b"]]
        last_place = place((7, 0), (7, half), (7, half + quarter))
        kv7, normed = project(last, last_place, member_ref, gain, [kv_job], keep=True)
        piece[7] = hand(kv7, 7)
        (qd,) = project(last, last_place, member_ref, gain, [q_job], ready=normed)
        context = attend(
            [q0, qa, qb, qc, qd],
            [kv0, kv2, kv1, kv4, kv3, kv6, kv5, kv7],
            [block_rows] * members,
            place(*((offset, 0) for offset in (0, 2, 1, 4, 3, 6, 5, 7))),
            member_ref,
        )
        pieces = [piece[k] for k in range(members)]
        heads_of = lambda m: [jnp.bitwise_xor(m, k) for k in range(members)]
    else:
        dec_heads, allowed, limits = prepared()
        state = decode_old(kv_pool, dec_heads, limits, dec_new_kv)
        moving = tokens
        queries, local_kvs, order = [], [], []
        group, group_steps = [tokens], [0]
        for step in range(members):
            if step:
                moving = from_behind(moving, "tp", subs)
                group.append(moving)
                group_steps.append(step)
            if len(group) == min(4, members) or step == members - 1:
                place = lambda m, steps=tuple(group_steps): [
                    jnp.bitwise_and(m - back, members - 1) * block_rows for back in steps
                ]
                q_part, kv_part = project(group, place, member_ref, gain, [q_job, kv_job])
                queries.append(q_part)
                local_kvs.append(kv_part)
                order += [(member - back) % members for back in group_steps]
                group, group_steps = [], []
        arrived_kv = jnp.concatenate(local_kvs, axis=0).reshape(members, block_rows, kv_width)
        local_kv = arrived_kv[jnp.argsort(jnp.stack(order))].reshape(count, kv_width)
        head_kv = local_kv
        for step in range(headmates.bit_length() - 1):
            other = swapped(head_kv, "tp", sub_bits + step)
            head_kv = ordered_pair(head_kv, other, member // 2**step % 2, 1)
        arrived_q = jnp.concatenate(queries, axis=0).reshape(members, block_rows, -1)
        all_q = arrived_q[jnp.argsort(jnp.stack(order))].reshape(count, -1)
        context = attend([all_q], [head_kv], [count], lambda m: [0], member_ref)
        crossed = swapped(local_kv, "role", 0)
        received = spread_members(
            crossed.reshape(members, block_rows, kv_width),
            member,
            sub_bits,
            member_bits,
            lambda part, bit: swapped(part, "tp", bit),
        )
        arrived = jnp.transpose(received, (1, 0, 2)).reshape(block_rows, members * kv_width)
        pieces = [arrived[:, k * 2 * HD : (k + 1) * 2 * HD] for k in range(KVH)]
        heads_of = lambda m: list(range(KVH))

    decoded = decode_new(pieces, heads_of, member_ref, rows, *state, dec_heads, allowed)
    return (context[None], decoded)


def solution(mesh):
    in_specs = (
        P("role", ("grp", "tp"), None),
        P(),
        P(None, "tp"),
        P(None, "tp"),
        P(("grp", "role", "tp"), None),
        P(("grp", "role", "tp"), None),
        P(("grp", "role", "tp"), None, None),
        P(("grp", "role", "tp"), None),
        P(("grp", "role", "tp")),
        P(("grp", "role", "tp"), None),
    )
    out_specs = (P("role", "grp", "tp"), P(("grp", "role", "tp"), None))
    return jax.shard_map(local, mesh=mesh, in_specs=in_specs, out_specs=out_specs, check_vma=False)
```

```python
import functools

import jax
import jax.numpy as jnp
from jax import lax
from jax.experimental import pallas as pl
from jax.experimental.pallas import tpu as pltpu
from jax.sharding import PartitionSpec as P

KVH = 8
HD = 128
GROUP = 8
MASKED = -1e30

norm_eps = 1e-05
rope_base = 500000.0


LOG2E = 1.4426950408889634
VMEM_LIMIT = 14 * 2**20


def swapped(value, axis, bit):
    mask = 2**bit
    pairs = [(source, source ^ mask) for source in range(lax.axis_size(axis))]
    return lax.ppermute(value, axis, pairs)


def from_behind(value, axis, steps):
    count = lax.axis_size(axis)
    pairs = [(source, (source + steps) % count) for source in range(count)]
    return lax.ppermute(value, axis, pairs)


def ordered_pair(mine, other, upper, axis):
    first = jnp.where(upper == 1, other, mine)
    second = jnp.where(upper == 1, mine, other)
    return jnp.concatenate((first, second), axis=axis)


def spread_members(blocks, member, low_bit, member_bits, mover):
    members = blocks.shape[0]
    order = jnp.bitwise_xor(member, jnp.arange(members))
    buffer = blocks[order]
    for step in range(member_bits):
        width = 2**step
        view = buffer.reshape(members // (2 * width), 2, width, blocks.shape[1], blocks.shape[2])
        arrived = mover(view[:, 1], low_bit + step)
        buffer = jnp.stack((view[:, 0], arrived), axis=1).reshape(blocks.shape)
    return buffer[order]


def rotation_tables(count, width, first_col, only_keys):
    columns = first_col + jnp.arange(width)
    pair_index = columns % HD // 2
    inverse = jnp.exp(
        -(2.0 * pair_index.astype(jnp.float32) / HD) * jnp.log(jnp.float32(rope_base))
    )
    angle = jnp.arange(count).astype(jnp.float32)[:, None] * inverse[None, :]
    cosine = jnp.cos(angle)
    sine = jnp.where(columns % 2 == 0, -1.0, 1.0)[None, :] * jnp.sin(angle)
    if only_keys:
        is_key = (columns % (2 * HD) < HD)[None, :]
        cosine = jnp.where(is_key, cosine, 1.0)
        sine = jnp.where(is_key, sine, 0.0)
    return cosine, sine


def turned(tile, cosine, sine):
    lane = lax.broadcasted_iota(jnp.int32, tile.shape, 1)
    after = pltpu.roll(tile, HD - 1, 1)
    before = pltpu.roll(tile, 1, 1)
    return tile * cosine + jnp.where(lane % 2 == 0, after, before) * sine


def normalize(x_refs, chunk_rows, gain, normed):
    width = normed.shape[1]
    part = 512
    first = 0
    for x_ref, rows in zip(x_refs, chunk_rows):

        def add(i, total, x_ref=x_ref):
            tile = x_ref[:, pl.ds(pl.multiple_of(i * part, part), part)].astype(jnp.float32)
            tile = tile * tile
            sums = [tile[:, col : col + 128] for col in range(0, part, 128)]
            return total + ((sums[0] + sums[1]) + (sums[2] + sums[3]))

        total = lax.fori_loop(
            0, width // part, add, jnp.zeros((rows, 128), jnp.float32), unroll=4
        )
        mean_sq = jnp.sum(total, axis=1, keepdims=True) / width
        scale = jnp.broadcast_to(lax.rsqrt(mean_sq + norm_eps), (rows, part))

        def write(i, carry, x_ref=x_ref, rows=rows, first=first, scale=scale):
            here = pl.ds(pl.multiple_of(i * part, part), part)
            normed[first : first + rows, here] = (
                x_ref[:, here].astype(jnp.float32) * scale * gain[:, here].astype(jnp.float32)
            ).astype(jnp.bfloat16)
            return carry

        lax.fori_loop(0, width // part, write, 0, unroll=4)
        first += rows


def project_kernel(chunk_rows, rotated, blocks, place, ready, member, *refs):
    jobs = len(rotated)
    n = 1 if ready else len(chunk_rows)
    x_refs, gain = refs[:n], refs[n]
    job_refs = refs[n + 1 : n + 1 + 3 * jobs]
    outs = refs[n + 1 + 3 * jobs :]
    starts = place(member[0])
    if ready:
        normed = x_refs[0]
    else:
        normed = refs[-1]
        normalize(x_refs, chunk_rows, gain, normed)
    for j in range(jobs):
        weight, cos_ref, sin_ref = job_refs[3 * j : 3 * j + 3]
        table = cos_ref.shape[1]
        columns = weight.shape[1]
        tile = min(256, columns)
        own_outs, outs = outs[: blocks[j]], outs[blocks[j] :]
        per_out = sum(chunk_rows) // blocks[j]
        for low in range(0, columns, tile):
            product = jnp.dot(
                normed[...], weight[:, low : low + tile], preferred_element_type=jnp.float32
            )
            first = 0
            for i, rows in enumerate(chunk_rows):
                where = pl.ds(pl.multiple_of(starts[i], rows), rows)
                for col in range(low, low + tile, HD):
                    here = product[first : first + rows, col - low : col - low + HD]
                    if rotated[j][col // HD]:
                        at = col % table
                        here = turned(
                            here, cos_ref[where, at : at + HD], sin_ref[where, at : at + HD]
                        )
                    at = first % per_out
                    own_outs[first // per_out][at : at + rows, col : col + HD] = here.astype(
                        jnp.bfloat16
                    )
                first += rows


def project(chunks, place, member, gain, jobs, ready=None, keep=False):
    chunk_rows = tuple(chunk.shape[0] for chunk in chunks)
    rows = sum(chunk_rows)
    width = chunks[0].shape[1]
    columns = [job[0].shape[1] for job in jobs]
    rows_in = [ready] if ready is not None else list(chunks)
    operands = [*rows_in, gain, *(part for job in jobs for part in job[:3])]
    vmem = pl.BlockSpec(memory_space=pltpu.VMEM)
    blocks = [job[4] for job in jobs]
    outs = [
        jax.ShapeDtypeStruct((rows // n, c), jnp.bfloat16)
        for n, c in zip(blocks, columns)
        for _ in range(n)
    ]
    normed = (rows, width)
    scratch = []
    if keep:
        outs.append(jax.ShapeDtypeStruct(normed, jnp.bfloat16))
    elif ready is None:
        scratch.append(pltpu.VMEM(normed, jnp.bfloat16))
    return pl.pallas_call(
        functools.partial(
            project_kernel,
            chunk_rows,
            [job[3] for job in jobs],
            blocks,
            place,
            ready is not None,
        ),
        out_shape=outs,
        in_specs=[pl.BlockSpec(memory_space=pltpu.SMEM)] + [vmem] * len(operands),
        out_specs=[vmem] * len(outs),
        scratch_shapes=scratch,
        compiler_params=pltpu.CompilerParams(vmem_limit_bytes=VMEM_LIMIT),
        cost_estimate=pl.CostEstimate(flops=10000000000, bytes_accessed=1000, transcendentals=0),
        name="project",
    )(member, *operands)


def attend_kernel(chunk_rows, n, place, member, *refs):
    starts = place(member[0])
    q_refs, kv_refs, (out, q_all, kv_all, keys_t, scores) = refs[:n], refs[n:-5], refs[-5:]
    count, columns = out.shape
    heads = columns // HD
    tile = scores.shape[0] // heads
    for sources, target in ((q_refs, q_all), (kv_refs, kv_all)):
        i = 0
        for source in sources:
            first = 0
            while first < source.shape[0]:
                rows = chunk_rows[i]
                where = pl.ds(pl.multiple_of(starts[i], rows), rows)
                target[where, :] = source[first : first + rows, :]
                first += rows
                i += 1
    keys_t[...] = kv_all[:, :HD].astype(jnp.float32).T.astype(jnp.bfloat16)
    scale = HD ** (-0.5) * LOG2E
    row = lax.broadcasted_iota(jnp.int32, (tile, tile), 0)
    col = lax.broadcasted_iota(jnp.int32, (tile, tile), 1)
    triangle = row >= col
    for low in range(0, count, tile):
        top = low + tile
        query = jnp.concatenate(
            [q_all[low:top, h * HD : (h + 1) * HD] for h in range(heads)], axis=0
        )
        scores[:, :top] = jnp.dot(query, keys_t[:, :top], preferred_element_type=jnp.float32)
        for h in range(heads):
            mine = slice(h * tile, (h + 1) * tile)
            edge = jnp.where(triangle, scores[mine, low:top], MASKED)
            highest = jnp.max(edge, axis=1, keepdims=True)
            if low:
                body = scores[mine, :low]
                highest = jnp.maximum(highest, jnp.max(body, axis=1, keepdims=True))
                body = jnp.exp2((body - highest) * scale)
            edge = jnp.exp2((edge - highest) * scale)
            total = jnp.sum(edge, axis=1, keepdims=True)
            if low:
                total = total + jnp.sum(body, axis=1, keepdims=True)
            share = 1.0 / total
            mixed = jnp.dot(
                edge.astype(jnp.bfloat16),
                kv_all[low:top, HD:],
                preferred_element_type=jnp.float32,
            )
            if low:
                mixed = mixed + jnp.dot(
                    body.astype(jnp.bfloat16),
                    kv_all[:low, HD:],
                    preferred_element_type=jnp.float32,
                )
            out[low:top, h * HD : (h + 1) * HD] = (mixed * share).astype(jnp.bfloat16)


def attend(queries, kvs, chunk_rows, place, member):
    count = sum(chunk_rows)
    q_width = queries[0].shape[1]
    tile = min(256, count)
    vmem = pl.BlockSpec(memory_space=pltpu.VMEM)
    return pl.pallas_call(
        functools.partial(
            attend_kernel, tuple(chunk_rows), len(queries), place
        ),
        out_shape=jax.ShapeDtypeStruct((count, q_width), jnp.bfloat16),
        in_specs=[pl.BlockSpec(memory_space=pltpu.SMEM)] + [vmem] * (len(queries) + len(kvs)),
        out_specs=vmem,
        scratch_shapes=[
            pltpu.VMEM((count, q_width), jnp.bfloat16),
            pltpu.VMEM((count, 2 * HD), jnp.bfloat16),
            pltpu.VMEM((HD, count), jnp.bfloat16),
            pltpu.VMEM((tile * (q_width // HD), count), jnp.float32),
        ],
        compiler_params=pltpu.CompilerParams(vmem_limit_bytes=VMEM_LIMIT),
        cost_estimate=pl.CostEstimate(flops=5000000000, bytes_accessed=1000, transcendentals=0),
        name="attend",
    )(member, *queries, *kvs)


def decode_prepare_kernel(tables, lengths, slots, query_ref, queries, allowed, limits):
    rows, pages = tables.shape
    handed = slots.shape[1]
    page = allowed.shape[0] // handed
    columns = queries.shape[1]
    per_head = columns // KVH
    lane = lax.broadcasted_iota(jnp.int32, (1, columns), 1)
    lane_row = lane % rows

    limits[...] = jnp.zeros_like(limits)

    def one_entry(e, owners):
        for r in range(rows):
            at = tables[r, e]
            count = jnp.clip(lengths[r] - e * page, 0, page)
            for j in range(handed):
                taken = slots[0, j] == at
                count = jnp.where(taken, 0, count)
                owners = owners[:j] + (jnp.where(taken, r, owners[j]),) + owners[j + 1 :]
            limits[pl.ds(at, 1), :] = jnp.where(lane_row == r, count, 0)
        return owners

    owners = lax.fori_loop(0, pages, one_entry, (jnp.int32(-1),) * handed)
    for j in range(handed):
        allowed[j * page : (j + 1) * page, :] = jnp.broadcast_to(
            jnp.where(lane_row == owners[j], 1.0, 0.0), (page, columns)
        )

    stacked = jnp.concatenate(
        [query_ref[:, i * HD : (i + 1) * HD].astype(jnp.float32) for i in range(KVH * GROUP)],
        axis=0,
    )
    turned_q = stacked.T.astype(jnp.bfloat16)
    for h in range(KVH):
        queries[2 * h * HD : (2 * h + 1) * HD, :] = jnp.where(
            lane // per_head == h, turned_q, jnp.zeros_like(turned_q)
        )
        queries[(2 * h + 1) * HD : (2 * h + 2) * HD, :] = jnp.zeros((HD, columns), jnp.bfloat16)


def decode_prepare(pool, tables, lengths, slots, queries):
    rows = tables.shape[0]
    columns = KVH * GROUP * rows
    total_pages, page, width = pool.shape
    vmem = pl.BlockSpec(memory_space=pltpu.VMEM)
    smem = pl.BlockSpec(memory_space=pltpu.SMEM)
    return pl.pallas_call(
        decode_prepare_kernel,
        out_shape=[
            jax.ShapeDtypeStruct((width, columns), jnp.bfloat16),
            jax.ShapeDtypeStruct((slots.shape[1] * page, columns), jnp.float32),
            jax.ShapeDtypeStruct((total_pages, columns), jnp.int32),
        ],
        in_specs=[smem, smem, smem, vmem],
        out_specs=[vmem] * 3,
        compiler_params=pltpu.CompilerParams(vmem_limit_bytes=VMEM_LIMIT),
        cost_estimate=pl.CostEstimate(flops=10**10, bytes_accessed=1000, transcendentals=0),
        name="decode_prepare",
    )(tables, lengths, slots, queries)


def decode_old_kernel(queries, limits, own_ref, pool, acc_ref, state_ref, scores, own):
    rows = own_ref.shape[0]
    total_pages, page, width = pool.shape
    columns = queries.shape[1]
    per_head = columns // KVH
    scale = HD ** (-0.5) * LOG2E
    lane_row = lax.broadcasted_iota(jnp.int32, (1, columns), 1) % rows

    own[...] = jnp.zeros_like(own)
    own[0:rows, :] = own_ref[...]
    own_score = jnp.dot(own[...], queries[...], preferred_element_type=jnp.float32)
    own_line = lax.broadcasted_iota(jnp.int32, own_score.shape, 0)
    own_score = jnp.where(own_line == lane_row, own_score, MASKED)
    highest = jnp.max(own_score, axis=0, keepdims=True)
    step = total_pages // 4
    line = lax.broadcasted_iota(jnp.int32, (step, page, columns), 1)
    for first in range(0, total_pages, step):
        score = jnp.dot(
            pool[first : first + step].reshape(step * page, width),
            queries[...],
            preferred_element_type=jnp.float32,
        ).reshape(step, page, columns)
        limit = limits[first : first + step, :].reshape(step, 1, columns)
        score = jnp.where(line < limit, score, MASKED)
        score = score.reshape(step * page, columns)
        scores[first * page : (first + step) * page, :] = score
        highest = jnp.maximum(highest, jnp.max(score, axis=0, keepdims=True))

    weight = jnp.exp2((own_score - highest) * scale)
    total = jnp.sum(weight, axis=0, keepdims=True)
    weight = weight.T.astype(jnp.bfloat16)
    mixed = [
        jnp.dot(
            weight[h * per_head : (h + 1) * per_head],
            own[:, (2 * h + 1) * HD : (2 * h + 2) * HD],
            preferred_element_type=jnp.float32,
        )
        for h in range(KVH)
    ]
    for first in range(0, total_pages, step):
        weight = jnp.exp2((scores[first * page : (first + step) * page, :] - highest) * scale)
        total = total + jnp.sum(weight, axis=0, keepdims=True)
        weight = weight.T.astype(jnp.bfloat16)
        for h in range(KVH):
            value = pool[first : first + step, :, (2 * h + 1) * HD : (2 * h + 2) * HD]
            mixed[h] = mixed[h] + jnp.dot(
                weight[h * per_head : (h + 1) * per_head],
                value.reshape(step * page, HD),
                preferred_element_type=jnp.float32,
            )
    for h in range(KVH):
        acc_ref[h] = mixed[h]
    state_ref[0:1, :] = highest
    state_ref[1:2, :] = total


def decode_old(pool, queries, limits, new_kv):
    rows = new_kv.shape[0]
    columns = queries.shape[1]
    total_pages, page, width = pool.shape
    vmem = pl.BlockSpec(memory_space=pltpu.VMEM)
    return pl.pallas_call(
        decode_old_kernel,
        out_shape=[
            jax.ShapeDtypeStruct((KVH, GROUP * rows, HD), jnp.float32),
            jax.ShapeDtypeStruct((2, columns), jnp.float32),
        ],
        in_specs=[vmem] * 4,
        out_specs=[vmem] * 2,
        scratch_shapes=[
            pltpu.VMEM((total_pages * page, columns), jnp.float32),
            pltpu.VMEM((page, width), jnp.bfloat16),
        ],
        compiler_params=pltpu.CompilerParams(vmem_limit_bytes=VMEM_LIMIT),
        cost_estimate=pl.CostEstimate(flops=5 * 10**9, bytes_accessed=1000, transcendentals=0),
        name="decode_old",
    )(queries, limits, new_kv, pool)


def decode_new_kernel(heads_of, member, q_ref, allowed_ref, acc_ref, state_ref, *refs):
    pieces, out, weights, keeps = refs[:-3], *refs[-3:]
    scale = HD ** (-0.5) * LOG2E
    columns = q_ref.shape[1]
    per_head = columns // KVH
    rows = out.shape[0]
    heads = heads_of(member[0])
    score = jnp.zeros((pieces[0].shape[0], columns), jnp.float32)
    for k in range(KVH):
        where = pl.ds(pl.multiple_of(heads[k] * 2 * HD, 2 * HD), 2 * HD)
        score = score + jnp.dot(pieces[k][...], q_ref[where, :], preferred_element_type=jnp.float32)
    score = jnp.where(allowed_ref[...] > 0.0, score, MASKED)
    before = state_ref[0:1, :]
    highest = jnp.maximum(before, jnp.max(score, axis=0, keepdims=True))
    keep = jnp.exp2((before - highest) * scale)
    weight = jnp.exp2((score - highest) * scale)
    share = 1.0 / (state_ref[1:2, :] * keep + jnp.sum(weight, axis=0, keepdims=True))
    weights[...] = (weight * share).T
    keeps[...] = jnp.broadcast_to(keep * share, (8, columns)).T
    for k in range(KVH):
        h = heads[k]
        mine = pl.ds(pl.multiple_of(h * per_head, per_head), per_head)
        mixed = acc_ref[h] * keeps[mine, 0:1] + jnp.dot(
            weights[mine, :].astype(jnp.bfloat16),
            pieces[k][:, HD:],
            preferred_element_type=jnp.float32,
        )
        for j in range(GROUP):
            lanes = pl.ds(pl.multiple_of((h * GROUP + j) * HD, HD), HD)
            out[:, lanes] = mixed[j * rows : (j + 1) * rows, :].astype(jnp.bfloat16)


def decode_new(pieces, heads_of, member, rows, acc, state, queries, allowed):
    vmem = pl.BlockSpec(memory_space=pltpu.VMEM)
    columns = queries.shape[1]
    return pl.pallas_call(
        functools.partial(decode_new_kernel, heads_of),
        out_shape=jax.ShapeDtypeStruct((rows, KVH * GROUP * HD), jnp.bfloat16),
        in_specs=[pl.BlockSpec(memory_space=pltpu.SMEM)] + [vmem] * (4 + len(pieces)),
        out_specs=vmem,
        scratch_shapes=[
            pltpu.VMEM((columns, pieces[0].shape[0]), jnp.float32),
            pltpu.VMEM((columns, 8), jnp.float32),
        ],
        compiler_params=pltpu.CompilerParams(vmem_limit_bytes=VMEM_LIMIT),
        name="decode_new",
    )(member, queries, allowed, acc, state, *pieces)


def exchange_plan(members, subs):
    def pairs(links):
        return [
            (source * subs + sub, target * subs + sub)
            for source, target in links
            for sub in range(subs)
        ]

    side = [(m, m ^ 1) for m in range(members)]
    outer = [(m, m ^ 2) for m in range(members)]
    outward = [(m, m ^ 2) for m in range(members) if m // 2 in (1, 2)]
    inner = [(m, m ^ 6) for m in range(members) if m // 2 in (1, 2)]
    return pairs(side), pairs(outer), pairs(outward), pairs(inner)


def local(
    stretch_tokens,
    norm_gain,
    q_weight,
    kv_weight,
    dec_query,
    dec_new_kv,
    kv_pool,
    page_table,
    cache_lengths,
    handoff_slot,
):
    devices_tp = lax.axis_size("tp")
    members = min(16, devices_tp)
    subs = devices_tp // members
    sub_bits = subs.bit_length() - 1
    member_bits = members.bit_length() - 1
    headmates = members // KVH
    position = lax.axis_index("tp")
    member = position // subs
    tokens = stretch_tokens[0]
    block_rows, width = tokens.shape
    count = members * block_rows
    gain = norm_gain.reshape(1, width)

    member_ref = member.reshape(1).astype(jnp.int32)
    rows = page_table.shape[0]

    q_block = q_weight
    kv_block = kv_weight
    for bit in range(sub_bits):
        other_q = swapped(q_block, "tp", bit)
        other_kv = swapped(kv_block, "tp", bit)
        upper = position // 2**bit % 2
        q_block = ordered_pair(q_block, other_q, upper, 1)
        kv_block = ordered_pair(kv_block, other_kv, upper, 1)
    q_cos, q_sin = rotation_tables(count, HD, 0, False)
    kv_width = kv_block.shape[1]
    if kv_width % (2 * HD) == 0:
        kv_job = (kv_block, q_cos, q_sin, (True, False) * (kv_width // (2 * HD)), 1)
    else:
        kv_cos, kv_sin = rotation_tables(count, kv_width, member * kv_width, True)
        kv_job = (kv_block, kv_cos, kv_sin, (True,) * max(1, kv_width // HD), 1)
    q_job = (q_block, q_cos, q_sin, (True,) * (q_block.shape[1] // HD), 1)
    kv_pair = kv_job[:4] + (2,)
    bar = lax.optimization_barrier

    def prepared():
        return decode_prepare(kv_pool, page_table, cache_lengths, handoff_slot, dec_query)

    if members == 8 and headmates == 1 and block_rows % 64 == 0:
        half, quarter = block_rows // 2, block_rows // 4
        side, outer, outward, inner = exchange_plan(members, subs)

        def move(value, pairs):
            return lax.ppermute(value, "tp", pairs)

        row = member // 2
        at_end = (row == 0) | (row == 3)

        def place(*chunks):
            return lambda m: [
                jnp.bitwise_xor(m, offset) * block_rows + first for offset, first in chunks
            ]

        def hand(kv, offset):
            pairs = [
                (r * devices_tp + m * subs + s, (1 - r) * devices_tp + (m ^ offset) * subs + s)
                for r in range(2)
                for m in range(members)
                for s in range(subs)
            ]
            return lax.ppermute(kv, ("role", "tp"), pairs)

        own = []
        for c in range(2):
            source = bar((tokens, own[0]))[0] if c else tokens
            own.append(source[c * half : (c + 1) * half])
        y, e1, e2 = {}, {}, {}
        e1[0] = move(tokens, outer)
        y[0] = move(tokens, side)
        for c in range(2):
            e2[c] = move(own[c], inner)
        dec_heads, allowed, limits = prepared()
        q0, kv0 = project([tokens], place((0, 0)), member_ref, gain, [q_job, kv_job])
        piece = {0: hand(kv0, 0)}
        y[2] = move(e1[0], side)
        for c in range(2):
            e1[2 + c] = move(e2[c], outward)
            passed = e1[0][c * half : (c + 1) * half]
            e2[2 + c] = move(passed, inner)
        qa, kv2, kv1 = project(
            [e1[0], y[0]], place((2, 0), (1, 0)), member_ref, gain, [q_job, kv_pair]
        )
        piece[2], piece[1] = hand(kv2, 2), hand(kv1, 1)
        two, three = {}, {}
        for c in range(2):
            two[c] = jnp.where(at_end, e1[2 + c], e2[2 + c])
            if c == 0:
                e1[4] = move(e2[2], outward)
            else:
                e1["5a"] = move(e2[3][:quarter], outward)
                e1["5b"] = move(e2[3][quarter:], outward)
            y[4 + c] = move(two[c], side)
        qb, kv4, kv3 = project(
            [two[0], two[1], y[2]],
            place((4, 0), (4, half), (3, 0)),
            member_ref,
            gain,
            [q_job, kv_pair],
        )
        piece[4], piece[3] = hand(kv4, 4), hand(kv3, 3)
        three[0] = jnp.where(at_end, e1[4], e2[0])
        e1[6] = move(y[4], outer)
        three[1] = jnp.where(at_end, e1["5a"], e2[1][:quarter])
        y["6a"] = move(three[1], side)
        state = decode_old(kv_pool, dec_heads, limits, dec_new_kv)
        e1["5b"], three[1] = bar((e1["5b"], three[1]))
        three[2] = jnp.where(at_end, e1["5b"], e2[1][quarter:])
        y["6b"] = move(three[2], side)
        qc, kv6, kv5 = project(
            [three[0], three[1], three[2], y[4], y[5]],
            place((6, 0), (6, half), (6, half + quarter), (5, 0), (5, half)),
            member_ref,
            gain,
            [q_job, kv_pair],
        )
        piece[6], piece[5] = hand(kv6, 6), hand(kv5, 5)
        last = [e1[6], y["6a"], y["6b"]]
        last_place = place((7, 0), (7, half), (7, half + quarter))
        kv7, normed = project(last, last_place, member_ref, gain, [kv_job], keep=True)
        piece[7] = hand(kv7, 7)
        (qd,) = project(last, last_place, member_ref, gain, [q_job], ready=normed)
        context = attend(
            [q0, qa, qb, qc, qd],
            [kv0, kv2, kv1, kv4, kv3, kv6, kv5, kv7],
            [block_rows] * members,
            place(*((offset, 0) for offset in (0, 2, 1, 4, 3, 6, 5, 7))),
            member_ref,
        )
        pieces = [piece[k] for k in range(members)]
        heads_of = lambda m: [jnp.bitwise_xor(m, k) for k in range(members)]
    else:
        dec_heads, allowed, limits = prepared()
        state = decode_old(kv_pool, dec_heads, limits, dec_new_kv)
        moving = tokens
        queries, local_kvs, order = [], [], []
        group, group_steps = [tokens], [0]
        for step in range(members):
            if step:
                moving = from_behind(moving, "tp", subs)
                group.append(moving)
                group_steps.append(step)
            if len(group) == min(4, members) or step == members - 1:
                place = lambda m, steps=tuple(group_steps): [
                    jnp.bitwise_and(m - back, members - 1) * block_rows for back in steps
                ]
                q_part, kv_part = project(group, place, member_ref, gain, [q_job, kv_job])
                queries.append(q_part)
                local_kvs.append(kv_part)
                order += [(member - back) % members for back in group_steps]
                group, group_steps = [], []
        arrived_kv = jnp.concatenate(local_kvs, axis=0).reshape(members, block_rows, kv_width)
        local_kv = arrived_kv[jnp.argsort(jnp.stack(order))].reshape(count, kv_width)
        head_kv = local_kv
        for step in range(headmates.bit_length() - 1):
            other = swapped(head_kv, "tp", sub_bits + step)
            head_kv = ordered_pair(head_kv, other, member // 2**step % 2, 1)
        arrived_q = jnp.concatenate(queries, axis=0).reshape(members, block_rows, -1)
        all_q = arrived_q[jnp.argsort(jnp.stack(order))].reshape(count, -1)
        context = attend([all_q], [head_kv], [count], lambda m: [0], member_ref)
        crossed = swapped(local_kv, "role", 0)
        received = spread_members(
            crossed.reshape(members, block_rows, kv_width),
            member,
            sub_bits,
            member_bits,
            lambda part, bit: swapped(part, "tp", bit),
        )
        arrived = jnp.transpose(received, (1, 0, 2)).reshape(block_rows, members * kv_width)
        pieces = [arrived[:, k * 2 * HD : (k + 1) * 2 * HD] for k in range(KVH)]
        heads_of = lambda m: list(range(KVH))

    decoded = decode_new(pieces, heads_of, member_ref, rows, *state, dec_heads, allowed)
    return (context[None], decoded)


def solution(mesh):
    in_specs = (
        P("role", ("grp", "tp"), None),
        P(),
        P(None, "tp"),
        P(None, "tp"),
        P(("grp", "role", "tp"), None),
        P(("grp", "role", "tp"), None),
        P(("grp", "role", "tp"), None, None),
        P(("grp", "role", "tp"), None),
        P(("grp", "role", "tp")),
        P(("grp", "role", "tp"), None),
    )
    out_specs = (P("role", "grp", "tp"), P(("grp", "role", "tp"), None))
    return jax.shard_map(local, mesh=mesh, in_specs=in_specs, out_specs=out_specs, check_vma=False)
```
